128 devices in a mesh: gx: 8 (over x, core), gy: 16 (over z, y).
Axes of the slice: x: 4, y: 4, z: 4, core: 2. Of those that a mesh axis runs over, the one named last changes fastest.
Arguments:
- density: float32 [2, 128, 1024], P(None, 'gy', 'gx'), may hold values from 0.1 to 10
- point_position: float32 [3, 2, 128, 1024], P(None, None, 'gy', 'gx'), may hold values from 0 to 1
- block_owner: int32 [2, 128, 128], P(None, 'gy', 'gx'), may hold values from 0 to 127, as said below
- block_slot: int32 [2, 128, 128], P(None, 'gy', 'gx'), may hold values from 0 to 511, as said below
- block_count: int32 [2, 128, 8], P(None, 'gy', 'gx'), may hold values from 8 to 16
- site_position: float32 [3, 8388608], P(None, ('gx', 'gy')), may hold values from 0 to 1
- site_weight: float32 [8388608], P(('gx', 'gy')), may hold values from -0.2 to 11.5
Outputs:
- potential: float32 [2, 128, 1024], P(None, 'gy', 'gx')
- site_mass: float32 [8388608], P(('gx', 'gy'))
- barycentre: float32 [3, 8388608], P(None, ('gx', 'gy'))
The draws below stay inside these ranges and needn't reach their ends.
Inputs may be any that keep to these rules, and one draw needn't show every extreme that they name: `block_owner`: owners are device indices with gx slowest. Among the entries held by one device, padding included, no owner is named more than 4 times, and one owner is named exactly 4 times by every device. `block_slot`: the entries held by one device name distinct blocks.
All inputs are finite; a program needn't handle non-finite values.
Results may differ from the reference program's by a relative error of at most 0.0003.
Values sent between devices are 32-bit elements; how exact they have to be, the bound alone decides.
No kernel may reach another device: no remote copies, remote signals or barrier semaphores. Data moves between devices by JAX's collectives and lax.ppermute only.
A program may use at most 64 MiB of HBM per device.

```python
import math
import jax
import jax.numpy as jnp
from jax import lax

PZ = 2
CY = 8
TILE = 128
CAND = 16
SITE_BLOCK = 128
SB_DEV = 512
HALF = 8
OWNERS = 128
CAP = 4
NX = 1024
NY = 128
SITES = 8388608
N_GX = 8


def route_table(seed_key):
    base_key = jax.random.fold_in(seed_key, 913)
    column_count = NX // TILE
    row_count = NY // CY
    slot_total = OWNERS * CAP
    entry_total = PZ * CY * CAND
    first_key, device_root = jax.random.split(base_key)
    hot_owner = jax.random.randint(first_key, (), 0, OWNERS)
    candidate = jnp.arange(slot_total)

    def per_device(device_key):
        order_key, shuffle_key, offset_key = jax.random.split(device_key, 3)
        priority = jax.random.permutation(order_key, slot_total)
        priority = jnp.where(candidate // CAP == hot_owner, priority - slot_total, priority)
        chosen = jnp.argsort(priority, stable=True)[:entry_total]
        chosen = chosen[jax.random.permutation(shuffle_key, entry_total)]
        owner_ids = chosen // CAP
        offsets = jax.random.randint(offset_key, (OWNERS,), 0, SB_DEV)
        slot_ids = (chosen % CAP + offsets[owner_ids]) % SB_DEV
        return (owner_ids, slot_ids)
    owner_ids, slot_ids = jax.vmap(per_device)(jax.random.split(device_root, OWNERS))

    def arrange(values):
        values = values.reshape(column_count, row_count, PZ, CY, CAND)
        values = jnp.transpose(values, (2, 1, 3, 0, 4))
        return values.reshape(PZ, NY, column_count * CAND).astype(jnp.int32)
    return (arrange(owner_ids), arrange(slot_ids))


def draw_block_owner(key, part):
    return route_table(key)[0]


def draw_block_slot(key, part):
    return route_table(key)[1]


def draw_site_weight(key, part):
    value_key = jax.random.fold_in(jax.random.fold_in(key, 31), 0)
    base_values = jax.random.uniform(value_key, (SITES,), jnp.float32, -0.2, 0.2)
    return base_values


def set_ends(entries, key, smallest, top_value):
    shape = entries.shape
    index_at = [jax.random.randint(jax.random.fold_in(key, axis), (), 0, shape[axis]) for axis in range(len(shape))]
    entries = entries.at[tuple(index_at)].set(smallest)
    longest = shape.index(max(shape))
    index_at[longest] = (index_at[longest] + 1) % shape[longest]
    return entries.at[tuple(index_at)].set(top_value)


def shard_levels(rng, extent, pieces, smallest, largest):
    def one(axis_at, shards_of):
        steps = jax.random.uniform(jax.random.fold_in(jax.random.fold_in(rng, 6), axis_at), (shards_of,), jnp.float32, smallest / len(pieces), largest / len(pieces))
        return jnp.repeat(jnp.exp(steps), extent[axis_at] // shards_of).reshape((-1,) + (1,) * (len(extent) - axis_at - 1))

    gain = one(*pieces[0])
    for cut in pieces[1:]:
        gain = gain * one(*cut)
    return gain


def setup_inputs(seed: int = 0) -> dict:
    seeds = jax.random.split(jax.random.key(seed), 8)
    density = jnp.clip(jnp.exp(math.log(10.0) - 4.6051702 * jax.random.uniform(seeds[0], (PZ, NY, NX), jnp.float32) ** shard_levels(seeds[0], (PZ, NY, NX), ((1, 16), (2, 8)), -0.2, 0.2)), 0.1, 10.0)
    point_position = jnp.clip(1.0 * jax.random.uniform(seeds[1], (3, PZ, NY, NX), jnp.float32) ** shard_levels(seeds[1], (3, PZ, NY, NX), ((2, 16), (3, 8)), -0.2, 0.2), 0.0, 1.0)
    block_owner = draw_block_owner(jax.random.fold_in(seeds[7], 71), 0)
    block_slot = draw_block_slot(jax.random.fold_in(seeds[7], 71), 0)
    block_count = set_ends(jax.random.randint(seeds[4], (PZ, NY, N_GX), CAND // 2, CAND + 1), jax.random.fold_in(seeds[4], 1), CAND // 2, CAND).astype(jnp.int32)
    site_position = jnp.clip(1.0 * jax.random.uniform(seeds[5], (3, SITES), jnp.float32) ** shard_levels(seeds[5], (3, SITES), ((1, 128),), -0.2, 0.2), 0.0, 1.0)
    site_weight = draw_site_weight(jax.random.fold_in(seeds[7], 71), 0)
    return {"density": density, "point_position": point_position, "block_owner": block_owner, "block_slot": block_slot, "block_count": block_count, "site_position": site_position, "site_weight": site_weight}


EPSILON = 0.05
PRIOR_MASS = 0.5
SIGMA_CELLS = 4.0


def gauss_kernel():
    offsets = jnp.arange(-HALF, HALF + 1).astype(jnp.float32)
    values = jnp.exp(-offsets * offsets / (2.0 * SIGMA_CELLS * SIGMA_CELLS))
    return values / jnp.sum(values)


def periodic_pass(field_in, kernel, axis_dim):
    running = jnp.zeros_like(field_in)
    for offset in range(2 * HALF + 1):
        running = running + kernel[offset] * jnp.roll(field_in, HALF - offset, axis=axis_dim)
    return running


def planar_pass(field_in, kernel):
    padded = jnp.pad(field_in, ((HALF, HALF), (0, 0), (0, 0)))
    running = jnp.zeros_like(field_in)
    for offset in range(2 * HALF + 1):
        running = running + kernel[offset] * padded[offset:offset + PZ]
    return running


def reference(density, point_position, block_owner, block_slot, block_count, site_position, site_weight):
    kernel = gauss_kernel()
    first_pass = periodic_pass(density, kernel, 2)
    second_pass = periodic_pass(first_pass, kernel, 1)
    smoothed = planar_pass(second_pass, kernel)
    row_tiles = NX // TILE
    blocks_all = OWNERS * SB_DEV
    site_table = jnp.concatenate([site_position, site_weight[None, :]], axis=0)
    site_table = site_table.reshape(4, blocks_all, SITE_BLOCK).transpose(1, 0, 2)
    row_ids = jnp.arange(PZ * NY).astype(jnp.int32)

    def row_step(moments, row_id):
        plane_id = row_id // NY
        grid_row = row_id % NY
        coords = point_position[:, plane_id, grid_row, :].reshape(3, row_tiles, TILE)
        weights_in = smoothed[plane_id, grid_row].reshape(row_tiles, TILE)
        owners = block_owner[plane_id, grid_row].reshape(row_tiles, CAND)
        slot_ids = block_slot[plane_id, grid_row].reshape(row_tiles, CAND)
        counts = block_count[plane_id, grid_row]
        block_ids = (owners * SB_DEV + slot_ids).astype(jnp.int32)
        chosen = site_table[block_ids]
        live_mask = jnp.arange(CAND)[None, :] < counts[:, None]
        distance = (coords[0][:, :, None, None] - chosen[:, None, :, 0, :]) ** 2
        distance = distance + (coords[1][:, :, None, None] - chosen[:, None, :, 1, :]) ** 2
        distance = distance + (coords[2][:, :, None, None] - chosen[:, None, :, 2, :]) ** 2
        scores = (chosen[:, None, :, 3, :] - distance) / EPSILON
        scores = jnp.where(live_mask[:, None, :, None], scores, -jnp.inf)
        row_max = jnp.max(scores, axis=(2, 3))
        row_potential = row_max + jnp.log(jnp.sum(jnp.exp(scores - row_max[:, :, None, None]), axis=(2, 3)))
        transport = jnp.exp(scores - row_potential[:, :, None, None])
        loadings = jnp.stack([weights_in, weights_in * coords[0], weights_in * coords[1], weights_in * coords[2]])
        partials = jnp.einsum("kgp,gpcs->gcks", loadings, transport, precision=lax.Precision.HIGHEST)
        moments = moments.at[block_ids.reshape(-1)].add(partials.reshape(row_tiles * CAND, 4, SITE_BLOCK))
        return moments, row_potential.reshape(NX)

    moments, potentials = lax.scan(row_step, jnp.zeros((blocks_all, 4, SITE_BLOCK), jnp.float32), row_ids)
    potential = potentials.reshape(PZ, NY, NX)
    site_mass = moments[:, 0, :].reshape(SITES)
    first_moment = moments[:, 1:4, :].transpose(1, 0, 2).reshape(3, SITES)
    barycentre = (first_moment + PRIOR_MASS * site_position) / (site_mass[None, :] + PRIOR_MASS)
    return potential, site_mass, barycentre
```

```python
import math

import jax
import jax.numpy as jnp
import numpy as np
from jax import lax
from jax.experimental import pallas as pl
from jax.experimental.pallas import tpu as pltpu
from jax.sharding import PartitionSpec as P

PZ = 2
CY = 8
TILE = 128
CAND = 16
SITE_BLOCK = 128
SB_DEV = 512
HALF = 8
CAP = 4
OWNERS = 128
TILES = PZ * CY
SLOTS = OWNERS * CAP
ENTRIES = TILES * CAND

EPSILON = 0.05
PRIOR_MASS = 0.5
SIGMA_CELLS = 4.0
KAPPA = math.log2(math.e) / EPSILON
DEAD = -1e30
F32 = jnp.float32
BF16 = jnp.bfloat16
I32 = jnp.int32
VMEM = pl.BlockSpec(memory_space=pltpu.VMEM)
SMEM = pl.BlockSpec(memory_space=pltpu.SMEM)
AXES = ("gx", "gy")


def gauss_values():
    offsets = np.arange(-HALF, HALF + 1, dtype=np.float64)
    values = np.exp(-offsets * offsets / (2.0 * SIGMA_CELLS * SIGMA_CELLS))
    return values / values.sum()


GAUSS = [float(v) for v in gauss_values()]
GAUSS_PEAK = GAUSS[HALF]


def iota(shape, dim):
    return lax.broadcasted_iota(I32, shape, dim)


def rounded(values):
    return values.astype(BF16).astype(F32)


def request_kernel(owner_ref, slot_ref, count_ref, request_ref, target_ref):
    owners = owner_ref[...]
    slots = slot_ref[...]
    counts = count_ref[...]
    lane = iota((TILES, 128), 1)
    hots = []
    values = []
    for k in range(CAND):
        hots.append((owners[:, k : k + 1] == lane).astype(F32))
        values.append(jnp.where(k < counts, slots[:, k : k + 1] + 1, 0))
    hot = jnp.concatenate(hots, axis=0)
    value = jnp.concatenate(values, axis=0)
    square = (ENTRIES, ENTRIES)
    lower = (iota(square, 1) < iota(square, 0)).astype(F32).astype(BF16)
    hot_low = hot.astype(BF16)
    before = jnp.dot(lower, hot_low, preferred_element_type=F32)
    rank = jnp.sum(before * hot, axis=1, keepdims=True).astype(I32)
    wide = iota((ENTRIES, 128), 1)
    high_part = (value & -32).astype(F32)
    low_part = (value & 31).astype(F32)
    spread = jnp.where(wide == rank, high_part, 0.0) + jnp.where(wide == rank + CAP, low_part, 0.0)
    request = lax.dot_general(
        hot_low, spread.astype(BF16), (((0,), (0,)), ((), ())), preferred_element_type=F32
    )
    request = request + pltpu.roll(request, 128 - CAP, 1)
    request_ref[...] = request.astype(I32) - 1
    target = jnp.where(lane == CAND, counts, 0)
    for k in range(CAND):
        place = owners[:, k : k + 1] * CAP + rank[k * TILES : (k + 1) * TILES]
        target = jnp.where(lane == k, place, target)
    target_ref[...] = target


def gather_kernel(asked_ref, position_ref, weight_ref, out_ref, ids_ref, ids_smem, sem):
    ids_ref[...] = jnp.transpose(asked_ref[...].astype(F32))[0:8].astype(I32)
    copy = pltpu.make_async_copy(ids_ref, ids_smem, sem)
    copy.start()
    copy.wait()

    def peer(step, carry):
        for r in range(CAP):
            asked = ids_smem[r, step]
            block = jnp.maximum(asked, 0)
            start = pl.multiple_of(block * SITE_BLOCK, SITE_BLOCK)
            weight = weight_ref[pl.ds(block, 1), :]
            out_ref[step * CAP + r, 0:3, :] = position_ref[:, pl.ds(start, SITE_BLOCK)]
            out_ref[step * CAP + r, 3:4, :] = jnp.where(asked >= 0, weight, DEAD)
        return carry

    lax.fori_loop(0, OWNERS, peer, 0, unroll=4)


def filter_kernel(left_ref, mid_ref, right_ref, out_ref):
    shape = (3 * TILE, TILE)
    shift = iota(shape, 0) - iota(shape, 1) - TILE
    taps = jnp.zeros(shape, F32)
    for offset in range(HALF + 1):
        taps = jnp.where(jnp.abs(shift) == offset, GAUSS[HALF + offset], taps)
    cells = jnp.concatenate([left_ref[...], mid_ref[...], right_ref[...]], axis=1)
    out_ref[...] = jnp.dot(
        cells, taps, preferred_element_type=F32, precision=lax.Precision.HIGHEST
    )


def transport_kernel(
    target_ref,
    arrived_ref,
    point_ref,
    above_ref,
    mid_ref,
    below_ref,
    potential_ref,
    out_ref,
    rows_ref,
    load_ref,
    top_ref,
    sum_ref,
    e_ref,
):
    planes = []
    for z in range(PZ):
        rows_ref[z, 0:CY, :] = above_ref[z * CY : (z + 1) * CY, :]
        rows_ref[z, CY : 2 * CY, :] = mid_ref[z * CY : (z + 1) * CY, :]
        rows_ref[z, 2 * CY : 3 * CY, :] = below_ref[z * CY : (z + 1) * CY, :]
        total = GAUSS[0] * rows_ref[z, 0:CY, :]
        for j in range(1, 2 * HALF + 1):
            total = total + GAUSS[j] * rows_ref[z, j : j + CY, :]
        planes.append(total)
    load_ref[0:CY, :] = GAUSS[HALF] * planes[0] + GAUSS[HALF + 1] * planes[1]
    load_ref[CY : 2 * CY, :] = GAUSS[HALF - 1] * planes[0] + GAUSS[HALF] * planes[1]

    def tile_top(t, carry):
        top = arrived_ref[target_ref[t, 0], 3:4, :]
        for k in range(1, CAND):
            top = jnp.maximum(top, arrived_ref[target_ref[t, k], 3:4, :])
        top_ref[pl.ds(t, 1), :] = top
        return carry

    lax.fori_loop(0, TILES, tile_top, 0)
    top_ref[...] = jnp.broadcast_to(
        jnp.max(top_ref[...], axis=1, keepdims=True), (TILES, 128)
    )

    row = iota((8, 128), 0)

    def tile_step(t, carry):
        coords = [point_ref[c, pl.ds(t, 1), :] for c in range(3)]
        point = jnp.where(
            row % 4 == 0,
            coords[0],
            jnp.where(row % 4 == 1, coords[1], jnp.where(row % 4 == 2, coords[2], 1.0)),
        )
        scaled = jnp.where(row < 3, (2.0 * KAPPA) * (point - 0.5), 0.0)
        a1 = rounded(scaled)
        rest = scaled - a1
        a2 = rounded(rest)
        a3 = rest - a2
        lead = jnp.where(row >= 4, 1.0, a1)
        lhs = jnp.concatenate([lead, lead, lead, a2, a2, a3], axis=0)
        lhs = jnp.transpose(lhs).astype(BF16)
        centre = jnp.where(row % 4 == 3, top_ref[pl.ds(t, 1), :], 0.5)

        def spread(k):
            block = arrived_ref[target_ref[t, k]]
            both = jnp.concatenate([block, block], axis=0) - centre
            terms = jnp.where(
                row < 4, both, both * jnp.where(row == 7, KAPPA, -KAPPA * both)
            )
            t1 = rounded(terms)
            rest = terms - t1
            t2 = rounded(rest)
            t3 = rest - t2
            return jnp.concatenate([t1, t2, t3, t1, t2, t1], axis=0).astype(BF16)

        total = None
        for q in range(CAND // 2):
            rhs = jnp.concatenate([spread(2 * q), spread(2 * q + 1)], axis=1)
            e = jnp.exp2(jnp.dot(lhs, rhs, preferred_element_type=F32))
            part = e[:, :128] + e[:, 128:]
            total = part if total is None else total + part
            high = e.astype(BF16)
            e_ref[q, 0:128, :] = high
            e_ref[q, 128:256, :] = (e - high.astype(F32)).astype(BF16)
        sums = jnp.sum(jnp.transpose(total), axis=0, keepdims=True)
        sum_ref[pl.ds(t, 1), :] = sums
        unit = load_ref[pl.ds(t, 1), :] / sums
        loads = unit * point
        high = rounded(loads)
        half = jnp.where(row < 4, high, loads - high).astype(BF16)
        lhs2 = jnp.concatenate([half, half], axis=1)
        for q in range(CAND // 2):
            found = jnp.dot(lhs2, e_ref[q], preferred_element_type=F32)
            found = found[0:4] + found[4:8]
            out_ref[target_ref[t, 2 * q]] = found[:, :128]
            out_ref[target_ref[t, 2 * q + 1]] = found[:, 128:]
        return carry

    lax.fori_loop(0, TILES, tile_step, 0)
    square = (
        (point_ref[0] - 0.5) ** 2 + (point_ref[1] - 0.5) ** 2 + (point_ref[2] - 0.5) ** 2
    )
    potential_ref[...] = jnp.log(sum_ref[...]) + (top_ref[...] - square) / EPSILON


def reduce_kernel(ids_ref, back_ref, position_ref, mass_ref, centre_ref, acc_ref, scale_ref):
    acc_ref[...] = jnp.zeros_like(acc_ref)

    def peer(step, carry):
        places = []
        sums = []
        for r in range(CAP):
            asked = ids_ref[r, step]
            place = jnp.where(asked < 0, SB_DEV + r, asked)
            places.append(place)
            sums.append(acc_ref[place] + back_ref[step * CAP + r])
        for place, total in zip(places, sums):
            acc_ref[place] = total
        return carry

    lax.fori_loop(0, OWNERS, peer, 0, unroll=2)
    mass = acc_ref[0:SB_DEV, 3, :]
    mass_ref[...] = mass
    scale_ref[...] = 1.0 / (mass + PRIOR_MASS)

    def finish(b, carry):
        start = pl.multiple_of(b * SITE_BLOCK, SITE_BLOCK)
        place = position_ref[:, pl.ds(start, SITE_BLOCK)]
        centre_ref[:, pl.ds(start, SITE_BLOCK)] = (
            acc_ref[b, 0:3, :] + PRIOR_MASS * place
        ) * scale_ref[pl.ds(b, 1), :]
        return carry

    lax.fori_loop(0, SB_DEV, finish, 0, unroll=8)


def shape_of(*dims, dtype=F32):
    return jax.ShapeDtypeStruct(dims, dtype)


def exchange(values):
    return lax.all_to_all(values, AXES, split_axis=0, concat_axis=0, tiled=True)


def neighbours(values, axis):
    count = lax.axis_size(axis)
    before = lax.ppermute(values, axis, [(i, (i + 1) % count) for i in range(count)])
    after = lax.ppermute(values, axis, [((i + 1) % count, i) for i in range(count)])
    return before, after


def local(
    density, point_position, block_owner, block_slot, block_count, site_position, site_weight
):
    cells = density.reshape(TILES, TILE)
    left, right = neighbours(cells, "gx")
    request, target = pl.pallas_call(
        request_kernel,
        out_shape=(shape_of(OWNERS, 128, dtype=I32), shape_of(TILES, 128, dtype=I32)),
        in_specs=[VMEM] * 3,
        out_specs=(VMEM, VMEM),
        name="request",
    )(
        block_owner.reshape(TILES, CAND),
        block_slot.reshape(TILES, CAND),
        block_count.reshape(TILES, 1),
    )
    asked = exchange(request)
    blocks, ids = pl.pallas_call(
        gather_kernel,
        out_shape=(shape_of(SLOTS, 4, SITE_BLOCK), shape_of(8, 128, dtype=I32)),
        in_specs=[VMEM] * 3,
        out_specs=(VMEM, VMEM),
        scratch_shapes=[pltpu.SMEM((8, 128), I32), pltpu.SemaphoreType.DMA],
        name="gather",
    )(asked, site_position, site_weight.reshape(SB_DEV, SITE_BLOCK))
    arrived = exchange(blocks)
    first_pass = pl.pallas_call(
        filter_kernel,
        out_shape=shape_of(TILES, TILE),
        in_specs=[VMEM] * 3,
        out_specs=VMEM,
        name="filter",
    )(left, cells, right)
    above, below = neighbours(first_pass, "gy")
    potential, moments = pl.pallas_call(
        transport_kernel,
        out_shape=(shape_of(TILES, TILE), shape_of(SLOTS, 4, SITE_BLOCK)),
        in_specs=[SMEM] + [VMEM] * 5,
        out_specs=(VMEM, VMEM),
        scratch_shapes=[
            pltpu.VMEM((PZ, 3 * CY, 128), F32),
            pltpu.VMEM((TILES, 128), F32),
            pltpu.VMEM((TILES, 128), F32),
            pltpu.VMEM((TILES, 128), F32),
            pltpu.VMEM((CAND // 2, 256, 256), BF16),
        ],
        name="transport",
    )(target, arrived, point_position.reshape(3, TILES, TILE), above, first_pass, below)
    returned = exchange(moments)
    site_mass, barycentre = pl.pallas_call(
        reduce_kernel,
        out_shape=(shape_of(SB_DEV, SITE_BLOCK), shape_of(3, SB_DEV * SITE_BLOCK)),
        in_specs=[SMEM] + [VMEM] * 2,
        out_specs=(VMEM, VMEM),
        scratch_shapes=[
            pltpu.VMEM((SB_DEV + CAP, 4, SITE_BLOCK), F32),
            pltpu.VMEM((SB_DEV, SITE_BLOCK), F32),
        ],
        name="reduce",
    )(ids, returned, site_position)
    return (
        potential.reshape(PZ, CY, TILE),
        site_mass.reshape(SB_DEV * SITE_BLOCK),
        barycentre,
    )


def solution(mesh):
    in_specs = (
        P(None, "gy", "gx"),
        P(None, None, "gy", "gx"),
        P(None, "gy", "gx"),
        P(None, "gy", "gx"),
        P(None, "gy", "gx"),
        P(None, ("gx", "gy")),
        P(("gx", "gy")),
    )
    out_specs = (P(None, "gy", "gx"), P(("gx", "gy")), P(None, ("gx", "gy")))
    return jax.shard_map(local, mesh=mesh, in_specs=in_specs, out_specs=out_specs, check_vma=False)
```

```python
import math

import jax
import jax.numpy as jnp
import numpy as np
from jax import lax
from jax.experimental import pallas as pl
from jax.experimental.pallas import tpu as pltpu
from jax.sharding import PartitionSpec as P

PZ = 2
CY = 8
TILE = 128
CAND = 16
SITE_BLOCK = 128
SB_DEV = 512
HALF = 8
CAP = 4
OWNERS = 128
TILES = PZ * CY
SLOTS = OWNERS * CAP
ENTRIES = TILES * CAND

EPSILON = 0.05
PRIOR_MASS = 0.5
SIGMA_CELLS = 4.0
KAPPA = math.log2(math.e) / EPSILON
DEAD = -1e30
F32 = jnp.float32
BF16 = jnp.bfloat16
I32 = jnp.int32
VMEM = pl.BlockSpec(memory_space=pltpu.VMEM)
SMEM = pl.BlockSpec(memory_space=pltpu.SMEM)
AXES = ("gx", "gy")
LIMIT = pltpu.CompilerParams(vmem_limit_bytes=16 << 20)


def gauss_values():
    offsets = np.arange(-HALF, HALF + 1, dtype=np.float64)
    values = np.exp(-offsets * offsets / (2.0 * SIGMA_CELLS * SIGMA_CELLS))
    return values / values.sum()


GAUSS = [float(v) for v in gauss_values()]
GAUSS_PEAK = GAUSS[HALF]


def iota(shape, dim):
    return lax.broadcasted_iota(I32, shape, dim)


def rounded(values):
    return values.astype(BF16).astype(F32)


def request_kernel(owner_ref, slot_ref, count_ref, request_ref, target_ref):
    owners = owner_ref[...]
    slots = slot_ref[...]
    lane = iota((TILES, 128), 1)
    corner = iota((CY, CY), 0) == iota((CY, CY), 1)
    counts = jnp.concatenate(
        [
            jnp.sum(jnp.where(corner, count_ref[z], 0), axis=1, keepdims=True)
            for z in range(PZ)
        ],
        axis=0,
    )
    hots = []
    values = []
    for k in range(CAND):
        hots.append((owners[:, k : k + 1] == lane).astype(F32))
        values.append(jnp.where(k < counts, slots[:, k : k + 1] + 1, 0))
    hot = jnp.concatenate(hots, axis=0)
    value = jnp.concatenate(values, axis=0)
    square = (ENTRIES, ENTRIES)
    lower = (iota(square, 1) < iota(square, 0)).astype(F32).astype(BF16)
    hot_low = hot.astype(BF16)
    before = jnp.dot(lower, hot_low, preferred_element_type=F32)
    rank = jnp.sum(before * hot, axis=1, keepdims=True).astype(I32)
    wide = iota((ENTRIES, 128), 1)
    high_part = (value & -32).astype(F32)
    low_part = (value & 31).astype(F32)
    spread = jnp.where(wide == rank, high_part, 0.0) + jnp.where(wide == rank + CAP, low_part, 0.0)
    request = lax.dot_general(
        hot_low, spread.astype(BF16), (((0,), (0,)), ((), ())), preferred_element_type=F32
    )
    request = request + pltpu.roll(request, 128 - CAP, 1)
    request_ref[...] = request.astype(I32) - 1
    target = jnp.where(lane == CAND, counts, 0)
    for k in range(CAND):
        place = owners[:, k : k + 1] * CAP + rank[k * TILES : (k + 1) * TILES]
        target = jnp.where(lane == k, place, target)
    target_ref[...] = target


def filter_columns(left_ref, mid_ref, right_ref, out_ref):
    shape = (3 * TILE, TILE)
    shift = iota(shape, 0) - iota(shape, 1) - TILE
    taps = jnp.zeros(shape, F32)
    for offset in range(HALF + 1):
        taps = jnp.where(jnp.abs(shift) == offset, GAUSS[HALF + offset], taps)
    cells = jnp.concatenate([left_ref[...], mid_ref[...], right_ref[...]], axis=1)
    out_ref[...] = jnp.dot(
        cells, taps, preferred_element_type=F32, precision=lax.Precision.HIGHEST
    )


def gather_kernel(
    asked_ref,
    position_ref,
    weight_ref,
    left_ref,
    mid_ref,
    right_ref,
    out_ref,
    ids_ref,
    first_ref,
    ids_smem,
    sem,
):
    ids_ref[...] = jnp.transpose(asked_ref[...].astype(F32))[0:8].astype(I32)
    copy = pltpu.make_async_copy(ids_ref, ids_smem, sem)
    copy.start()
    filter_columns(left_ref, mid_ref, right_ref, first_ref)
    copy.wait()

    def peer(step, carry):
        for r in range(CAP):
            asked = ids_smem[r, step]
            block = jnp.maximum(asked, 0)
            start = pl.multiple_of(block * SITE_BLOCK, SITE_BLOCK)
            weight = weight_ref[pl.ds(block, 1), :]
            out_ref[step * CAP + r, 0:3, :] = position_ref[:, pl.ds(start, SITE_BLOCK)]
            out_ref[step * CAP + r, 3:4, :] = jnp.where(asked >= 0, weight, DEAD)
        return carry

    lax.fori_loop(0, OWNERS, peer, 0, unroll=4)


def transport_kernel(
    target_ref,
    arrived_ref,
    point_ref,
    above_ref,
    mid_ref,
    below_ref,
    potential_ref,
    out_ref,
    rows_ref,
    load_ref,
    top_ref,
    sum_ref,
    e_ref,
):
    planes = []
    for z in range(PZ):
        rows_ref[z, 0:CY, :] = above_ref[z * CY : (z + 1) * CY, :]
        rows_ref[z, CY : 2 * CY, :] = mid_ref[z * CY : (z + 1) * CY, :]
        rows_ref[z, 2 * CY : 3 * CY, :] = below_ref[z * CY : (z + 1) * CY, :]
        total = GAUSS[0] * rows_ref[z, 0:CY, :]
        for j in range(1, 2 * HALF + 1):
            total = total + GAUSS[j] * rows_ref[z, j : j + CY, :]
        planes.append(total)
    load_ref[0:CY, :] = GAUSS[HALF] * planes[0] + GAUSS[HALF + 1] * planes[1]
    load_ref[CY : 2 * CY, :] = GAUSS[HALF - 1] * planes[0] + GAUSS[HALF] * planes[1]

    def tile_top(t, carry):
        top = arrived_ref[target_ref[t, 0], 3:4, :]
        for k in range(1, CAND):
            top = jnp.maximum(top, arrived_ref[target_ref[t, k], 3:4, :])
        top_ref[pl.ds(t, 1), :] = top
        return carry

    lax.fori_loop(0, TILES, tile_top, 0)
    top_ref[...] = jnp.broadcast_to(
        jnp.max(top_ref[...], axis=1, keepdims=True), (TILES, 128)
    )

    row = iota((8, 128), 0)

    def tile_step(t, carry):
        coords = [point_ref[c, pl.ds(t, 1), :] for c in range(3)]
        point = jnp.where(
            row % 4 == 0,
            coords[0],
            jnp.where(row % 4 == 1, coords[1], jnp.where(row % 4 == 2, coords[2], 1.0)),
        )
        scaled = jnp.where(row < 3, (2.0 * KAPPA) * (point - 0.5), 0.0)
        a1 = rounded(scaled)
        rest = scaled - a1
        a2 = rounded(rest)
        a3 = rest - a2
        lead = jnp.where(row >= 4, 1.0, a1)
        lhs = jnp.concatenate([lead, lead, lead, a2, a2, a3], axis=0)
        lhs = jnp.transpose(lhs).astype(BF16)
        centre = jnp.where(row % 4 == 3, top_ref[pl.ds(t, 1), :], 0.5)

        def spread(k):
            block = arrived_ref[target_ref[t, k]]
            both = jnp.concatenate([block, block], axis=0) - centre
            terms = jnp.where(
                row < 4, both, both * jnp.where(row == 7, KAPPA, -KAPPA * both)
            )
            t1 = rounded(terms)
            rest = terms - t1
            t2 = rounded(rest)
            t3 = rest - t2
            return jnp.concatenate([t1, t2, t3, t1, t2, t1], axis=0).astype(BF16)

        total = None
        for q in range(CAND // 2):
            rhs = jnp.concatenate([spread(2 * q), spread(2 * q + 1)], axis=1)
            e = jnp.exp2(jnp.dot(lhs, rhs, preferred_element_type=F32))
            part = e[:, :128] + e[:, 128:]
            total = part if total is None else total + part
            high = e.astype(BF16)
            e_ref[q, 0:128, :] = high
            e_ref[q, 128:256, :] = (e - high.astype(F32)).astype(BF16)
        sums = jnp.sum(jnp.transpose(total), axis=0, keepdims=True)
        sum_ref[pl.ds(t, 1), :] = sums
        unit = load_ref[pl.ds(t, 1), :] / sums
        loads = unit * point
        high = rounded(loads)
        half = jnp.where(row < 4, high, loads - high).astype(BF16)
        lhs2 = jnp.concatenate([half, half], axis=1)
        for q in range(CAND // 2):
            found = jnp.dot(lhs2, e_ref[q], preferred_element_type=F32)
            found = found[0:4] + found[4:8]
            out_ref[target_ref[t, 2 * q]] = found[:, :128]
            out_ref[target_ref[t, 2 * q + 1]] = found[:, 128:]
        return carry

    lax.fori_loop(0, TILES, tile_step, 0)
    square = (
        (point_ref[0] - 0.5) ** 2 + (point_ref[1] - 0.5) ** 2 + (point_ref[2] - 0.5) ** 2
    )
    potential_ref[...] = jnp.log(sum_ref[...]) + (top_ref[...] - square) / EPSILON


def reduce_kernel(ids_ref, back_ref, position_ref, mass_ref, centre_ref, acc_ref, scale_ref):
    acc_ref[...] = jnp.zeros_like(acc_ref)

    def peer(step, carry):
        places = []
        sums = []
        for r in range(CAP):
            asked = ids_ref[r, step]
            place = jnp.where(asked < 0, SB_DEV + r, asked)
            places.append(place)
            sums.append(acc_ref[place] + back_ref[step * CAP + r])
        for place, total in zip(places, sums):
            acc_ref[place] = total
        return carry

    lax.fori_loop(0, OWNERS, peer, 0, unroll=2)
    mass = acc_ref[0:SB_DEV, 3, :]
    mass_ref[...] = mass
    scale_ref[...] = 1.0 / (mass + PRIOR_MASS)

    def finish(b, carry):
        start = pl.multiple_of(b * SITE_BLOCK, SITE_BLOCK)
        place = position_ref[:, pl.ds(start, SITE_BLOCK)]
        centre_ref[:, pl.ds(start, SITE_BLOCK)] = (
            acc_ref[b, 0:3, :] + PRIOR_MASS * place
        ) * scale_ref[pl.ds(b, 1), :]
        return carry

    lax.fori_loop(0, SB_DEV, finish, 0, unroll=8)


def shape_of(*dims, dtype=F32):
    return jax.ShapeDtypeStruct(dims, dtype)


def exchange(values):
    return lax.all_to_all(values, AXES, split_axis=0, concat_axis=0, tiled=True)


def neighbours(values, axis):
    count = lax.axis_size(axis)
    before = lax.ppermute(values, axis, [(i, (i + 1) % count) for i in range(count)])
    after = lax.ppermute(values, axis, [((i + 1) % count, i) for i in range(count)])
    return before, after


def local(
    density, point_position, block_owner, block_slot, block_count, site_position, site_weight
):
    cells = density.reshape(TILES, TILE)
    left, right = neighbours(cells, "gx")
    request, target = pl.pallas_call(
        request_kernel,
        out_shape=(shape_of(OWNERS, 128, dtype=I32), shape_of(TILES, 128, dtype=I32)),
        in_specs=[VMEM] * 3,
        out_specs=(VMEM, VMEM),
        compiler_params=LIMIT,
        name="request",
    )(
        block_owner.reshape(TILES, CAND),
        block_slot.reshape(TILES, CAND),
        jnp.transpose(block_count, (0, 2, 1)),
    )
    asked = exchange(request)
    blocks, ids, first_pass = pl.pallas_call(
        gather_kernel,
        out_shape=(
            shape_of(SLOTS, 4, SITE_BLOCK),
            shape_of(8, 128, dtype=I32),
            shape_of(TILES, TILE),
        ),
        in_specs=[VMEM] * 6,
        out_specs=(VMEM, VMEM, VMEM),
        compiler_params=LIMIT,
        scratch_shapes=[pltpu.SMEM((8, 128), I32), pltpu.SemaphoreType.DMA],
        name="gather",
    )(asked, site_position, site_weight.reshape(SB_DEV, SITE_BLOCK), left, cells, right)
    arrived = exchange(blocks)
    above, below = neighbours(first_pass, "gy")
    potential, moments = pl.pallas_call(
        transport_kernel,
        out_shape=(shape_of(TILES, TILE), shape_of(SLOTS, 4, SITE_BLOCK)),
        in_specs=[SMEM] + [VMEM] * 5,
        out_specs=(VMEM, VMEM),
        scratch_shapes=[
            pltpu.VMEM((PZ, 3 * CY, 128), F32),
            pltpu.VMEM((TILES, 128), F32),
            pltpu.VMEM((TILES, 128), F32),
            pltpu.VMEM((TILES, 128), F32),
            pltpu.VMEM((CAND // 2, 256, 256), BF16),
        ],
        compiler_params=LIMIT,
        name="transport",
    )(target, arrived, point_position.reshape(3, TILES, TILE), above, first_pass, below)
    returned = exchange(moments)
    site_mass, barycentre = pl.pallas_call(
        reduce_kernel,
        out_shape=(shape_of(SB_DEV, SITE_BLOCK), shape_of(3, SB_DEV * SITE_BLOCK)),
        in_specs=[SMEM] + [VMEM] * 2,
        out_specs=(VMEM, VMEM),
        scratch_shapes=[
            pltpu.VMEM((SB_DEV + CAP, 4, SITE_BLOCK), F32),
            pltpu.VMEM((SB_DEV, SITE_BLOCK), F32),
        ],
        compiler_params=LIMIT,
        name="reduce",
    )(ids, returned, site_position)
    return (
        potential.reshape(PZ, CY, TILE),
        site_mass.reshape(SB_DEV * SITE_BLOCK),
        barycentre,
    )


def solution(mesh):
    in_specs = (
        P(None, "gy", "gx"),
        P(None, None, "gy", "gx"),
        P(None, "gy", "gx"),
        P(None, "gy", "gx"),
        P(None, "gy", "gx"),
        P(None, ("gx", "gy")),
        P(("gx", "gy")),
    )
    out_specs = (P(None, "gy", "gx"), P(("gx", "gy")), P(None, ("gx", "gy")))
    return jax.shard_map(local, mesh=mesh, in_specs=in_specs, out_specs=out_specs, check_vma=False)
```

```python
import math

import jax
import jax.numpy as jnp
import numpy as np
from jax import lax
from jax.experimental import pallas as pl
from jax.experimental.pallas import tpu as pltpu
from jax.sharding import PartitionSpec as P

PZ = 2
CY = 8
TILE = 128
CAND = 16
SITE_BLOCK = 128
SB_DEV = 512
HALF = 8
CAP = 4
OWNERS = 128
TILES = PZ * CY
SLOTS = OWNERS * CAP
ENTRIES = TILES * CAND

EPSILON = 0.05
PRIOR_MASS = 0.5
SIGMA_CELLS = 4.0
KAPPA = math.log2(math.e) / EPSILON
ROOT = math.sqrt(KAPPA)
DEAD = -1e30
F32 = jnp.float32
BF16 = jnp.bfloat16
I32 = jnp.int32
VMEM = pl.BlockSpec(memory_space=pltpu.VMEM)
HBM = pl.BlockSpec(memory_space=pltpu.HBM)
SMEM = pl.BlockSpec(memory_space=pltpu.SMEM)
AXES = ("gx", "gy")
LIMIT = pltpu.CompilerParams(vmem_limit_bytes=16 << 20)
WIDE = pltpu.CompilerParams(vmem_limit_bytes=60 * 1024 * 1024)


def gauss_values():
    offsets = np.arange(-HALF, HALF + 1, dtype=np.float64)
    values = np.exp(-offsets * offsets / (2.0 * SIGMA_CELLS * SIGMA_CELLS))
    return values / values.sum()


GAUSS = [float(v) for v in gauss_values()]
GAUSS_PEAK = GAUSS[HALF]


def iota(shape, dim):
    return lax.broadcasted_iota(I32, shape, dim)


def rounded(values):
    return values.astype(BF16).astype(F32)


def request_kernel(
    owner_hbm, slot_hbm, count_hbm, request_ref, target_ref, owner_ref, slot_ref, count_ref, sems
):
    copies = [
        pltpu.make_async_copy(owner_hbm, owner_ref, sems.at[0]),
        pltpu.make_async_copy(slot_hbm, slot_ref, sems.at[1]),
        pltpu.make_async_copy(count_hbm, count_ref, sems.at[2]),
    ]
    for copy in copies:
        copy.start()
    lane = iota((TILES, 128), 1)
    corner = iota((CY, CY), 0) == iota((CY, CY), 1)
    square = (ENTRIES, ENTRIES)
    lower = (iota(square, 1) < iota(square, 0)).astype(F32).astype(BF16)
    for copy in copies:
        copy.wait()
    owners = owner_ref[...]
    slots = slot_ref[...]
    counts = jnp.concatenate(
        [
            jnp.sum(jnp.where(corner, count_ref[z], 0), axis=1, keepdims=True)
            for z in range(PZ)
        ],
        axis=0,
    )
    hots = []
    values = []
    for k in range(CAND):
        hots.append((owners[:, k : k + 1] == lane).astype(F32))
        values.append(jnp.where(k < counts, slots[:, k : k + 1] + 1, 0))
    hot = jnp.concatenate(hots, axis=0)
    value = jnp.concatenate(values, axis=0)
    hot_low = hot.astype(BF16)
    before = jnp.dot(lower, hot_low, preferred_element_type=F32)
    rank = jnp.sum(before * hot, axis=1, keepdims=True).astype(I32)
    wide = iota((ENTRIES, 128), 1)
    high_part = (value & -32).astype(F32)
    low_part = (value & 31).astype(F32)
    spread = jnp.where(wide == rank, high_part, 0.0) + jnp.where(wide == rank + CAP, low_part, 0.0)
    request = lax.dot_general(
        hot_low, spread.astype(BF16), (((0,), (0,)), ((), ())), preferred_element_type=F32
    )
    request = request + pltpu.roll(request, 128 - CAP, 1)
    request_ref[...] = request.astype(I32) - 1
    target = jnp.where(lane == CAND, counts, 0)
    for k in range(CAND):
        place = owners[:, k : k + 1] * CAP + rank[k * TILES : (k + 1) * TILES]
        target = jnp.where(lane == k, place, target)
    target_ref[...] = target


def table_kernel(position_hbm, weight_hbm, table_ref, start_ref, position_ref, weight_ref, sems):
    first = pltpu.make_async_copy(position_hbm, position_ref, sems.at[0])
    second = pltpu.make_async_copy(weight_hbm, weight_ref, sems.at[1])
    first.start()
    second.start()
    row = iota((4, 128), 0)
    dead = jnp.where(row == 3, DEAD, 0.0)
    for r in range(CAP):
        table_ref[SB_DEV + r] = dead
        start_ref[(SB_DEV + r) * 4 : (SB_DEV + r + 1) * 4, :] = jnp.zeros((4, 128), F32)
    first.wait()
    second.wait()

    def block(b, carry):
        start = pl.multiple_of(b * SITE_BLOCK, SITE_BLOCK)
        place = position_ref[:, pl.ds(start, SITE_BLOCK)]
        table_ref[b, 0:3, :] = (place - 0.5) * ROOT
        table_ref[b, 3:4, :] = weight_ref[pl.ds(b, 1), :]
        line = pl.multiple_of(b * 4, 4)
        start_ref[pl.ds(line, 3), :] = PRIOR_MASS * place
        start_ref[pl.ds(line + 3, 1), :] = jnp.zeros((1, 128), F32)
        return carry

    lax.fori_loop(0, SB_DEV, block, 0, unroll=8)


def filter_columns(left_ref, mid_ref, right_ref, out_ref):
    shape = (3 * TILE, TILE)
    shift = iota(shape, 0) - iota(shape, 1) - TILE
    taps = jnp.zeros(shape, F32)
    for offset in range(HALF + 1):
        taps = jnp.where(jnp.abs(shift) == offset, GAUSS[HALF + offset], taps)
    cells = jnp.concatenate([left_ref[...], mid_ref[...], right_ref[...]], axis=1)
    out_ref[...] = jnp.dot(
        cells, taps, preferred_element_type=F32, precision=lax.Precision.HIGHEST
    )


def gather_kernel(
    asked_ref,
    table_ref,
    left_ref,
    mid_ref,
    right_ref,
    out_ref,
    ids_ref,
    first_ref,
    ids_smem,
    sem,
):
    asked = jnp.transpose(asked_ref[...].astype(F32))[0:8].astype(I32)
    ids_ref[...] = jnp.where(asked < 0, SB_DEV + iota((8, 128), 0) % CAP, asked)
    copy = pltpu.make_async_copy(ids_ref, ids_smem, sem)
    copy.start()
    filter_columns(left_ref, mid_ref, right_ref, first_ref)
    copy.wait()

    def peer(step, carry):
        for r in range(CAP):
            out_ref[step * CAP + r] = table_ref[ids_smem[r, step]]
        return carry

    lax.fori_loop(0, OWNERS, peer, 0, unroll=8)


def prepare_kernel(point_ref, lhs_ref):
    row = iota((8, 128), 0)

    def tile(t, carry):
        coords = [point_ref[c, pl.ds(t, 1), :] for c in range(3)]
        point = jnp.where(row == 0, coords[0], jnp.where(row == 1, coords[1], coords[2]))
        scaled = jnp.where(row < 3, (2.0 * ROOT) * (point - 0.5), 0.0)
        a1 = rounded(scaled)
        rest = scaled - a1
        a2 = rounded(rest)
        a3 = rest - a2
        lead = jnp.where(row == 7, 1.0, jnp.where(row >= 4, -1.0, a1))
        lhs = jnp.concatenate([lead, lead, lead, a2, a2, a3], axis=0)
        lhs_ref[t] = jnp.transpose(lhs).astype(BF16)
        return carry

    lax.fori_loop(0, TILES, tile, 0, unroll=4)


def transport_kernel(
    target_ref,
    arrived_ref,
    lhs_ref,
    point_ref,
    above_ref,
    mid_ref,
    below_ref,
    potential_ref,
    out_ref,
    rows_ref,
    load_ref,
    top_ref,
    sum_ref,
    even_ref,
    odd_ref,
    even_load_ref,
    odd_load_ref,
):
    planes = []
    for z in range(PZ):
        rows_ref[z, 0:CY, :] = above_ref[z * CY : (z + 1) * CY, :]
        rows_ref[z, CY : 2 * CY, :] = mid_ref[z * CY : (z + 1) * CY, :]
        rows_ref[z, 2 * CY : 3 * CY, :] = below_ref[z * CY : (z + 1) * CY, :]
        total = GAUSS[0] * rows_ref[z, 0:CY, :]
        for j in range(1, 2 * HALF + 1):
            total = total + GAUSS[j] * rows_ref[z, j : j + CY, :]
        planes.append(total)
    load_ref[0:CY, :] = GAUSS[HALF] * planes[0] + GAUSS[HALF + 1] * planes[1]
    load_ref[CY : 2 * CY, :] = GAUSS[HALF - 1] * planes[0] + GAUSS[HALF] * planes[1]

    row = iota((8, 128), 0)
    fixed = (row < 4) | (row == 7)
    factor = jnp.where(row == 7, KAPPA, 1.0)

    def find_top(t):
        tops = [arrived_ref[target_ref[t, k], 3:4, :] for k in range(CAND)]
        while len(tops) > 1:
            tops = [jnp.maximum(a, b) for a, b in zip(tops[::2], tops[1::2])]
        top = jnp.max(tops[0], axis=1, keepdims=True)
        top_ref[pl.ds(t, 1), :] = jnp.broadcast_to(top, (1, 128))

    def scores(t, e_ref, unit_ref):
        lhs = lhs_ref[t]
        centre = jnp.where(row % 4 == 3, top_ref[pl.ds(t, 1), :], 0.0)

        def spread(k):
            block = arrived_ref[target_ref[t, k]]
            both = jnp.concatenate([block, block], axis=0) - centre
            terms = both * jnp.where(fixed, factor, both)
            t1 = rounded(terms)
            rest = terms - t1
            t2 = rounded(rest)
            t3 = rest - t2
            return jnp.concatenate([t1, t2, t3, t1, t2, t1], axis=0).astype(BF16)

        total = None
        for q in range(CAND // 2):
            rhs = jnp.concatenate([spread(2 * q), spread(2 * q + 1)], axis=1)
            e = jnp.exp2(jnp.dot(lhs, rhs, preferred_element_type=F32))
            part = e[:, :128] + e[:, 128:]
            total = part if total is None else total + part
            high = e.astype(BF16)
            e_ref[q, 0:128, :] = high
            e_ref[q, 128:256, :] = (e - high.astype(F32)).astype(BF16)
        sums = jnp.sum(jnp.transpose(total), axis=0, keepdims=True)
        sum_ref[pl.ds(t, 1), :] = sums
        coords = [point_ref[c, pl.ds(t, 1), :] for c in range(3)]
        point = jnp.where(
            row % 4 == 0,
            coords[0],
            jnp.where(row % 4 == 1, coords[1], jnp.where(row % 4 == 2, coords[2], 1.0)),
        )
        loads = (load_ref[pl.ds(t, 1), :] / sums) * point
        high = rounded(loads)
        unit_ref[...] = jnp.where(row < 4, high, loads - high)

    def moments(t, e_ref, unit_ref):
        half = unit_ref[...].astype(BF16)
        lhs = jnp.concatenate([half, half], axis=1)
        for q in range(CAND // 2):
            found = jnp.dot(lhs, e_ref[q], preferred_element_type=F32)
            found = found[0:4] + found[4:8]
            out_ref[target_ref[t, 2 * q]] = found[:, :128]
            out_ref[target_ref[t, 2 * q + 1]] = found[:, 128:]

    find_top(0)

    def two_tiles(i, carry):
        t = 2 * i
        find_top(t + 1)
        scores(t, even_ref, even_load_ref)
        moments(jnp.maximum(t - 1, 0), odd_ref, odd_load_ref)
        find_top(jnp.minimum(t + 2, TILES - 1))
        scores(t + 1, odd_ref, odd_load_ref)
        moments(t, even_ref, even_load_ref)
        return carry

    lax.fori_loop(0, TILES // 2, two_tiles, 0)
    moments(TILES - 1, odd_ref, odd_load_ref)
    square = (
        (point_ref[0] - 0.5) ** 2 + (point_ref[1] - 0.5) ** 2 + (point_ref[2] - 0.5) ** 2
    )
    potential_ref[...] = jnp.log(sum_ref[...]) + (top_ref[...] - square) / EPSILON


def reduce_kernel(ids_ref, back_ref, start_ref, mass_ref, centre_ref, acc_ref, scale_ref):
    def peer(step, carry):
        places = []
        sums = []
        for r in range(CAP):
            place = pl.ds(pl.multiple_of(ids_ref[r, step] * 4, 4), 4)
            places.append(place)
            sums.append(acc_ref[place, :] + back_ref[step * CAP + r])
        for place, total in zip(places, sums):
            acc_ref[place, :] = total
        return carry

    lax.fori_loop(0, OWNERS, peer, 0, unroll=4)
    mass = acc_ref[pl.ds(3, SB_DEV, stride=4), :]
    mass_ref[...] = mass
    scale_ref[...] = 1.0 / (mass + PRIOR_MASS)

    def finish(b, carry):
        start = pl.multiple_of(b * SITE_BLOCK, SITE_BLOCK)
        line = pl.multiple_of(b * 4, 4)
        centre_ref[:, pl.ds(start, SITE_BLOCK)] = (
            acc_ref[pl.ds(line, 3), :] * scale_ref[pl.ds(b, 1), :]
        )
        return carry

    lax.fori_loop(0, SB_DEV, finish, 0, unroll=16)


def shape_of(*dims, dtype=F32):
    return jax.ShapeDtypeStruct(dims, dtype)


def exchange(values):
    return lax.all_to_all(values, AXES, split_axis=0, concat_axis=0, tiled=True)


def neighbours(values, axis):
    count = lax.axis_size(axis)
    before = lax.ppermute(values, axis, [(i, (i + 1) % count) for i in range(count)])
    after = lax.ppermute(values, axis, [((i + 1) % count, i) for i in range(count)])
    return before, after


def local(
    density, point_position, block_owner, block_slot, block_count, site_position, site_weight
):
    cells = density.reshape(TILES, TILE)
    left, right = neighbours(cells, "gx")
    request, target = pl.pallas_call(
        request_kernel,
        out_shape=(shape_of(OWNERS, 128, dtype=I32), shape_of(TILES, 128, dtype=I32)),
        in_specs=[HBM] * 3,
        out_specs=(VMEM, VMEM),
        scratch_shapes=[
            pltpu.VMEM((TILES, CAND), I32),
            pltpu.VMEM((TILES, CAND), I32),
            pltpu.VMEM((PZ, 1, CY), I32),
            pltpu.SemaphoreType.DMA((3,)),
        ],
        compiler_params=WIDE,
        name="request",
    )(
        block_owner.reshape(TILES, CAND),
        block_slot.reshape(TILES, CAND),
        jnp.transpose(block_count, (0, 2, 1)),
    )
    asked = exchange(request)
    table, start = pl.pallas_call(
        table_kernel,
        out_shape=(shape_of(SB_DEV + CAP, 4, SITE_BLOCK), shape_of((SB_DEV + CAP) * 4, SITE_BLOCK)),
        in_specs=[HBM] * 2,
        out_specs=(VMEM, VMEM),
        scratch_shapes=[
            pltpu.VMEM((3, SB_DEV * SITE_BLOCK), F32),
            pltpu.VMEM((SB_DEV, SITE_BLOCK), F32),
            pltpu.SemaphoreType.DMA((2,)),
        ],
        compiler_params=LIMIT,
        name="table",
    )(site_position, site_weight.reshape(SB_DEV, SITE_BLOCK))
    blocks, ids, first_pass = pl.pallas_call(
        gather_kernel,
        out_shape=(
            shape_of(SLOTS, 4, SITE_BLOCK),
            shape_of(8, 128, dtype=I32),
            shape_of(TILES, TILE),
        ),
        in_specs=[VMEM] * 5,
        out_specs=(VMEM, VMEM, VMEM),
        compiler_params=LIMIT,
        scratch_shapes=[pltpu.SMEM((8, 128), I32), pltpu.SemaphoreType.DMA],
        name="gather",
    )(asked, table, left, cells, right)
    arrived = exchange(blocks)
    points = point_position.reshape(3, TILES, TILE)
    lhs = pl.pallas_call(
        prepare_kernel,
        out_shape=shape_of(TILES, TILE, 48, dtype=BF16),
        in_specs=[VMEM],
        out_specs=VMEM,
        compiler_params=LIMIT,
        name="prepare",
    )(points)
    above, below = neighbours(first_pass, "gy")
    potential, moments = pl.pallas_call(
        transport_kernel,
        out_shape=(shape_of(TILES, TILE), shape_of(SLOTS, 4, SITE_BLOCK)),
        in_specs=[SMEM] + [VMEM] * 6,
        out_specs=(VMEM, VMEM),
        scratch_shapes=[
            pltpu.VMEM((PZ, 3 * CY, 128), F32),
            pltpu.VMEM((TILES, 128), F32),
            pltpu.VMEM((TILES, 128), F32),
            pltpu.VMEM((TILES, 128), F32),
            pltpu.VMEM((CAND // 2, 256, 256), BF16),
            pltpu.VMEM((CAND // 2, 256, 256), BF16),
            pltpu.VMEM((8, 128), F32),
            pltpu.VMEM((8, 128), F32),
        ],
        compiler_params=LIMIT,
        name="transport",
    )(target, arrived, lhs, points, above, first_pass, below)
    returned = exchange(moments)
    site_mass, barycentre, _ = pl.pallas_call(
        reduce_kernel,
        out_shape=(
            shape_of(SB_DEV, SITE_BLOCK),
            shape_of(3, SB_DEV * SITE_BLOCK),
            shape_of((SB_DEV + CAP) * 4, SITE_BLOCK),
        ),
        in_specs=[SMEM] + [VMEM] * 2,
        out_specs=(VMEM, VMEM, VMEM),
        scratch_shapes=[pltpu.VMEM((SB_DEV, SITE_BLOCK), F32)],
        input_output_aliases={2: 2},
        compiler_params=LIMIT,
        name="reduce",
    )(ids, returned, start)
    return (
        potential.reshape(PZ, CY, TILE),
        site_mass.reshape(SB_DEV * SITE_BLOCK),
        barycentre,
    )


def solution(mesh):
    in_specs = (
        P(None, "gy", "gx"),
        P(None, None, "gy", "gx"),
        P(None, "gy", "gx"),
        P(None, "gy", "gx"),
        P(None, "gy", "gx"),
        P(None, ("gx", "gy")),
        P(("gx", "gy")),
    )
    out_specs = (P(None, "gy", "gx"), P(("gx", "gy")), P(None, ("gx", "gy")))
    return jax.shard_map(local, mesh=mesh, in_specs=in_specs, out_specs=out_specs, check_vma=False)
```

```python
import math

import jax
import jax.numpy as jnp
import numpy as np
from jax import lax
from jax.experimental import pallas as pl
from jax.experimental.pallas import tpu as pltpu
from jax.sharding import PartitionSpec as P

PZ = 2
CY = 8
TILE = 128
CAND = 16
SITE_BLOCK = 128
SB_DEV = 512
HALF = 8
CAP = 4
OWNERS = 128
TILES = PZ * CY
SLOTS = OWNERS * CAP
ENTRIES = TILES * CAND

EPSILON = 0.05
PRIOR_MASS = 0.5
SIGMA_CELLS = 4.0
KAPPA = math.log2(math.e) / EPSILON
ROOT = math.sqrt(KAPPA)
DEAD = -1e30
PIECES = 4
F32 = jnp.float32
BF16 = jnp.bfloat16
I32 = jnp.int32
VMEM = pl.BlockSpec(memory_space=pltpu.VMEM)
HBM = pl.BlockSpec(memory_space=pltpu.HBM)
SMEM = pl.BlockSpec(memory_space=pltpu.SMEM)
AXES = ("gx", "gy")
LIMIT = pltpu.CompilerParams(vmem_limit_bytes=16 << 20)


def gauss_values():
    offsets = np.arange(-HALF, HALF + 1, dtype=np.float64)
    values = np.exp(-offsets * offsets / (2.0 * SIGMA_CELLS * SIGMA_CELLS))
    return values / values.sum()


GAUSS = [float(v) for v in gauss_values()]
GAUSS_PEAK = GAUSS[HALF]


def iota(shape, dim):
    return lax.broadcasted_iota(I32, shape, dim)


def rounded(values):
    return values.astype(BF16).astype(F32)


def request_kernel(
    owner_hbm,
    slot_hbm,
    count_hbm,
    cells_hbm,
    request_ref,
    target_ref,
    owner_ref,
    slot_ref,
    count_ref,
    cells_ref,
    sems,
):
    copies = [
        pltpu.make_async_copy(owner_hbm, owner_ref, sems.at[0]),
        pltpu.make_async_copy(slot_hbm, slot_ref, sems.at[1]),
        pltpu.make_async_copy(count_hbm, count_ref, sems.at[2]),
        pltpu.make_async_copy(cells_hbm, cells_ref, sems.at[3]),
    ]
    for copy in copies:
        copy.start()
    lane = iota((TILES, 128), 1)
    corner = iota((CY, CY), 0) == iota((CY, CY), 1)
    square = (ENTRIES, ENTRIES)
    lower = (iota(square, 1) < iota(square, 0)).astype(F32).astype(BF16)
    for copy in copies:
        copy.wait()
    owners = owner_ref[...]
    slots = slot_ref[...]
    counts = jnp.concatenate(
        [
            jnp.sum(jnp.where(corner, count_ref[z], 0), axis=1, keepdims=True)
            for z in range(PZ)
        ],
        axis=0,
    )
    hots = []
    values = []
    for k in range(CAND):
        hots.append((owners[:, k : k + 1] == lane).astype(F32))
        values.append(jnp.where(k < counts, slots[:, k : k + 1] + 1, 0))
    hot = jnp.concatenate(hots, axis=0)
    value = jnp.concatenate(values, axis=0)
    hot_low = hot.astype(BF16)
    before = jnp.dot(lower, hot_low, preferred_element_type=F32)
    rank = jnp.sum(before * hot, axis=1, keepdims=True).astype(I32)
    wide = iota((ENTRIES, 128), 1)
    high_part = (value & -32).astype(F32)
    low_part = (value & 31).astype(F32)
    spread = jnp.where(wide == rank, high_part, 0.0) + jnp.where(wide == rank + CAP, low_part, 0.0)
    request = lax.dot_general(
        hot_low, spread.astype(BF16), (((0,), (0,)), ((), ())), preferred_element_type=F32
    )
    request = request + pltpu.roll(request, 128 - CAP, 1)
    request_ref[pl.ds(0, OWNERS, stride=2), :] = request - 1.0
    edge_shape = (TILE, 2 * TILE)
    edge_lane = iota(edge_shape, 1)
    column = jnp.where(edge_lane < TILE, 0, TILE - HALF) + edge_lane % HALF
    pick = (iota(edge_shape, 0) == column).astype(F32)
    edges = jnp.dot(
        cells_ref[...], pick, preferred_element_type=F32, precision=lax.Precision.HIGHEST
    )
    edge_shape = (TILES, 2 * TILE)
    own_row = (iota(edge_shape, 1) % TILE) // HALF == iota(edge_shape, 0)
    edges = jnp.sum(jnp.where(own_row, edges, 0.0), axis=0, keepdims=True)
    columns = lax.axis_size("gx")
    after = lax.rem(lax.axis_index("gx") + 1, columns)
    to_after = iota((OWNERS, 128), 0) // (OWNERS // columns) == after
    request_ref[pl.ds(1, OWNERS, stride=2), :] = jnp.where(
        to_after, edges[:, TILE:], edges[:, :TILE]
    )
    target = jnp.where(lane == CAND, counts, 0)
    for k in range(CAND):
        place = owners[:, k : k + 1] * CAP + rank[k * TILES : (k + 1) * TILES]
        target = jnp.where(lane == k, place, target)
    target_ref[...] = target


def prepare(point_ref, lhs_ref):
    row = iota((8, 128), 0)

    def tile(t, carry):
        coords = [point_ref[c, pl.ds(t, 1), :] for c in range(3)]
        point = jnp.where(row == 0, coords[0], jnp.where(row == 1, coords[1], coords[2]))
        scaled = jnp.where(row < 3, (2.0 * ROOT) * (point - 0.5), 0.0)
        a1 = rounded(scaled)
        rest = scaled - a1
        a2 = rounded(rest)
        a3 = rest - a2
        lead = jnp.where(row == 7, 1.0, jnp.where(row >= 4, -1.0, a1))
        lhs = jnp.concatenate([lead, lead, lead, a2, a2, a3], axis=0)
        lhs_ref[t] = jnp.transpose(lhs).astype(BF16)
        return carry

    lax.fori_loop(0, TILES, tile, 0, unroll=4)


def table_kernel(
    position_hbm,
    weight_hbm,
    point_hbm,
    table_ref,
    start_ref,
    lhs_ref,
    position_ref,
    weight_ref,
    point_ref,
    sems,
):
    points = pltpu.make_async_copy(point_hbm, point_ref, sems.at[PIECES + 1])
    points.start()
    copies = [pltpu.make_async_copy(weight_hbm, weight_ref, sems.at[PIECES])]
    width = SB_DEV * SITE_BLOCK // PIECES
    for piece in range(PIECES):
        part = pl.ds(piece * width, width)
        copies.append(
            pltpu.make_async_copy(
                position_hbm.at[:, part], position_ref.at[:, part], sems.at[piece]
            )
        )
    for copy in copies:
        copy.start()
    row = iota((4, 128), 0)
    dead = jnp.where(row == 3, DEAD, 0.0)
    for r in range(CAP):
        table_ref[SB_DEV + r] = dead
        start_ref[(SB_DEV + r) * 4 : (SB_DEV + r + 1) * 4, :] = jnp.zeros((4, 128), F32)

    def block(b, carry):
        start = pl.multiple_of(b * SITE_BLOCK, SITE_BLOCK)
        place = position_ref[:, pl.ds(start, SITE_BLOCK)]
        table_ref[b, 0:3, :] = (place - 0.5) * ROOT
        table_ref[b, 3:4, :] = weight_ref[pl.ds(b, 1), :]
        line = pl.multiple_of(b * 4, 4)
        start_ref[pl.ds(line, 3), :] = PRIOR_MASS * place
        start_ref[pl.ds(line + 3, 1), :] = jnp.zeros((1, 128), F32)
        return carry

    points.wait()
    prepare(point_ref, lhs_ref)
    copies[0].wait()
    blocks = SB_DEV // PIECES
    for piece in range(PIECES):
        copies[piece + 1].wait()
        lax.fori_loop(piece * blocks, (piece + 1) * blocks, block, 0, unroll=8)


def smooth(halo_ref, tiles, rows_ref, load_ref):
    count_x, count_y = lax.axis_size("gx"), lax.axis_size("gy")
    here_x, here_y = lax.axis_index("gx"), lax.axis_index("gy")
    shape = (3 * TILE, TILE)
    row = iota(shape, 0)
    source = jnp.where(
        row < TILE, row, row % HALF + jnp.where(row < 2 * TILE, -HALF, TILE)
    )
    shift = (source - iota(shape, 1)).astype(F32)
    taps = jnp.where(
        jnp.abs(shift) <= HALF,
        GAUSS_PEAK * jnp.exp(shift * shift * (-0.5 / (SIGMA_CELLS * SIGMA_CELLS))),
        0.0,
    )
    shape = (TILES, TILE)
    own_row = iota(shape, 1) // HALF == iota(shape, 0)
    rows = []
    for step, tile in zip((count_y - 1, 0, 1), tiles):
        parts = [tile]
        for side in (count_x - 1, 1):
            peer = lax.rem(here_x + side, count_x) * count_y + lax.rem(here_y + step, count_y)
            halo = halo_ref[pl.ds(2 * peer + 1, 1), :]
            parts.append(jnp.where(own_row, halo, 0.0))
        rows.append(jnp.concatenate(parts, axis=1))
    first = jnp.dot(
        jnp.concatenate(rows, axis=0),
        taps,
        preferred_element_type=F32,
        precision=lax.Precision.HIGHEST,
    )
    planes = []
    for z in range(PZ):
        for part in range(3):
            at = part * TILES + z * CY
            rows_ref[z, part * CY : (part + 1) * CY, :] = first[at : at + CY]
        total = GAUSS[0] * rows_ref[z, 0:CY, :]
        for j in range(1, 2 * HALF + 1):
            total = total + GAUSS[j] * rows_ref[z, j : j + CY, :]
        planes.append(total)
    load_ref[0:CY, :] = GAUSS[HALF] * planes[0] + GAUSS[HALF + 1] * planes[1]
    load_ref[CY : 2 * CY, :] = GAUSS[HALF - 1] * planes[0] + GAUSS[HALF] * planes[1]


def gather_kernel(
    asked_ref,
    table_ref,
    above_ref,
    mid_ref,
    below_ref,
    out_ref,
    ids_ref,
    load_ref,
    rows_ref,
    ids_smem,
    sem,
):
    asked = jnp.transpose(asked_ref[pl.ds(0, OWNERS, stride=2), :])[0:8].astype(I32)
    ids_ref[...] = jnp.where(asked < 0, SB_DEV + iota((8, 128), 0) % CAP, asked)
    copy = pltpu.make_async_copy(ids_ref, ids_smem, sem)
    copy.start()
    smooth(asked_ref, (above_ref[...], mid_ref[...], below_ref[...]), rows_ref, load_ref)
    copy.wait()

    def peer(step, carry):
        for r in range(CAP):
            out_ref[step * CAP + r] = table_ref[ids_smem[r, step]]
        return carry

    lax.fori_loop(0, OWNERS, peer, 0, unroll=8)


def transport_kernel(
    target_ref,
    arrived_ref,
    lhs_ref,
    point_ref,
    load_ref,
    potential_ref,
    out_ref,
    top_ref,
    sum_ref,
    even_ref,
    odd_ref,
    even_load_ref,
    odd_load_ref,
):
    row = iota((8, 128), 0)
    fixed = (row < 4) | (row == 7)
    factor = jnp.where(row == 7, KAPPA, 1.0)

    def find_top(t):
        tops = [arrived_ref[target_ref[t, k], 3:4, :] for k in range(CAND)]
        while len(tops) > 1:
            tops = [jnp.maximum(a, b) for a, b in zip(tops[::2], tops[1::2])]
        top = jnp.max(tops[0], axis=1, keepdims=True)
        top_ref[pl.ds(t, 1), :] = jnp.broadcast_to(top, (1, 128))

    def scores(t, e_ref, unit_ref):
        lhs = lhs_ref[t]
        centre = jnp.where(row % 4 == 3, top_ref[pl.ds(t, 1), :], 0.0)

        def spread(k):
            block = arrived_ref[target_ref[t, k]]
            both = jnp.concatenate([block, block], axis=0) - centre
            terms = both * jnp.where(fixed, factor, both)
            t1 = rounded(terms)
            rest = terms - t1
            t2 = rounded(rest)
            t3 = rest - t2
            return jnp.concatenate([t1, t2, t3, t1, t2, t1], axis=0).astype(BF16)

        total = None
        for q in range(CAND // 2):
            rhs = jnp.concatenate([spread(2 * q), spread(2 * q + 1)], axis=1)
            e = jnp.exp2(jnp.dot(lhs, rhs, preferred_element_type=F32))
            part = e[:, :128] + e[:, 128:]
            total = part if total is None else total + part
            high = e.astype(BF16)
            e_ref[q, 0:128, :] = high
            e_ref[q, 128:256, :] = (e - high.astype(F32)).astype(BF16)
        sums = jnp.sum(jnp.transpose(total), axis=0, keepdims=True)
        sum_ref[pl.ds(t, 1), :] = sums
        coords = [point_ref[c, pl.ds(t, 1), :] for c in range(3)]
        point = jnp.where(
            row % 4 == 0,
            coords[0],
            jnp.where(row % 4 == 1, coords[1], jnp.where(row % 4 == 2, coords[2], 1.0)),
        )
        loads = (load_ref[pl.ds(t, 1), :] / sums) * point
        high = rounded(loads)
        unit_ref[...] = jnp.where(row < 4, high, loads - high)

    def moments(t, e_ref, unit_ref):
        half = unit_ref[...].astype(BF16)
        lhs = jnp.concatenate([half, half], axis=1)
        for q in range(CAND // 2):
            found = jnp.dot(lhs, e_ref[q], preferred_element_type=F32)
            found = found[0:4] + found[4:8]
            out_ref[target_ref[t, 2 * q]] = found[:, :128]
            out_ref[target_ref[t, 2 * q + 1]] = found[:, 128:]

    find_top(0)

    def two_tiles(i, carry):
        t = 2 * i
        find_top(t + 1)
        scores(t, even_ref, even_load_ref)
        moments(jnp.maximum(t - 1, 0), odd_ref, odd_load_ref)
        find_top(jnp.minimum(t + 2, TILES - 1))
        scores(t + 1, odd_ref, odd_load_ref)
        moments(t, even_ref, even_load_ref)
        return carry

    lax.fori_loop(0, TILES // 2, two_tiles, 0)
    moments(TILES - 1, odd_ref, odd_load_ref)
    square = (
        (point_ref[0] - 0.5) ** 2 + (point_ref[1] - 0.5) ** 2 + (point_ref[2] - 0.5) ** 2
    )
    potential_ref[...] = jnp.log(sum_ref[...]) + (top_ref[...] - square) / EPSILON


def reduce_kernel(ids_ref, back_ref, start_ref, mass_ref, centre_ref, acc_ref, scale_ref):
    def peer(step, carry):
        places = []
        sums = []
        for r in range(CAP):
            place = pl.ds(pl.multiple_of(ids_ref[r, step] * 4, 4), 4)
            places.append(place)
            sums.append(acc_ref[place, :] + back_ref[step * CAP + r])
        for place, total in zip(places, sums):
            acc_ref[place, :] = total
        return carry

    lax.fori_loop(0, OWNERS, peer, 0, unroll=4)
    mass = acc_ref[pl.ds(3, SB_DEV, stride=4), :]
    mass_ref[...] = mass
    scale_ref[...] = 1.0 / (mass + PRIOR_MASS)

    def finish(b, carry):
        start = pl.multiple_of(b * SITE_BLOCK, SITE_BLOCK)
        line = pl.multiple_of(b * 4, 4)
        centre_ref[:, pl.ds(start, SITE_BLOCK)] = (
            acc_ref[pl.ds(line, 3), :] * scale_ref[pl.ds(b, 1), :]
        )
        return carry

    lax.fori_loop(0, SB_DEV, finish, 0, unroll=16)


def shape_of(*dims, dtype=F32):
    return jax.ShapeDtypeStruct(dims, dtype)


def in_hbm(values):
    return pltpu.with_memory_space_constraint(values, pltpu.HBM)


def exchange(values):
    return lax.all_to_all(values, AXES, split_axis=0, concat_axis=0, tiled=True)


def neighbours(values, axis):
    count = lax.axis_size(axis)
    before = lax.ppermute(values, axis, [(i, (i + 1) % count) for i in range(count)])
    after = lax.ppermute(values, axis, [((i + 1) % count, i) for i in range(count)])
    return before, after


def local(
    density, point_position, block_owner, block_slot, block_count, site_position, site_weight
):
    cells = density.reshape(TILES, TILE)
    points = point_position.reshape(3, TILES, TILE)
    above, below = neighbours(cells, "gy")
    request, target = pl.pallas_call(
        request_kernel,
        out_shape=(
            shape_of(2 * OWNERS, 128),
            shape_of(TILES, 128, dtype=I32),
        ),
        in_specs=[HBM] * 4,
        out_specs=(VMEM, VMEM),
        scratch_shapes=[
            pltpu.VMEM((TILES, CAND), I32),
            pltpu.VMEM((TILES, CAND), I32),
            pltpu.VMEM((PZ, 1, CY), I32),
            pltpu.VMEM((TILES, TILE), F32),
            pltpu.SemaphoreType.DMA((4,)),
        ],
        compiler_params=LIMIT,
        name="request",
    )(
        in_hbm(block_owner.reshape(TILES, CAND)),
        in_hbm(block_slot.reshape(TILES, CAND)),
        in_hbm(jnp.transpose(block_count, (0, 2, 1))),
        in_hbm(cells),
    )
    asked = exchange(request)
    table, start, lhs = pl.pallas_call(
        table_kernel,
        out_shape=(
            shape_of(SB_DEV + CAP, 4, SITE_BLOCK),
            shape_of((SB_DEV + CAP) * 4, SITE_BLOCK),
            shape_of(TILES, TILE, 48, dtype=BF16),
        ),
        in_specs=[HBM] * 3,
        out_specs=(VMEM,) * 3,
        scratch_shapes=[
            pltpu.VMEM((3, SB_DEV * SITE_BLOCK), F32),
            pltpu.VMEM((SB_DEV, SITE_BLOCK), F32),
            pltpu.VMEM((3, TILES, TILE), F32),
            pltpu.SemaphoreType.DMA((PIECES + 2,)),
        ],
        compiler_params=LIMIT,
        name="table",
    )(
        in_hbm(site_position),
        in_hbm(site_weight.reshape(SB_DEV, SITE_BLOCK)),
        in_hbm(points),
    )
    blocks, ids, load = pl.pallas_call(
        gather_kernel,
        out_shape=(
            shape_of(SLOTS, 4, SITE_BLOCK),
            shape_of(8, 128, dtype=I32),
            shape_of(TILES, TILE),
        ),
        in_specs=[VMEM] * 5,
        out_specs=(VMEM, VMEM, VMEM),
        compiler_params=LIMIT,
        scratch_shapes=[
            pltpu.VMEM((PZ, 3 * CY, 128), F32),
            pltpu.SMEM((8, 128), I32),
            pltpu.SemaphoreType.DMA,
        ],
        name="gather",
    )(asked, table, above, cells, below)
    arrived = exchange(blocks)
    potential, moments = pl.pallas_call(
        transport_kernel,
        out_shape=(shape_of(TILES, TILE), shape_of(SLOTS, 4, SITE_BLOCK)),
        in_specs=[SMEM] + [VMEM] * 4,
        out_specs=(VMEM, VMEM),
        scratch_shapes=[
            pltpu.VMEM((TILES, 128), F32),
            pltpu.VMEM((TILES, 128), F32),
            pltpu.VMEM((CAND // 2, 256, 256), BF16),
            pltpu.VMEM((CAND // 2, 256, 256), BF16),
            pltpu.VMEM((8, 128), F32),
            pltpu.VMEM((8, 128), F32),
        ],
        compiler_params=LIMIT,
        name="transport",
    )(target, arrived, lhs, points, load)
    returned = exchange(moments)
    site_mass, barycentre, _ = pl.pallas_call(
        reduce_kernel,
        out_shape=(
            shape_of(SB_DEV, SITE_BLOCK),
            shape_of(3, SB_DEV * SITE_BLOCK),
            shape_of((SB_DEV + CAP) * 4, SITE_BLOCK),
        ),
        in_specs=[SMEM] + [VMEM] * 2,
        out_specs=(VMEM, VMEM, VMEM),
        scratch_shapes=[pltpu.VMEM((SB_DEV, SITE_BLOCK), F32)],
        input_output_aliases={2: 2},
        compiler_params=LIMIT,
        name="reduce",
    )(ids, returned, start)
    return (
        potential.reshape(PZ, CY, TILE),
        site_mass.reshape(SB_DEV * SITE_BLOCK),
        barycentre,
    )


def solution(mesh):
    in_specs = (
        P(None, "gy", "gx"),
        P(None, None, "gy", "gx"),
        P(None, "gy", "gx"),
        P(None, "gy", "gx"),
        P(None, "gy", "gx"),
        P(None, ("gx", "gy")),
        P(("gx", "gy")),
    )
    out_specs = (P(None, "gy", "gx"), P(("gx", "gy")), P(None, ("gx", "gy")))
    return jax.shard_map(local, mesh=mesh, in_specs=in_specs, out_specs=out_specs, check_vma=False)
```

```python
import math

import jax
import jax.numpy as jnp
import numpy as np
from jax import lax
from jax.experimental import pallas as pl
from jax.experimental.pallas import tpu as pltpu
from jax.sharding import PartitionSpec as P

PZ = 2
CY = 8
TILE = 128
CAND = 16
SITE_BLOCK = 128
SB_DEV = 512
HALF = 8
CAP = 4
OWNERS = 128
TILES = PZ * CY
SLOTS = OWNERS * CAP
ENTRIES = TILES * CAND

EPSILON = 0.05
PRIOR_MASS = 0.5
SIGMA_CELLS = 4.0
KAPPA = math.log2(math.e) / EPSILON
ROOT = math.sqrt(KAPPA)
DEAD = -1e30
PIECES = 4
F32 = jnp.float32
BF16 = jnp.bfloat16
I32 = jnp.int32
VMEM = pl.BlockSpec(memory_space=pltpu.VMEM)
HBM = pl.BlockSpec(memory_space=pltpu.HBM)
SMEM = pl.BlockSpec(memory_space=pltpu.SMEM)
AXES = ("gx", "gy")
LIMIT = pltpu.CompilerParams(vmem_limit_bytes=16 << 20)


def gauss_values():
    offsets = np.arange(-HALF, HALF + 1, dtype=np.float64)
    values = np.exp(-offsets * offsets / (2.0 * SIGMA_CELLS * SIGMA_CELLS))
    return values / values.sum()


GAUSS = [float(v) for v in gauss_values()]
GAUSS_PEAK = GAUSS[HALF]


def iota(shape, dim):
    return lax.broadcasted_iota(I32, shape, dim)


def rounded(values):
    return values.astype(BF16).astype(F32)


def request_kernel(
    owner_hbm,
    slot_hbm,
    count_hbm,
    cells_hbm,
    request_ref,
    target_ref,
    owner_ref,
    slot_ref,
    count_ref,
    cells_ref,
    sems,
):
    copies = [
        pltpu.make_async_copy(owner_hbm, owner_ref, sems.at[0]),
        pltpu.make_async_copy(slot_hbm, slot_ref, sems.at[1]),
        pltpu.make_async_copy(count_hbm, count_ref, sems.at[2]),
        pltpu.make_async_copy(cells_hbm, cells_ref, sems.at[3]),
    ]
    for copy in copies:
        copy.start()
    lane = iota((TILES, 128), 1)
    corner = iota((CY, CY), 0) == iota((CY, CY), 1)
    square = (ENTRIES, ENTRIES)
    lower = (iota(square, 1) < iota(square, 0)).astype(F32).astype(BF16)
    for copy in copies:
        copy.wait()
    owners = owner_ref[...]
    slots = slot_ref[...]
    counts = jnp.concatenate(
        [
            jnp.sum(jnp.where(corner, count_ref[z], 0), axis=1, keepdims=True)
            for z in range(PZ)
        ],
        axis=0,
    )
    hots = []
    values = []
    for k in range(CAND):
        hots.append((owners[:, k : k + 1] == lane).astype(F32))
        values.append(jnp.where(k < counts, slots[:, k : k + 1] + 1, 0))
    hot = jnp.concatenate(hots, axis=0)
    value = jnp.concatenate(values, axis=0)
    hot_low = hot.astype(BF16)
    before = jnp.dot(lower, hot_low, preferred_element_type=F32)
    rank = jnp.sum(before * hot, axis=1, keepdims=True).astype(I32)
    wide = iota((ENTRIES, 128), 1)
    high_part = (value & -32).astype(F32)
    low_part = (value & 31).astype(F32)
    spread = jnp.where(wide == rank, high_part, 0.0) + jnp.where(wide == rank + CAP, low_part, 0.0)
    request = lax.dot_general(
        hot_low, spread.astype(BF16), (((0,), (0,)), ((), ())), preferred_element_type=F32
    )
    request = request + pltpu.roll(request, 128 - CAP, 1)
    request_ref[pl.ds(0, OWNERS, stride=2), :] = request - 1.0
    edge_shape = (TILE, 2 * TILE)
    edge_lane = iota(edge_shape, 1)
    column = jnp.where(edge_lane < TILE, 0, TILE - HALF) + edge_lane % HALF
    pick = (iota(edge_shape, 0) == column).astype(F32)
    edges = jnp.dot(
        cells_ref[...], pick, preferred_element_type=F32, precision=lax.Precision.HIGHEST
    )
    edge_shape = (TILES, 2 * TILE)
    own_row = (iota(edge_shape, 1) % TILE) // HALF == iota(edge_shape, 0)
    edges = jnp.sum(jnp.where(own_row, edges, 0.0), axis=0, keepdims=True)
    columns = lax.axis_size("gx")
    after = lax.rem(lax.axis_index("gx") + 1, columns)
    to_after = iota((OWNERS, 128), 0) // (OWNERS // columns) == after
    request_ref[pl.ds(1, OWNERS, stride=2), :] = jnp.where(
        to_after, edges[:, TILE:], edges[:, :TILE]
    )
    target = jnp.where(lane == CAND, counts, 0)
    for k in range(CAND):
        place = owners[:, k : k + 1] * CAP + rank[k * TILES : (k + 1) * TILES]
        target = jnp.where(lane == k, place, target)
    target_ref[...] = target


def prepare(point_ref, lhs_ref):
    row = iota((8, 128), 0)

    def tile(t, carry):
        coords = [point_ref[c, pl.ds(t, 1), :] for c in range(3)]
        point = jnp.where(row == 0, coords[0], jnp.where(row == 1, coords[1], coords[2]))
        scaled = jnp.where(row < 3, (2.0 * ROOT) * (point - 0.5), 0.0)
        a1 = rounded(scaled)
        rest = scaled - a1
        a2 = rounded(rest)
        a3 = rest - a2
        lead = jnp.where(row == 7, 1.0, jnp.where(row >= 4, -1.0, a1))
        lhs = jnp.concatenate([lead, lead, lead, a2, a2, a3], axis=0)
        lhs_ref[t] = jnp.transpose(lhs).astype(BF16)
        return carry

    lax.fori_loop(0, TILES, tile, 0, unroll=4)


def table_kernel(
    position_hbm,
    weight_hbm,
    point_hbm,
    table_ref,
    start_ref,
    lhs_ref,
    position_ref,
    weight_ref,
    point_ref,
    sems,
):
    points = pltpu.make_async_copy(point_hbm, point_ref, sems.at[PIECES + 1])
    points.start()
    copies = [pltpu.make_async_copy(weight_hbm, weight_ref, sems.at[PIECES])]
    width = SB_DEV * SITE_BLOCK // PIECES
    for piece in range(PIECES):
        part = pl.ds(piece * width, width)
        copies.append(
            pltpu.make_async_copy(
                position_hbm.at[:, part], position_ref.at[:, part], sems.at[piece]
            )
        )
    for copy in copies:
        copy.start()
    row = iota((4, 128), 0)
    dead = jnp.where(row == 3, DEAD, 0.0)
    for r in range(CAP):
        table_ref[SB_DEV + r] = dead
        start_ref[(SB_DEV + r) * 4 : (SB_DEV + r + 1) * 4, :] = jnp.zeros((4, 128), F32)

    def block(b, carry):
        start = pl.multiple_of(b * SITE_BLOCK, SITE_BLOCK)
        place = position_ref[:, pl.ds(start, SITE_BLOCK)]
        table_ref[b, 0:3, :] = (place - 0.5) * ROOT
        table_ref[b, 3:4, :] = weight_ref[pl.ds(b, 1), :]
        line = pl.multiple_of(b * 4, 4)
        start_ref[pl.ds(line, 3), :] = PRIOR_MASS * place
        start_ref[pl.ds(line + 3, 1), :] = jnp.zeros((1, 128), F32)
        return carry

    points.wait()
    prepare(point_ref, lhs_ref)
    copies[0].wait()
    blocks = SB_DEV // PIECES
    for piece in range(PIECES):
        copies[piece + 1].wait()
        lax.fori_loop(piece * blocks, (piece + 1) * blocks, block, 0, unroll=8)


def smooth(halo_ref, tiles, rows_ref, load_ref):
    count_x, count_y = lax.axis_size("gx"), lax.axis_size("gy")
    here_x, here_y = lax.axis_index("gx"), lax.axis_index("gy")
    shape = (3 * TILE, TILE)
    row = iota(shape, 0)
    source = jnp.where(
        row < TILE, row, row % HALF + jnp.where(row < 2 * TILE, -HALF, TILE)
    )
    shift = (source - iota(shape, 1)).astype(F32)
    taps = jnp.where(
        jnp.abs(shift) <= HALF,
        GAUSS_PEAK * jnp.exp(shift * shift * (-0.5 / (SIGMA_CELLS * SIGMA_CELLS))),
        0.0,
    )
    shape = (TILES, TILE)
    own_row = iota(shape, 1) // HALF == iota(shape, 0)
    rows = []
    for step, tile in zip((count_y - 1, 0, 1), tiles):
        parts = [tile]
        for side in (count_x - 1, 1):
            peer = lax.rem(here_x + side, count_x) * count_y + lax.rem(here_y + step, count_y)
            halo = halo_ref[pl.ds(2 * peer + 1, 1), :]
            parts.append(jnp.where(own_row, halo, 0.0))
        rows.append(jnp.concatenate(parts, axis=1))
    first = jnp.dot(
        jnp.concatenate(rows, axis=0),
        taps,
        preferred_element_type=F32,
        precision=lax.Precision.HIGHEST,
    )
    planes = []
    for z in range(PZ):
        for part in range(3):
            at = part * TILES + z * CY
            rows_ref[z, part * CY : (part + 1) * CY, :] = first[at : at + CY]
        total = GAUSS[0] * rows_ref[z, 0:CY, :]
        for j in range(1, 2 * HALF + 1):
            total = total + GAUSS[j] * rows_ref[z, j : j + CY, :]
        planes.append(total)
    load_ref[0:CY, :] = GAUSS[HALF] * planes[0] + GAUSS[HALF + 1] * planes[1]
    load_ref[CY : 2 * CY, :] = GAUSS[HALF - 1] * planes[0] + GAUSS[HALF] * planes[1]


def gather_kernel(
    asked_ref,
    table_ref,
    above_hbm,
    mid_hbm,
    below_hbm,
    out_ref,
    ids_ref,
    load_ref,
    rows_ref,
    tiles_ref,
    ids_smem,
    sem,
    tile_sems,
):
    copies = [
        pltpu.make_async_copy(tile, tiles_ref.at[part], tile_sems.at[part])
        for part, tile in enumerate((above_hbm, mid_hbm, below_hbm))
    ]
    for tile_copy in copies:
        tile_copy.start()
    asked = jnp.transpose(asked_ref[pl.ds(0, OWNERS, stride=2), :])[0:8].astype(I32)
    ids_ref[...] = jnp.where(asked < 0, SB_DEV + iota((8, 128), 0) % CAP, asked)
    copy = pltpu.make_async_copy(ids_ref, ids_smem, sem)
    copy.start()
    for tile_copy in copies:
        tile_copy.wait()
    smooth(asked_ref, [tiles_ref[part] for part in range(3)], rows_ref, load_ref)
    copy.wait()

    def peer(step, carry):
        for r in range(CAP):
            out_ref[step * CAP + r] = table_ref[ids_smem[r, step]]
        return carry

    lax.fori_loop(0, OWNERS, peer, 0, unroll=8)


def transport_kernel(
    target_ref,
    arrived_ref,
    lhs_ref,
    point_ref,
    load_ref,
    potential_ref,
    out_ref,
    top_ref,
    sum_ref,
    even_ref,
    odd_ref,
    even_load_ref,
    odd_load_ref,
):
    row = iota((8, 128), 0)
    fixed = (row < 4) | (row == 7)
    factor = jnp.where(row == 7, KAPPA, 1.0)

    def find_top(t):
        tops = [arrived_ref[target_ref[t, k], 3:4, :] for k in range(CAND)]
        while len(tops) > 1:
            tops = [jnp.maximum(a, b) for a, b in zip(tops[::2], tops[1::2])]
        top = jnp.max(tops[0], axis=1, keepdims=True)
        top_ref[pl.ds(t, 1), :] = jnp.broadcast_to(top, (1, 128))

    def scores(t, e_ref, unit_ref):
        lhs = lhs_ref[t]
        centre = jnp.where(row % 4 == 3, top_ref[pl.ds(t, 1), :], 0.0)

        def spread(k):
            block = arrived_ref[target_ref[t, k]]
            both = jnp.concatenate([block, block], axis=0) - centre
            terms = both * jnp.where(fixed, factor, both)
            t1 = rounded(terms)
            rest = terms - t1
            t2 = rounded(rest)
            t3 = rest - t2
            return jnp.concatenate([t1, t2, t3, t1, t2, t1], axis=0).astype(BF16)

        total = None
        for q in range(CAND // 2):
            rhs = jnp.concatenate([spread(2 * q), spread(2 * q + 1)], axis=1)
            e = jnp.exp2(jnp.dot(lhs, rhs, preferred_element_type=F32))
            part = e[:, :128] + e[:, 128:]
            total = part if total is None else total + part
            high = e.astype(BF16)
            e_ref[q, 0:128, :] = high
            e_ref[q, 128:256, :] = (e - high.astype(F32)).astype(BF16)
        sums = jnp.sum(jnp.transpose(total), axis=0, keepdims=True)
        sum_ref[pl.ds(t, 1), :] = sums
        coords = [point_ref[c, pl.ds(t, 1), :] for c in range(3)]
        point = jnp.where(
            row % 4 == 0,
            coords[0],
            jnp.where(row % 4 == 1, coords[1], jnp.where(row % 4 == 2, coords[2], 1.0)),
        )
        loads = (load_ref[pl.ds(t, 1), :] / sums) * point
        high = rounded(loads)
        unit_ref[...] = jnp.where(row < 4, high, loads - high)

    def moments(t, e_ref, unit_ref):
        half = unit_ref[...].astype(BF16)
        lhs = jnp.concatenate([half, half], axis=1)
        for q in range(CAND // 2):
            found = jnp.dot(lhs, e_ref[q], preferred_element_type=F32)
            found = found[0:4] + found[4:8]
            out_ref[target_ref[t, 2 * q]] = found[:, :128]
            out_ref[target_ref[t, 2 * q + 1]] = found[:, 128:]

    find_top(0)

    def two_tiles(i, carry):
        t = 2 * i
        find_top(t + 1)
        scores(t, even_ref, even_load_ref)
        moments(jnp.maximum(t - 1, 0), odd_ref, odd_load_ref)
        find_top(jnp.minimum(t + 2, TILES - 1))
        scores(t + 1, odd_ref, odd_load_ref)
        moments(t, even_ref, even_load_ref)
        return carry

    lax.fori_loop(0, TILES // 2, two_tiles, 0)
    moments(TILES - 1, odd_ref, odd_load_ref)
    square = (
        (point_ref[0] - 0.5) ** 2 + (point_ref[1] - 0.5) ** 2 + (point_ref[2] - 0.5) ** 2
    )
    potential_ref[...] = jnp.log(sum_ref[...]) + (top_ref[...] - square) / EPSILON


def reduce_kernel(ids_ref, back_ref, start_ref, mass_ref, centre_ref, acc_ref, scale_ref):
    def peer(step, carry):
        places = []
        sums = []
        for r in range(CAP):
            place = pl.ds(pl.multiple_of(ids_ref[r, step] * 4, 4), 4)
            places.append(place)
            sums.append(acc_ref[place, :] + back_ref[step * CAP + r])
        for place, total in zip(places, sums):
            acc_ref[place, :] = total
        return carry

    lax.fori_loop(0, OWNERS, peer, 0, unroll=4)
    mass = acc_ref[pl.ds(3, SB_DEV, stride=4), :]
    mass_ref[...] = mass
    scale_ref[...] = 1.0 / (mass + PRIOR_MASS)

    def finish(b, carry):
        start = pl.multiple_of(b * SITE_BLOCK, SITE_BLOCK)
        line = pl.multiple_of(b * 4, 4)
        centre_ref[:, pl.ds(start, SITE_BLOCK)] = (
            acc_ref[pl.ds(line, 3), :] * scale_ref[pl.ds(b, 1), :]
        )
        return carry

    lax.fori_loop(0, SB_DEV, finish, 0, unroll=16)


def shape_of(*dims, dtype=F32):
    return jax.ShapeDtypeStruct(dims, dtype)


def in_hbm(values):
    return pltpu.with_memory_space_constraint(values, pltpu.HBM)


def exchange(values):
    return lax.all_to_all(values, AXES, split_axis=0, concat_axis=0, tiled=True)


def neighbours(values, axis):
    count = lax.axis_size(axis)
    before = lax.ppermute(values, axis, [(i, (i + 1) % count) for i in range(count)])
    after = lax.ppermute(values, axis, [((i + 1) % count, i) for i in range(count)])
    return before, after


def transport_step(
    density, point_position, block_owner, block_slot, block_count, site_position, site_weight
):
    cells = density.reshape(TILES, TILE)
    points = point_position.reshape(3, TILES, TILE)
    above, below = neighbours(in_hbm(cells), "gy")
    request, target = pl.pallas_call(
        request_kernel,
        out_shape=(
            shape_of(2 * OWNERS, 128),
            shape_of(TILES, 128, dtype=I32),
        ),
        in_specs=[HBM] * 4,
        out_specs=(VMEM, VMEM),
        scratch_shapes=[
            pltpu.VMEM((TILES, CAND), I32),
            pltpu.VMEM((TILES, CAND), I32),
            pltpu.VMEM((PZ, 1, CY), I32),
            pltpu.VMEM((TILES, TILE), F32),
            pltpu.SemaphoreType.DMA((4,)),
        ],
        compiler_params=LIMIT,
        name="request",
    )(
        in_hbm(block_owner.reshape(TILES, CAND)),
        in_hbm(block_slot.reshape(TILES, CAND)),
        in_hbm(jnp.transpose(block_count, (0, 2, 1))),
        in_hbm(cells),
    )
    asked = exchange(request)
    table, start, lhs = pl.pallas_call(
        table_kernel,
        out_shape=(
            shape_of(SB_DEV + CAP, 4, SITE_BLOCK),
            shape_of((SB_DEV + CAP) * 4, SITE_BLOCK),
            shape_of(TILES, TILE, 48, dtype=BF16),
        ),
        in_specs=[HBM] * 3,
        out_specs=(VMEM,) * 3,
        scratch_shapes=[
            pltpu.VMEM((3, SB_DEV * SITE_BLOCK), F32),
            pltpu.VMEM((SB_DEV, SITE_BLOCK), F32),
            pltpu.VMEM((3, TILES, TILE), F32),
            pltpu.SemaphoreType.DMA((PIECES + 2,)),
        ],
        compiler_params=LIMIT,
        name="table",
    )(
        in_hbm(site_position),
        in_hbm(site_weight.reshape(SB_DEV, SITE_BLOCK)),
        in_hbm(points),
    )
    blocks, ids, load = pl.pallas_call(
        gather_kernel,
        out_shape=(
            shape_of(SLOTS, 4, SITE_BLOCK),
            shape_of(8, 128, dtype=I32),
            shape_of(TILES, TILE),
        ),
        in_specs=[VMEM] * 2 + [HBM] * 3,
        out_specs=(VMEM, VMEM, VMEM),
        compiler_params=LIMIT,
        scratch_shapes=[
            pltpu.VMEM((PZ, 3 * CY, 128), F32),
            pltpu.VMEM((3, TILES, TILE), F32),
            pltpu.SMEM((8, 128), I32),
            pltpu.SemaphoreType.DMA,
            pltpu.SemaphoreType.DMA((3,)),
        ],
        name="gather",
    )(asked, table, in_hbm(above), in_hbm(cells), in_hbm(below))
    arrived = exchange(blocks)
    potential, moments = pl.pallas_call(
        transport_kernel,
        out_shape=(shape_of(TILES, TILE), shape_of(SLOTS, 4, SITE_BLOCK)),
        in_specs=[SMEM] + [VMEM] * 4,
        out_specs=(VMEM, VMEM),
        scratch_shapes=[
            pltpu.VMEM((TILES, 128), F32),
            pltpu.VMEM((TILES, 128), F32),
            pltpu.VMEM((CAND // 2, 256, 256), BF16),
            pltpu.VMEM((CAND // 2, 256, 256), BF16),
            pltpu.VMEM((8, 128), F32),
            pltpu.VMEM((8, 128), F32),
        ],
        compiler_params=LIMIT,
        name="transport",
    )(target, arrived, lhs, points, load)
    returned = exchange(moments)
    site_mass, barycentre, _ = pl.pallas_call(
        reduce_kernel,
        out_shape=(
            shape_of(SB_DEV, SITE_BLOCK),
            shape_of(3, SB_DEV * SITE_BLOCK),
            shape_of((SB_DEV + CAP) * 4, SITE_BLOCK),
        ),
        in_specs=[SMEM] + [VMEM] * 2,
        out_specs=(VMEM, VMEM, VMEM),
        scratch_shapes=[pltpu.VMEM((SB_DEV, SITE_BLOCK), F32)],
        input_output_aliases={2: 2},
        compiler_params=LIMIT,
        name="reduce",
    )(ids, returned, start)
    return (
        potential.reshape(PZ, CY, TILE),
        site_mass.reshape(SB_DEV * SITE_BLOCK),
        barycentre,
    )


def solution(mesh):
    in_specs = (
        P(None, "gy", "gx"),
        P(None, None, "gy", "gx"),
        P(None, "gy", "gx"),
        P(None, "gy", "gx"),
        P(None, "gy", "gx"),
        P(None, ("gx", "gy")),
        P(("gx", "gy")),
    )
    out_specs = (P(None, "gy", "gx"), P(("gx", "gy")), P(None, ("gx", "gy")))
    return jax.shard_map(transport_step, mesh=mesh, in_specs=in_specs, out_specs=out_specs, check_vma=False)
```

```python
import math

import jax
import jax.numpy as jnp
import numpy as np
from jax import lax
from jax.experimental import pallas as pl
from jax.experimental.pallas import tpu as pltpu
from jax.sharding import PartitionSpec as P

PZ = 2
CY = 8
TILE = 128
CAND = 16
SITE_BLOCK = 128
SB_DEV = 512
HALF = 8
CAP = 4
OWNERS = 128
TILES = PZ * CY
SLOTS = OWNERS * CAP
ENTRIES = TILES * CAND

EPSILON = 0.05
PRIOR_MASS = 0.5
SIGMA_CELLS = 4.0
KAPPA = math.log2(math.e) / EPSILON
ROOT = math.sqrt(KAPPA)
DEAD = -1e30
PIECES = 4
F32 = jnp.float32
BF16 = jnp.bfloat16
I32 = jnp.int32
VMEM = pl.BlockSpec(memory_space=pltpu.VMEM)
HBM = pl.BlockSpec(memory_space=pltpu.HBM)
SMEM = pl.BlockSpec(memory_space=pltpu.SMEM)
AXES = ("gx", "gy")
LIMIT = pltpu.CompilerParams(vmem_limit_bytes=16 << 20)


def gauss_values():
    offsets = np.arange(-HALF, HALF + 1, dtype=np.float64)
    values = np.exp(-offsets * offsets / (2.0 * SIGMA_CELLS * SIGMA_CELLS))
    return values / values.sum()


GAUSS = [float(v) for v in gauss_values()]
GAUSS_PEAK = GAUSS[HALF]


def iota(shape, dim):
    return lax.broadcasted_iota(I32, shape, dim)


def rounded(values):
    return values.astype(BF16).astype(F32)


def request_kernel(
    owner_hbm,
    slot_hbm,
    count_hbm,
    cells_hbm,
    request_ref,
    target_ref,
    owner_ref,
    slot_ref,
    count_ref,
    cells_ref,
    sems,
):
    copies = [
        pltpu.make_async_copy(owner_hbm, owner_ref, sems.at[0]),
        pltpu.make_async_copy(slot_hbm, slot_ref, sems.at[1]),
        pltpu.make_async_copy(count_hbm, count_ref, sems.at[2]),
        pltpu.make_async_copy(cells_hbm, cells_ref, sems.at[3]),
    ]
    for copy in copies:
        copy.start()
    lane = iota((TILES, 128), 1)
    corner = iota((CY, CY), 0) == iota((CY, CY), 1)
    square = (ENTRIES, ENTRIES)
    lower = (iota(square, 1) < iota(square, 0)).astype(F32).astype(BF16)
    for copy in copies:
        copy.wait()
    owners = owner_ref[...]
    slots = slot_ref[...]
    counts = jnp.concatenate(
        [
            jnp.sum(jnp.where(corner, count_ref[z], 0), axis=1, keepdims=True)
            for z in range(PZ)
        ],
        axis=0,
    )
    hots = []
    values = []
    for k in range(CAND):
        hots.append((owners[:, k : k + 1] == lane).astype(F32))
        values.append(jnp.where(k < counts, slots[:, k : k + 1] + 1, 0))
    hot = jnp.concatenate(hots, axis=0)
    value = jnp.concatenate(values, axis=0)
    hot_low = hot.astype(BF16)
    before = jnp.dot(lower, hot_low, preferred_element_type=F32)
    rank = jnp.sum(before * hot, axis=1, keepdims=True).astype(I32)
    wide = iota((ENTRIES, 128), 1)
    high_part = (value & -32).astype(F32)
    low_part = (value & 31).astype(F32)
    spread = jnp.where(wide == rank, high_part, 0.0) + jnp.where(wide == rank + CAP, low_part, 0.0)
    request = lax.dot_general(
        hot_low, spread.astype(BF16), (((0,), (0,)), ((), ())), preferred_element_type=F32
    )
    request = request + pltpu.roll(request, 128 - CAP, 1)
    request_ref[pl.ds(0, OWNERS, stride=2), :] = request - 1.0
    edge_shape = (TILE, 2 * TILE)
    edge_lane = iota(edge_shape, 1)
    column = jnp.where(edge_lane < TILE, 0, TILE - HALF) + edge_lane % HALF
    pick = (iota(edge_shape, 0) == column).astype(F32)
    edges = jnp.dot(
        cells_ref[...], pick, preferred_element_type=F32, precision=lax.Precision.HIGHEST
    )
    edge_shape = (TILES, 2 * TILE)
    own_row = (iota(edge_shape, 1) % TILE) // HALF == iota(edge_shape, 0)
    edges = jnp.sum(jnp.where(own_row, edges, 0.0), axis=0, keepdims=True)
    columns = lax.axis_size("gx")
    after = lax.rem(lax.axis_index("gx") + 1, columns)
    to_after = iota((OWNERS, 128), 0) // (OWNERS // columns) == after
    request_ref[pl.ds(1, OWNERS, stride=2), :] = jnp.where(
        to_after, edges[:, TILE:], edges[:, :TILE]
    )
    target = jnp.where(lane == CAND, counts, 0)
    for k in range(CAND):
        place = owners[:, k : k + 1] * CAP + rank[k * TILES : (k + 1) * TILES]
        target = jnp.where(lane == k, place, target)
    target_ref[...] = target


def prepare(point_ref, lhs_ref):
    row = iota((8, 128), 0)

    def tile(t, carry):
        coords = [point_ref[c, pl.ds(t, 1), :] for c in range(3)]
        point = jnp.where(row == 0, coords[0], jnp.where(row == 1, coords[1], coords[2]))
        scaled = jnp.where(row < 3, (2.0 * ROOT) * (point - 0.5), 0.0)
        a1 = rounded(scaled)
        rest = scaled - a1
        a2 = rounded(rest)
        a3 = rest - a2
        lead = jnp.where(row == 7, 1.0, jnp.where(row >= 4, -1.0, a1))
        lhs = jnp.concatenate([lead, lead, lead, a2, a2, a3], axis=0)
        lhs_ref[t] = jnp.transpose(lhs).astype(BF16)
        return carry

    lax.fori_loop(0, TILES, tile, 0, unroll=4)


def table_kernel(
    position_hbm,
    weight_hbm,
    point_hbm,
    table_ref,
    start_ref,
    lhs_ref,
    position_ref,
    weight_ref,
    point_ref,
    sems,
):
    points = pltpu.make_async_copy(point_hbm, point_ref, sems.at[PIECES + 1])
    points.start()
    copies = [pltpu.make_async_copy(weight_hbm, weight_ref, sems.at[PIECES])]
    width = SB_DEV * SITE_BLOCK // PIECES
    for piece in range(PIECES):
        part = pl.ds(piece * width, width)
        copies.append(
            pltpu.make_async_copy(
                position_hbm.at[:, part], position_ref.at[:, part], sems.at[piece]
            )
        )
    for copy in copies:
        copy.start()
    row = iota((4, 128), 0)
    dead = jnp.where(row == 3, DEAD, 0.0)
    for r in range(CAP):
        table_ref[SB_DEV + r] = dead
        start_ref[(SB_DEV + r) * 4 : (SB_DEV + r + 1) * 4, :] = jnp.zeros((4, 128), F32)

    def block(b, carry):
        start = pl.multiple_of(b * SITE_BLOCK, SITE_BLOCK)
        place = position_ref[:, pl.ds(start, SITE_BLOCK)]
        table_ref[b, 0:3, :] = (place - 0.5) * ROOT
        table_ref[b, 3:4, :] = weight_ref[pl.ds(b, 1), :]
        line = pl.multiple_of(b * 4, 4)
        start_ref[pl.ds(line, 3), :] = PRIOR_MASS * place
        start_ref[pl.ds(line + 3, 1), :] = jnp.zeros((1, 128), F32)
        return carry

    points.wait()
    prepare(point_ref, lhs_ref)
    copies[0].wait()
    blocks = SB_DEV // PIECES
    for piece in range(PIECES):
        copies[piece + 1].wait()
        lax.fori_loop(piece * blocks, (piece + 1) * blocks, block, 0, unroll=8)


def smooth_kernel(halo_ref, above_ref, mid_ref, below_ref, load_ref, rows_ref):
    tiles = (above_ref[...], mid_ref[...], below_ref[...])
    count_x, count_y = lax.axis_size("gx"), lax.axis_size("gy")
    here_x, here_y = lax.axis_index("gx"), lax.axis_index("gy")
    shape = (3 * TILE, TILE)
    row = iota(shape, 0)
    source = jnp.where(
        row < TILE, row, row % HALF + jnp.where(row < 2 * TILE, -HALF, TILE)
    )
    shift = (source - iota(shape, 1)).astype(F32)
    taps = jnp.where(
        jnp.abs(shift) <= HALF,
        GAUSS_PEAK * jnp.exp(shift * shift * (-0.5 / (SIGMA_CELLS * SIGMA_CELLS))),
        0.0,
    )
    shape = (TILES, TILE)
    own_row = iota(shape, 1) // HALF == iota(shape, 0)
    rows = []
    for step, tile in zip((count_y - 1, 0, 1), tiles):
        parts = [tile]
        for side in (count_x - 1, 1):
            peer = lax.rem(here_x + side, count_x) * count_y + lax.rem(here_y + step, count_y)
            halo = halo_ref[pl.ds(2 * peer + 1, 1), :]
            parts.append(jnp.where(own_row, halo, 0.0))
        rows.append(jnp.concatenate(parts, axis=1))
    first = jnp.dot(
        jnp.concatenate(rows, axis=0),
        taps,
        preferred_element_type=F32,
        precision=lax.Precision.HIGHEST,
    )
    planes = []
    for z in range(PZ):
        for part in range(3):
            at = part * TILES + z * CY
            rows_ref[z, part * CY : (part + 1) * CY, :] = first[at : at + CY]
        total = GAUSS[0] * rows_ref[z, 0:CY, :]
        for j in range(1, 2 * HALF + 1):
            total = total + GAUSS[j] * rows_ref[z, j : j + CY, :]
        planes.append(total)
    load_ref[0:CY, :] = GAUSS[HALF] * planes[0] + GAUSS[HALF + 1] * planes[1]
    load_ref[CY : 2 * CY, :] = GAUSS[HALF - 1] * planes[0] + GAUSS[HALF] * planes[1]


def gather_kernel(
    asked_ref,
    table_ref,
    out_ref,
    ids_ref,
    ids_smem,
    sem,
):
    asked = jnp.transpose(asked_ref[pl.ds(0, OWNERS, stride=2), :])[0:8].astype(I32)
    ids_ref[...] = jnp.where(asked < 0, SB_DEV + iota((8, 128), 0) % CAP, asked)
    copy = pltpu.make_async_copy(ids_ref, ids_smem, sem)
    copy.start()
    copy.wait()

    def peer(step, carry):
        for r in range(CAP):
            out_ref[step * CAP + r] = table_ref[ids_smem[r, step]]
        return carry

    lax.fori_loop(0, OWNERS, peer, 0, unroll=8)


def transport_kernel(
    target_ref,
    arrived_ref,
    lhs_ref,
    point_ref,
    load_ref,
    potential_ref,
    out_ref,
    top_ref,
    sum_ref,
    even_ref,
    odd_ref,
    even_load_ref,
    odd_load_ref,
):
    row = iota((8, 128), 0)
    fixed = (row < 4) | (row == 7)
    factor = jnp.where(row == 7, KAPPA, 1.0)

    def find_top(t):
        tops = [arrived_ref[target_ref[t, k], 3:4, :] for k in range(CAND)]
        while len(tops) > 1:
            tops = [jnp.maximum(a, b) for a, b in zip(tops[::2], tops[1::2])]
        top = jnp.max(tops[0], axis=1, keepdims=True)
        top_ref[pl.ds(t, 1), :] = jnp.broadcast_to(top, (1, 128))

    def scores(t, e_ref, unit_ref):
        lhs = lhs_ref[t]
        centre = jnp.where(row % 4 == 3, top_ref[pl.ds(t, 1), :], 0.0)

        def spread(k):
            block = arrived_ref[target_ref[t, k]]
            both = jnp.concatenate([block, block], axis=0) - centre
            terms = both * jnp.where(fixed, factor, both)
            t1 = rounded(terms)
            rest = terms - t1
            t2 = rounded(rest)
            t3 = rest - t2
            return jnp.concatenate([t1, t2, t3, t1, t2, t1], axis=0).astype(BF16)

        total = None
        for q in range(CAND // 2):
            rhs = jnp.concatenate([spread(2 * q), spread(2 * q + 1)], axis=1)
            e = jnp.exp2(jnp.dot(lhs, rhs, preferred_element_type=F32))
            part = e[:, :128] + e[:, 128:]
            total = part if total is None else total + part
            high = e.astype(BF16)
            e_ref[q, 0:128, :] = high
            e_ref[q, 128:256, :] = (e - high.astype(F32)).astype(BF16)
        sums = jnp.sum(jnp.transpose(total), axis=0, keepdims=True)
        sum_ref[pl.ds(t, 1), :] = sums
        coords = [point_ref[c, pl.ds(t, 1), :] for c in range(3)]
        point = jnp.where(
            row % 4 == 0,
            coords[0],
            jnp.where(row % 4 == 1, coords[1], jnp.where(row % 4 == 2, coords[2], 1.0)),
        )
        loads = (load_ref[pl.ds(t, 1), :] / sums) * point
        high = rounded(loads)
        unit_ref[...] = jnp.where(row < 4, high, loads - high)

    def moments(t, e_ref, unit_ref):
        half = unit_ref[...].astype(BF16)
        lhs = jnp.concatenate([half, half], axis=1)
        for q in range(CAND // 2):
            found = jnp.dot(lhs, e_ref[q], preferred_element_type=F32)
            found = found[0:4] + found[4:8]
            out_ref[target_ref[t, 2 * q]] = found[:, :128]
            out_ref[target_ref[t, 2 * q + 1]] = found[:, 128:]

    find_top(0)

    def two_tiles(i, carry):
        t = 2 * i
        find_top(t + 1)
        scores(t, even_ref, even_load_ref)
        moments(jnp.maximum(t - 1, 0), odd_ref, odd_load_ref)
        find_top(jnp.minimum(t + 2, TILES - 1))
        scores(t + 1, odd_ref, odd_load_ref)
        moments(t, even_ref, even_load_ref)
        return carry

    lax.fori_loop(0, TILES // 2, two_tiles, 0)
    moments(TILES - 1, odd_ref, odd_load_ref)
    square = (
        (point_ref[0] - 0.5) ** 2 + (point_ref[1] - 0.5) ** 2 + (point_ref[2] - 0.5) ** 2
    )
    potential_ref[...] = jnp.log(sum_ref[...]) + (top_ref[...] - square) / EPSILON


def reduce_kernel(ids_ref, back_ref, start_ref, mass_ref, centre_ref, acc_ref, scale_ref):
    def peer(step, carry):
        places = []
        sums = []
        for r in range(CAP):
            place = pl.ds(pl.multiple_of(ids_ref[r, step] * 4, 4), 4)
            places.append(place)
            sums.append(acc_ref[place, :] + back_ref[step * CAP + r])
        for place, total in zip(places, sums):
            acc_ref[place, :] = total
        return carry

    lax.fori_loop(0, OWNERS, peer, 0, unroll=4)
    mass = acc_ref[pl.ds(3, SB_DEV, stride=4), :]
    mass_ref[...] = mass
    scale_ref[...] = 1.0 / (mass + PRIOR_MASS)

    def finish(b, carry):
        start = pl.multiple_of(b * SITE_BLOCK, SITE_BLOCK)
        line = pl.multiple_of(b * 4, 4)
        centre_ref[:, pl.ds(start, SITE_BLOCK)] = (
            acc_ref[pl.ds(line, 3), :] * scale_ref[pl.ds(b, 1), :]
        )
        return carry

    lax.fori_loop(0, SB_DEV, finish, 0, unroll=16)


def shape_of(*dims, dtype=F32):
    return jax.ShapeDtypeStruct(dims, dtype)


def in_hbm(values):
    return pltpu.with_memory_space_constraint(values, pltpu.HBM)


def exchange(values):
    return lax.all_to_all(values, AXES, split_axis=0, concat_axis=0, tiled=True)


def neighbours(values, axis):
    count = lax.axis_size(axis)
    before = lax.ppermute(values, axis, [(i, (i + 1) % count) for i in range(count)])
    after = lax.ppermute(values, axis, [((i + 1) % count, i) for i in range(count)])
    return before, after


def local(
    density, point_position, block_owner, block_slot, block_count, site_position, site_weight
):
    cells = density.reshape(TILES, TILE)
    points = point_position.reshape(3, TILES, TILE)
    request, target = pl.pallas_call(
        request_kernel,
        out_shape=(
            shape_of(2 * OWNERS, 128),
            shape_of(TILES, 128, dtype=I32),
        ),
        in_specs=[HBM] * 4,
        out_specs=(VMEM, VMEM),
        scratch_shapes=[
            pltpu.VMEM((TILES, CAND), I32),
            pltpu.VMEM((TILES, CAND), I32),
            pltpu.VMEM((PZ, 1, CY), I32),
            pltpu.VMEM((TILES, TILE), F32),
            pltpu.SemaphoreType.DMA((4,)),
        ],
        compiler_params=LIMIT,
        name="request",
    )(
        in_hbm(block_owner.reshape(TILES, CAND)),
        in_hbm(block_slot.reshape(TILES, CAND)),
        in_hbm(jnp.transpose(block_count, (0, 2, 1))),
        in_hbm(cells),
    )
    asked = exchange(request)
    table, start, lhs = pl.pallas_call(
        table_kernel,
        out_shape=(
            shape_of(SB_DEV + CAP, 4, SITE_BLOCK),
            shape_of((SB_DEV + CAP) * 4, SITE_BLOCK),
            shape_of(TILES, TILE, 48, dtype=BF16),
        ),
        in_specs=[HBM] * 3,
        out_specs=(VMEM,) * 3,
        scratch_shapes=[
            pltpu.VMEM((3, SB_DEV * SITE_BLOCK), F32),
            pltpu.VMEM((SB_DEV, SITE_BLOCK), F32),
            pltpu.VMEM((3, TILES, TILE), F32),
            pltpu.SemaphoreType.DMA((PIECES + 2,)),
        ],
        compiler_params=LIMIT,
        name="table",
    )(
        in_hbm(site_position),
        in_hbm(site_weight.reshape(SB_DEV, SITE_BLOCK)),
        in_hbm(points),
    )
    blocks, ids = pl.pallas_call(
        gather_kernel,
        out_shape=(
            shape_of(SLOTS, 4, SITE_BLOCK),
            shape_of(8, 128, dtype=I32),
        ),
        in_specs=[VMEM] * 2,
        out_specs=(VMEM, VMEM),
        compiler_params=LIMIT,
        scratch_shapes=[pltpu.SMEM((8, 128), I32), pltpu.SemaphoreType.DMA],
        name="gather",
    )(asked, table)
    cells, blocks = lax.optimization_barrier((cells, blocks))
    arrived = exchange(blocks)
    above, below = neighbours(cells, "gy")
    load = pl.pallas_call(
        smooth_kernel,
        out_shape=shape_of(TILES, TILE),
        in_specs=[VMEM] * 4,
        out_specs=VMEM,
        scratch_shapes=[pltpu.VMEM((PZ, 3 * CY, 128), F32)],
        compiler_params=LIMIT,
        name="smooth",
    )(asked, above, cells, below)
    potential, moments = pl.pallas_call(
        transport_kernel,
        out_shape=(shape_of(TILES, TILE), shape_of(SLOTS, 4, SITE_BLOCK)),
        in_specs=[SMEM] + [VMEM] * 4,
        out_specs=(VMEM, VMEM),
        scratch_shapes=[
            pltpu.VMEM((TILES, 128), F32),
            pltpu.VMEM((TILES, 128), F32),
            pltpu.VMEM((CAND // 2, 256, 256), BF16),
            pltpu.VMEM((CAND // 2, 256, 256), BF16),
            pltpu.VMEM((8, 128), F32),
            pltpu.VMEM((8, 128), F32),
        ],
        compiler_params=LIMIT,
        name="transport",
    )(target, arrived, lhs, points, load)
    returned = exchange(moments)
    site_mass, barycentre, _ = pl.pallas_call(
        reduce_kernel,
        out_shape=(
            shape_of(SB_DEV, SITE_BLOCK),
            shape_of(3, SB_DEV * SITE_BLOCK),
            shape_of((SB_DEV + CAP) * 4, SITE_BLOCK),
        ),
        in_specs=[SMEM] + [VMEM] * 2,
        out_specs=(VMEM, VMEM, VMEM),
        scratch_shapes=[pltpu.VMEM((SB_DEV, SITE_BLOCK), F32)],
        input_output_aliases={2: 2},
        compiler_params=LIMIT,
        name="reduce",
    )(ids, returned, start)
    return (
        potential.reshape(PZ, CY, TILE),
        site_mass.reshape(SB_DEV * SITE_BLOCK),
        barycentre,
    )


def solution(mesh):
    in_specs = (
        P(None, "gy", "gx"),
        P(None, None, "gy", "gx"),
        P(None, "gy", "gx"),
        P(None, "gy", "gx"),
        P(None, "gy", "gx"),
        P(None, ("gx", "gy")),
        P(("gx", "gy")),
    )
    out_specs = (P(None, "gy", "gx"), P(("gx", "gy")), P(None, ("gx", "gy")))
    return jax.shard_map(local, mesh=mesh, in_specs=in_specs, out_specs=out_specs, check_vma=False)
```

```python
import math

import jax
import jax.numpy as jnp
import numpy as np
from jax import lax
from jax.experimental import pallas as pl
from jax.experimental.pallas import tpu as pltpu
from jax.sharding import PartitionSpec as P

PZ = 2
CY = 8
TILE = 128
CAND = 16
SITE_BLOCK = 128
SB_DEV = 512
HALF = 8
CAP = 4
OWNERS = 128
TILES = PZ * CY
SLOTS = OWNERS * CAP
ENTRIES = TILES * CAND

EPSILON = 0.05
PRIOR_MASS = 0.5
SIGMA_CELLS = 4.0
KAPPA = math.log2(math.e) / EPSILON
ROOT = math.sqrt(KAPPA)
DEAD = -1e30
PIECES = 4
BLOCKS = SB_DEV // PIECES
F32 = jnp.float32
BF16 = jnp.bfloat16
I32 = jnp.int32
VMEM = pl.BlockSpec(memory_space=pltpu.VMEM)
HBM = pl.BlockSpec(memory_space=pltpu.HBM)
SMEM = pl.BlockSpec(memory_space=pltpu.SMEM)
AXES = ("gx", "gy")
LIMIT = pltpu.CompilerParams(vmem_limit_bytes=8 << 20)


def gauss_values():
    offsets = np.arange(-HALF, HALF + 1, dtype=np.float64)
    values = np.exp(-offsets * offsets / (2.0 * SIGMA_CELLS * SIGMA_CELLS))
    return values / values.sum()


GAUSS = [float(v) for v in gauss_values()]
GAUSS_PEAK = GAUSS[HALF]


def iota(shape, dim):
    return lax.broadcasted_iota(I32, shape, dim)


def rounded(values):
    return values.astype(BF16).astype(F32)


def request_kernel(
    owner_hbm,
    slot_hbm,
    count_hbm,
    cells_hbm,
    request_ref,
    target_ref,
    owner_ref,
    slot_ref,
    count_ref,
    cells_ref,
    sems,
):
    copies = [
        pltpu.make_async_copy(owner_hbm, owner_ref, sems.at[0]),
        pltpu.make_async_copy(slot_hbm, slot_ref, sems.at[1]),
        pltpu.make_async_copy(count_hbm, count_ref, sems.at[2]),
        pltpu.make_async_copy(cells_hbm, cells_ref, sems.at[3]),
    ]
    for copy in copies:
        copy.start()
    lane = iota((TILES, 128), 1)
    corner = iota((CY, CY), 0) == iota((CY, CY), 1)
    square = (ENTRIES, ENTRIES)
    lower = (iota(square, 1) < iota(square, 0)).astype(F32).astype(BF16)
    for copy in copies:
        copy.wait()
    owners = owner_ref[...]
    slots = slot_ref[...]
    counts = jnp.concatenate(
        [
            jnp.sum(jnp.where(corner, count_ref[z], 0), axis=1, keepdims=True)
            for z in range(PZ)
        ],
        axis=0,
    )
    hots = []
    values = []
    for k in range(CAND):
        hots.append((owners[:, k : k + 1] == lane).astype(F32))
        values.append(jnp.where(k < counts, slots[:, k : k + 1] + 1, 0))
    hot = jnp.concatenate(hots, axis=0)
    value = jnp.concatenate(values, axis=0)
    hot_low = hot.astype(BF16)
    before = jnp.dot(lower, hot_low, preferred_element_type=F32)
    rank = jnp.sum(before * hot, axis=1, keepdims=True).astype(I32)
    own_rank = iota((ENTRIES, 128), 1) % CAP == rank
    high_part = (value & -32).astype(F32)
    low_part = (value & 31).astype(F32)
    spread = jnp.concatenate(
        [jnp.where(own_rank, high_part, 0.0), jnp.where(own_rank, low_part, 0.0)], axis=1
    )
    request = lax.dot_general(
        hot_low, spread.astype(BF16), (((0,), (0,)), ((), ())), preferred_element_type=F32
    )
    request_ref[pl.ds(0, OWNERS, stride=2), :] = request[:, :128] + request[:, 128:] - 1.0
    edge_shape = (TILE, 2 * TILE)
    edge_lane = iota(edge_shape, 1)
    column = jnp.where(edge_lane < TILE, 0, TILE - HALF) + edge_lane % HALF
    pick = (iota(edge_shape, 0) == column).astype(F32)
    edges = jnp.dot(
        cells_ref[...], pick, preferred_element_type=F32, precision=lax.Precision.HIGHEST
    )
    edge_shape = (TILES, 2 * TILE)
    own_row = (iota(edge_shape, 1) % TILE) // HALF == iota(edge_shape, 0)
    edges = jnp.sum(jnp.where(own_row, edges, 0.0), axis=0, keepdims=True)
    columns = lax.axis_size("gx")
    after = lax.rem(lax.axis_index("gx") + 1, columns)
    to_after = iota((OWNERS, 128), 0) // (OWNERS // columns) == after
    request_ref[pl.ds(1, OWNERS, stride=2), :] = jnp.where(
        to_after, edges[:, TILE:], edges[:, :TILE]
    )
    target = jnp.where(lane == CAND, counts, 0)
    for k in range(CAND):
        place = owners[:, k : k + 1] * CAP + rank[k * TILES : (k + 1) * TILES]
        target = jnp.where(lane == k, place, target)
    target_ref[...] = target


def prepare(point_ref, lhs_ref):
    row = iota((8, 128), 0)

    def tile(t, carry):
        coords = [point_ref[c, pl.ds(t, 1), :] for c in range(3)]
        point = jnp.where(row == 0, coords[0], jnp.where(row == 1, coords[1], coords[2]))
        scaled = jnp.where(row < 3, (2.0 * ROOT) * (point - 0.5), 0.0)
        a1 = rounded(scaled)
        rest = scaled - a1
        a2 = rounded(rest)
        a3 = rest - a2
        lead = jnp.where(row == 7, 1.0, jnp.where(row >= 4, -1.0, a1))
        lhs = jnp.concatenate([lead, lead, lead, a2, a2, a3], axis=0)
        lhs_ref[t] = jnp.transpose(lhs).astype(BF16)
        return carry

    lax.fori_loop(0, TILES, tile, 0, unroll=4)


def piece_copies(source, target, sems):
    width = SB_DEV * SITE_BLOCK // PIECES
    copies = []
    for piece in range(PIECES):
        part = pl.ds(piece * width, width)
        copies.append(
            pltpu.make_async_copy(source.at[:, part], target.at[:, part], sems.at[piece])
        )
    return copies


def table_kernel(position_hbm, weight_hbm, table_ref, position_ref, weight_ref, sems):
    weights = pltpu.make_async_copy(weight_hbm, weight_ref, sems.at[PIECES])
    copies = piece_copies(position_hbm, position_ref, sems)
    weights.start()
    for copy in copies:
        copy.start()
    dead = jnp.where(iota((4, 128), 0) == 3, DEAD, 0.0)
    for r in range(CAP):
        table_ref[(SB_DEV + r) * 4 : (SB_DEV + r + 1) * 4, :] = dead
    weights.wait()
    for piece in range(PIECES):
        copies[piece].wait()
        for b in range(piece * BLOCKS, (piece + 1) * BLOCKS):
            place = position_ref[:, b * SITE_BLOCK : (b + 1) * SITE_BLOCK]
            table_ref[4 * b : 4 * b + 3, :] = (place - 0.5) * ROOT
            table_ref[4 * b + 3 : 4 * b + 4, :] = weight_ref[b : b + 1, :]


def setup_kernel(position_hbm, point_ref, start_ref, lhs_ref, position_ref, sems):
    copies = piece_copies(position_hbm, position_ref, sems)
    for copy in copies:
        copy.start()
    prepare(point_ref, lhs_ref)
    for r in range(CAP):
        start_ref[(SB_DEV + r) * 4 : (SB_DEV + r + 1) * 4, :] = jnp.zeros((4, 128), F32)

    def block(b, carry):
        start = pl.multiple_of(b * SITE_BLOCK, SITE_BLOCK)
        line = pl.multiple_of(b * 4, 4)
        start_ref[pl.ds(line, 3), :] = PRIOR_MASS * position_ref[:, pl.ds(start, SITE_BLOCK)]
        start_ref[pl.ds(line + 3, 1), :] = jnp.zeros((1, 128), F32)
        return carry

    for piece in range(PIECES):
        copies[piece].wait()
        lax.fori_loop(piece * BLOCKS, (piece + 1) * BLOCKS, block, 0, unroll=8)


def smooth_kernel(halo_ref, above_ref, mid_ref, below_ref, load_ref, rows_ref):
    tiles = (above_ref[...], mid_ref[...], below_ref[...])
    count_x, count_y = lax.axis_size("gx"), lax.axis_size("gy")
    here_x, here_y = lax.axis_index("gx"), lax.axis_index("gy")
    shape = (3 * TILE, TILE)
    row = iota(shape, 0)
    source = jnp.where(
        row < TILE, row, row % HALF + jnp.where(row < 2 * TILE, -HALF, TILE)
    )
    shift = (source - iota(shape, 1)).astype(F32)
    taps = jnp.where(
        jnp.abs(shift) <= HALF,
        GAUSS_PEAK * jnp.exp(shift * shift * (-0.5 / (SIGMA_CELLS * SIGMA_CELLS))),
        0.0,
    )
    shape = (TILES, TILE)
    own_row = iota(shape, 1) // HALF == iota(shape, 0)
    rows = []
    for step, tile in zip((count_y - 1, 0, 1), tiles):
        parts = [tile]
        for side in (count_x - 1, 1):
            peer = lax.rem(here_x + side, count_x) * count_y + lax.rem(here_y + step, count_y)
            halo = halo_ref[pl.ds(2 * peer + 1, 1), :]
            parts.append(jnp.where(own_row, halo, 0.0))
        rows.append(jnp.concatenate(parts, axis=1))
    first = jnp.dot(
        jnp.concatenate(rows, axis=0),
        taps,
        preferred_element_type=F32,
        precision=lax.Precision.HIGHEST,
    )
    planes = []
    for z in range(PZ):
        for part in range(3):
            at = part * TILES + z * CY
            rows_ref[z, part * CY : (part + 1) * CY, :] = first[at : at + CY]
        total = GAUSS[0] * rows_ref[z, 0:CY, :]
        for j in range(1, 2 * HALF + 1):
            total = total + GAUSS[j] * rows_ref[z, j : j + CY, :]
        planes.append(total)
    load_ref[0:CY, :] = GAUSS[HALF] * planes[0] + GAUSS[HALF + 1] * planes[1]
    load_ref[CY : 2 * CY, :] = GAUSS[HALF - 1] * planes[0] + GAUSS[HALF] * planes[1]


def gather_kernel(asked_ref, table_ref, out_hbm, ids_ref, out_ref, ids_smem, sem, out_sems):
    shape = (OWNERS, 128)
    asked = asked_ref[pl.ds(0, OWNERS, stride=2), :]
    lane = iota(shape, 1)
    place = jnp.where(asked < 0.0, (SB_DEV + lane % CAP).astype(F32), asked) * 4.0
    own = iota(shape, 0) % (128 // CAP) == lane // CAP
    place = jnp.where(own, place, 0.0)
    rows = [
        jnp.sum(place[g * 32 : (g + 1) * 32], axis=0, keepdims=True) for g in range(PIECES)
    ]
    ids_ref[...] = jnp.concatenate(rows + rows, axis=0).astype(I32)
    copy = pltpu.make_async_copy(ids_ref, ids_smem, sem)
    copy.start()
    copy.wait()
    copies = []
    for piece in range(PIECES):
        for c in range(BLOCKS):
            line = pl.multiple_of(ids_smem[piece, c], 4)
            out_ref[piece * BLOCKS + c] = table_ref[pl.ds(line, 4), :]
        part = pl.ds(piece * BLOCKS, BLOCKS)
        copies.append(
            pltpu.make_async_copy(out_ref.at[part], out_hbm.at[part], out_sems.at[piece])
        )
        copies[piece].start()
    for copy in copies:
        copy.wait()


def transport_kernel(
    target_ref,
    arrived_ref,
    lhs_ref,
    point_ref,
    load_ref,
    potential_ref,
    out_ref,
    top_ref,
    sum_ref,
    even_ref,
    odd_ref,
    even_load_ref,
    odd_load_ref,
):
    row = iota((8, 128), 0)
    fixed = (row < 4) | (row == 7)
    factor = jnp.where(row == 7, KAPPA, 1.0)

    def find_top(t):
        tops = [arrived_ref[target_ref[t, k], 3:4, :] for k in range(CAND)]
        while len(tops) > 1:
            tops = [jnp.maximum(a, b) for a, b in zip(tops[::2], tops[1::2])]
        top = jnp.max(tops[0], axis=1, keepdims=True)
        top_ref[pl.ds(t, 1), :] = jnp.broadcast_to(top, (1, 128))

    def scores(t, e_ref, unit_ref):
        lhs = lhs_ref[t]
        centre = jnp.where(row % 4 == 3, top_ref[pl.ds(t, 1), :], 0.0)

        def spread(k):
            block = arrived_ref[target_ref[t, k]]
            both = jnp.concatenate([block, block], axis=0) - centre
            terms = both * jnp.where(fixed, factor, both)
            t1 = rounded(terms)
            rest = terms - t1
            t2 = rounded(rest)
            t3 = rest - t2
            return jnp.concatenate([t1, t2, t3, t1, t2, t1], axis=0).astype(BF16)

        total = None
        for q in range(CAND // 2):
            rhs = jnp.concatenate([spread(2 * q), spread(2 * q + 1)], axis=1)
            e = jnp.exp2(jnp.dot(lhs, rhs, preferred_element_type=F32))
            part = e[:, :128] + e[:, 128:]
            total = part if total is None else total + part
            high = e.astype(BF16)
            e_ref[q, 0:128, :] = high
            e_ref[q, 128:256, :] = (e - high.astype(F32)).astype(BF16)
        sums = jnp.sum(jnp.transpose(total), axis=0, keepdims=True)
        sum_ref[pl.ds(t, 1), :] = sums
        coords = [point_ref[c, pl.ds(t, 1), :] for c in range(3)]
        point = jnp.where(
            row % 4 == 0,
            coords[0],
            jnp.where(row % 4 == 1, coords[1], jnp.where(row % 4 == 2, coords[2], 1.0)),
        )
        loads = (load_ref[pl.ds(t, 1), :] / sums) * point
        high = rounded(loads)
        unit_ref[...] = jnp.where(row < 4, high, loads - high)

    def moments(t, e_ref, unit_ref):
        half = unit_ref[...].astype(BF16)
        lhs = jnp.concatenate([half, half], axis=1)
        for q in range(CAND // 2):
            found = jnp.dot(lhs, e_ref[q], preferred_element_type=F32)
            found = found[0:4] + found[4:8]
            out_ref[target_ref[t, 2 * q]] = found[:, :128]
            out_ref[target_ref[t, 2 * q + 1]] = found[:, 128:]

    find_top(0)

    def two_tiles(i, carry):
        t = 2 * i
        find_top(t + 1)
        scores(t, even_ref, even_load_ref)
        moments(jnp.maximum(t - 1, 0), odd_ref, odd_load_ref)
        find_top(jnp.minimum(t + 2, TILES - 1))
        scores(t + 1, odd_ref, odd_load_ref)
        moments(t, even_ref, even_load_ref)
        return carry

    lax.fori_loop(0, TILES // 2, two_tiles, 0)
    moments(TILES - 1, odd_ref, odd_load_ref)
    square = (
        (point_ref[0] - 0.5) ** 2 + (point_ref[1] - 0.5) ** 2 + (point_ref[2] - 0.5) ** 2
    )
    potential_ref[...] = jnp.log(sum_ref[...]) + (top_ref[...] - square) / EPSILON


def reduce_kernel(
    ids_ref, back_ref, start_ref, mass_hbm, centre_hbm, acc_ref, mass_ref, scale_ref, centre_ref, sems
):
    for piece in range(PIECES):
        for peer in range(BLOCKS // CAP):
            places = []
            sums = []
            for r in range(CAP):
                c = peer * CAP + r
                place = pl.ds(pl.multiple_of(ids_ref[piece, c], 4), 4)
                places.append(place)
                sums.append(acc_ref[place, :] + back_ref[piece * BLOCKS + c])
            for place, total in zip(places, sums):
                acc_ref[place, :] = total
    copies = []
    width = BLOCKS * SITE_BLOCK
    for piece in range(PIECES):
        part = pl.ds(piece * BLOCKS, BLOCKS)
        mass = acc_ref[pl.ds(piece * BLOCKS * 4 + 3, BLOCKS, stride=4), :]
        mass_ref[part, :] = mass
        copies.append(
            pltpu.make_async_copy(
                mass_ref.at[part], mass_hbm.at[part], sems.at[PIECES + piece]
            )
        )
        copies[-1].start()
        scale_ref[part, :] = 1.0 / (mass + PRIOR_MASS)
        for b in range(piece * BLOCKS, (piece + 1) * BLOCKS):
            centre_ref[:, b * SITE_BLOCK : (b + 1) * SITE_BLOCK] = (
                acc_ref[4 * b : 4 * b + 3, :] * scale_ref[b : b + 1, :]
            )
        part = pl.ds(piece * width, width)
        copies.append(
            pltpu.make_async_copy(
                centre_ref.at[:, part], centre_hbm.at[:, part], sems.at[piece]
            )
        )
        copies[-1].start()
    for copy in copies:
        copy.wait()


def shape_of(*dims, dtype=F32):
    return jax.ShapeDtypeStruct(dims, dtype)


def in_hbm(values):
    return pltpu.with_memory_space_constraint(values, pltpu.HBM)


def exchange(values):
    return lax.all_to_all(values, AXES, split_axis=0, concat_axis=0, tiled=True)


def neighbours(values, axis):
    count = lax.axis_size(axis)
    before = lax.ppermute(values, axis, [(i, (i + 1) % count) for i in range(count)])
    after = lax.ppermute(values, axis, [((i + 1) % count, i) for i in range(count)])
    return before, after


def local(
    density, point_position, block_owner, block_slot, block_count, site_position, site_weight
):
    cells = density.reshape(TILES, TILE)
    points = point_position.reshape(3, TILES, TILE)
    request, target = pl.pallas_call(
        request_kernel,
        out_shape=(
            shape_of(2 * OWNERS, 128),
            shape_of(TILES, 128, dtype=I32),
        ),
        in_specs=[HBM] * 4,
        out_specs=(VMEM, VMEM),
        scratch_shapes=[
            pltpu.VMEM((TILES, CAND), I32),
            pltpu.VMEM((TILES, CAND), I32),
            pltpu.VMEM((PZ, 1, CY), I32),
            pltpu.VMEM((TILES, TILE), F32),
            pltpu.SemaphoreType.DMA((4,)),
        ],
        compiler_params=LIMIT,
        name="request",
    )(
        in_hbm(block_owner.reshape(TILES, CAND)),
        in_hbm(block_slot.reshape(TILES, CAND)),
        in_hbm(jnp.transpose(block_count, (0, 2, 1))),
        in_hbm(cells),
    )
    asked = exchange(request)
    table = pl.pallas_call(
        table_kernel,
        out_shape=shape_of((SB_DEV + CAP) * 4, SITE_BLOCK),
        in_specs=[HBM] * 2,
        out_specs=VMEM,
        scratch_shapes=[
            pltpu.VMEM((3, SB_DEV * SITE_BLOCK), F32),
            pltpu.VMEM((SB_DEV, SITE_BLOCK), F32),
            pltpu.SemaphoreType.DMA((PIECES + 1,)),
        ],
        compiler_params=LIMIT,
        name="table",
    )(in_hbm(site_position), in_hbm(site_weight.reshape(SB_DEV, SITE_BLOCK)))
    blocks, ids = pl.pallas_call(
        gather_kernel,
        out_shape=(shape_of(SLOTS, 4, SITE_BLOCK), shape_of(8, 128, dtype=I32)),
        in_specs=[VMEM] * 2,
        out_specs=(HBM, VMEM),
        compiler_params=LIMIT,
        scratch_shapes=[
            pltpu.VMEM((SLOTS, 4, SITE_BLOCK), F32),
            pltpu.SMEM((8, 128), I32),
            pltpu.SemaphoreType.DMA,
            pltpu.SemaphoreType.DMA((PIECES,)),
        ],
        name="gather",
    )(asked, table)
    cells, points, site_position, blocks = lax.optimization_barrier(
        (cells, points, site_position, blocks)
    )
    arrived = exchange(blocks)
    above, below = neighbours(cells, "gy")
    start, lhs = pl.pallas_call(
        setup_kernel,
        out_shape=(
            shape_of((SB_DEV + CAP) * 4, SITE_BLOCK),
            shape_of(TILES, TILE, 48, dtype=BF16),
        ),
        in_specs=[HBM, VMEM],
        out_specs=(VMEM, VMEM),
        scratch_shapes=[
            pltpu.VMEM((3, SB_DEV * SITE_BLOCK), F32),
            pltpu.SemaphoreType.DMA((PIECES,)),
        ],
        compiler_params=LIMIT,
        name="setup",
    )(in_hbm(site_position), points)
    load = pl.pallas_call(
        smooth_kernel,
        out_shape=shape_of(TILES, TILE),
        in_specs=[VMEM] * 4,
        out_specs=VMEM,
        scratch_shapes=[pltpu.VMEM((PZ, 3 * CY, 128), F32)],
        compiler_params=LIMIT,
        name="smooth",
    )(asked, above, cells, below)
    potential, moments = pl.pallas_call(
        transport_kernel,
        out_shape=(shape_of(TILES, TILE), shape_of(SLOTS, 4, SITE_BLOCK)),
        in_specs=[SMEM] + [VMEM] * 4,
        out_specs=(VMEM, VMEM),
        scratch_shapes=[
            pltpu.VMEM((TILES, 128), F32),
            pltpu.VMEM((TILES, 128), F32),
            pltpu.VMEM((CAND // 2, 256, 256), BF16),
            pltpu.VMEM((CAND // 2, 256, 256), BF16),
            pltpu.VMEM((8, 128), F32),
            pltpu.VMEM((8, 128), F32),
        ],
        compiler_params=LIMIT,
        name="transport",
    )(target, arrived, lhs, points, load)
    returned = exchange(moments)
    site_mass, barycentre, _ = pl.pallas_call(
        reduce_kernel,
        out_shape=(
            shape_of(SB_DEV, SITE_BLOCK),
            shape_of(3, SB_DEV * SITE_BLOCK),
            shape_of((SB_DEV + CAP) * 4, SITE_BLOCK),
        ),
        in_specs=[SMEM] + [VMEM] * 2,
        out_specs=(HBM, HBM, VMEM),
        scratch_shapes=[
            pltpu.VMEM((SB_DEV, SITE_BLOCK), F32),
            pltpu.VMEM((SB_DEV, SITE_BLOCK), F32),
            pltpu.VMEM((3, SB_DEV * SITE_BLOCK), F32),
            pltpu.SemaphoreType.DMA((2 * PIECES,)),
        ],
        input_output_aliases={2: 2},
        compiler_params=LIMIT,
        name="reduce",
    )(ids, returned, start)
    return (
        potential.reshape(PZ, CY, TILE),
        site_mass.reshape(SB_DEV * SITE_BLOCK),
        barycentre,
    )


def solution(mesh):
    in_specs = (
        P(None, "gy", "gx"),
        P(None, None, "gy", "gx"),
        P(None, "gy", "gx"),
        P(None, "gy", "gx"),
        P(None, "gy", "gx"),
        P(None, ("gx", "gy")),
        P(("gx", "gy")),
    )
    out_specs = (P(None, "gy", "gx"), P(("gx", "gy")), P(None, ("gx", "gy")))
    return jax.shard_map(local, mesh=mesh, in_specs=in_specs, out_specs=out_specs, check_vma=False)
```

```python
import math

import jax
import jax.numpy as jnp
import numpy as np
from jax import lax
from jax.experimental import pallas as pl
from jax.experimental.pallas import tpu as pltpu
from jax.sharding import PartitionSpec as P

PZ = 2
CY = 8
TILE = 128
CAND = 16
SITE_BLOCK = 128
SB_DEV = 512
HALF = 8
CAP = 4
OWNERS = 128
TILES = PZ * CY
SLOTS = OWNERS * CAP
ENTRIES = TILES * CAND

EPSILON = 0.05
PRIOR_MASS = 0.5
SIGMA_CELLS = 4.0
KAPPA = math.log2(math.e) / EPSILON
ROOT = math.sqrt(KAPPA)
DEAD = -1e30
PIECES = 4
BLOCKS = SB_DEV // PIECES
F32 = jnp.float32
BF16 = jnp.bfloat16
I32 = jnp.int32
VMEM = pl.BlockSpec(memory_space=pltpu.VMEM)
HBM = pl.BlockSpec(memory_space=pltpu.HBM)
SMEM = pl.BlockSpec(memory_space=pltpu.SMEM)
AXES = ("gx", "gy")
LIMIT = pltpu.CompilerParams(vmem_limit_bytes=8 << 20)


def gauss_values():
    offsets = np.arange(-HALF, HALF + 1, dtype=np.float64)
    values = np.exp(-offsets * offsets / (2.0 * SIGMA_CELLS * SIGMA_CELLS))
    return values / values.sum()


GAUSS = [float(v) for v in gauss_values()]
GAUSS_PEAK = GAUSS[HALF]


def iota(shape, dim):
    return lax.broadcasted_iota(I32, shape, dim)


def rounded(values):
    return values.astype(BF16).astype(F32)


def request_kernel(
    owner_hbm,
    slot_hbm,
    count_hbm,
    cells_hbm,
    request_ref,
    target_ref,
    owner_ref,
    slot_ref,
    count_ref,
    cells_ref,
    sems,
):
    copies = [
        pltpu.make_async_copy(owner_hbm, owner_ref, sems.at[0]),
        pltpu.make_async_copy(slot_hbm, slot_ref, sems.at[1]),
        pltpu.make_async_copy(count_hbm, count_ref, sems.at[2]),
        pltpu.make_async_copy(cells_hbm, cells_ref, sems.at[3]),
    ]
    for copy in copies:
        copy.start()
    corner = iota((CY, CY), 0) == iota((CY, CY), 1)
    square = (ENTRIES, ENTRIES)
    upper = (iota(square, 0) < iota(square, 1)).astype(F32).astype(BF16)
    pick = (iota((CAND, ENTRIES), 0) == iota((CAND, ENTRIES), 1) % CAND).astype(F32).astype(BF16)
    own_tile = iota((TILES, ENTRIES), 0) == iota((TILES, ENTRIES), 1) // CAND
    fold = (iota((ENTRIES, 128), 0) % CAND == iota((ENTRIES, 128), 1)).astype(F32)
    fold = jnp.concatenate([fold * CAP, fold], axis=0).astype(BF16)
    repeat = (iota((2 * CAP, 128), 0) % CAP == iota((2 * CAP, 128), 1) % CAP).astype(F32)
    for copy in copies:
        copy.wait()
    counts = jnp.concatenate(
        [
            jnp.sum(jnp.where(corner, count_ref[z], 0), axis=1, keepdims=True)
            for z in range(PZ)
        ],
        axis=0,
    )
    value = jnp.where(iota((TILES, CAND), 1) < counts, slot_ref[...] + 1, 0)
    parts = jnp.concatenate([owner_ref[...], value & -32, value & 31], axis=0)
    parts = jnp.dot(parts.astype(F32).astype(BF16), pick, preferred_element_type=F32)
    owner, high_part, low_part = [
        jnp.sum(
            jnp.where(own_tile, parts[g * TILES : (g + 1) * TILES], 0.0), axis=0, keepdims=True
        )
        for g in range(3)
    ]
    hot = (iota((OWNERS, ENTRIES), 0).astype(F32) == owner).astype(F32)
    hot_low = hot.astype(BF16)
    before = jnp.dot(hot_low, upper, preferred_element_type=F32)
    rank = jnp.sum(before * hot, axis=0, keepdims=True)
    shape = (2 * CAP, ENTRIES)
    own_rank = (iota(shape, 0) % CAP).astype(F32) == rank
    spread = jnp.where(own_rank, jnp.where(iota(shape, 0) < CAP, high_part, low_part), 0.0)
    request = lax.dot_general(
        hot_low, spread.astype(BF16), (((1,), (1,)), ((), ())), preferred_element_type=F32
    )
    request = jnp.dot(request.astype(BF16), repeat.astype(BF16), preferred_element_type=F32)
    request_ref[pl.ds(0, OWNERS, stride=2), :] = request - 1.0
    place = jnp.concatenate(
        [jnp.where(own_tile, owner, 0.0), jnp.where(own_tile, rank, 0.0)], axis=1
    )
    place = jnp.dot(place.astype(BF16), fold, preferred_element_type=F32)
    target_ref[...] = place.astype(I32)
    edge_shape = (TILE, 2 * TILE)
    edge_lane = iota(edge_shape, 1)
    column = jnp.where(edge_lane < TILE, 0, TILE - HALF) + edge_lane % HALF
    pick = (iota(edge_shape, 0) == column).astype(F32)
    edges = jnp.dot(
        cells_ref[...], pick, preferred_element_type=F32, precision=lax.Precision.HIGHEST
    )
    edge_shape = (TILES, 2 * TILE)
    own_row = (iota(edge_shape, 1) % TILE) // HALF == iota(edge_shape, 0)
    edges = jnp.sum(jnp.where(own_row, edges, 0.0), axis=0, keepdims=True)
    columns = lax.axis_size("gx")
    after = lax.rem(lax.axis_index("gx") + 1, columns)
    to_after = iota((OWNERS, 128), 0) // (OWNERS // columns) == after
    request_ref[pl.ds(1, OWNERS, stride=2), :] = jnp.where(
        to_after, edges[:, TILE:], edges[:, :TILE]
    )


def prepare(point_ref, lhs_ref):
    row = iota((8, 128), 0)

    def tile(t, carry):
        coords = [point_ref[c, pl.ds(t, 1), :] for c in range(3)]
        point = jnp.where(row == 0, coords[0], jnp.where(row == 1, coords[1], coords[2]))
        scaled = jnp.where(row < 3, (2.0 * ROOT) * (point - 0.5), 0.0)
        a1 = rounded(scaled)
        rest = scaled - a1
        a2 = rounded(rest)
        a3 = rest - a2
        lead = jnp.where(row == 7, 1.0, jnp.where(row >= 4, -1.0, a1))
        lhs = jnp.concatenate([lead, a2, lead, a2, lead, a3], axis=0)
        lhs_ref[t] = jnp.transpose(lhs).astype(BF16)
        return carry

    lax.fori_loop(0, TILES, tile, 0, unroll=4)


def piece_copies(source, target, sems):
    width = SB_DEV * SITE_BLOCK // PIECES
    copies = []
    for piece in range(PIECES):
        part = pl.ds(piece * width, width)
        copies.append(
            pltpu.make_async_copy(source.at[:, part], target.at[:, part], sems.at[piece])
        )
    return copies


def table_kernel(position_hbm, weight_hbm, table_ref, position_ref, weight_ref, sems):
    weights = pltpu.make_async_copy(weight_hbm, weight_ref, sems.at[PIECES])
    copies = piece_copies(position_hbm, position_ref, sems)
    weights.start()
    for copy in copies:
        copy.start()
    dead = jnp.where(iota((4, 128), 0) == 3, DEAD, 0.0)
    for r in range(CAP):
        table_ref[(SB_DEV + r) * 4 : (SB_DEV + r + 1) * 4, :] = dead
    weights.wait()
    for piece in range(PIECES):
        copies[piece].wait()
        for b in range(piece * BLOCKS, (piece + 1) * BLOCKS):
            place = position_ref[:, b * SITE_BLOCK : (b + 1) * SITE_BLOCK]
            table_ref[4 * b : 4 * b + 3, :] = (place - 0.5) * ROOT
            table_ref[4 * b + 3 : 4 * b + 4, :] = weight_ref[b : b + 1, :]


def setup_kernel(position_hbm, point_ref, start_ref, lhs_ref, position_ref, sems):
    copies = piece_copies(position_hbm, position_ref, sems)
    for copy in copies:
        copy.start()
    prepare(point_ref, lhs_ref)
    for r in range(CAP):
        start_ref[(SB_DEV + r) * 4 : (SB_DEV + r + 1) * 4, :] = jnp.zeros((4, 128), F32)

    def block(b, carry):
        start = pl.multiple_of(b * SITE_BLOCK, SITE_BLOCK)
        line = pl.multiple_of(b * 4, 4)
        start_ref[pl.ds(line, 3), :] = PRIOR_MASS * position_ref[:, pl.ds(start, SITE_BLOCK)]
        start_ref[pl.ds(line + 3, 1), :] = jnp.zeros((1, 128), F32)
        return carry

    for piece in range(PIECES):
        copies[piece].wait()
        lax.fori_loop(piece * BLOCKS, (piece + 1) * BLOCKS, block, 0, unroll=8)


def smooth_kernel(halo_ref, above_ref, mid_ref, below_ref, load_ref, rows_ref):
    tiles = (above_ref[...], mid_ref[...], below_ref[...])
    count_x, count_y = lax.axis_size("gx"), lax.axis_size("gy")
    here_x, here_y = lax.axis_index("gx"), lax.axis_index("gy")
    shape = (3 * TILE, TILE)
    row = iota(shape, 0)
    source = jnp.where(
        row < TILE, row, row % HALF + jnp.where(row < 2 * TILE, -HALF, TILE)
    )
    shift = (source - iota(shape, 1)).astype(F32)
    taps = jnp.where(
        jnp.abs(shift) <= HALF,
        GAUSS_PEAK * jnp.exp(shift * shift * (-0.5 / (SIGMA_CELLS * SIGMA_CELLS))),
        0.0,
    )
    shape = (TILES, TILE)
    own_row = iota(shape, 1) // HALF == iota(shape, 0)
    rows = []
    for step, tile in zip((count_y - 1, 0, 1), tiles):
        parts = [tile]
        for side in (count_x - 1, 1):
            peer = lax.rem(here_x + side, count_x) * count_y + lax.rem(here_y + step, count_y)
            halo = halo_ref[pl.ds(2 * peer + 1, 1), :]
            parts.append(jnp.where(own_row, halo, 0.0))
        rows.append(jnp.concatenate(parts, axis=1))
    first = jnp.dot(
        jnp.concatenate(rows, axis=0),
        taps,
        preferred_element_type=F32,
        precision=lax.Precision.HIGHEST,
    )
    planes = []
    for z in range(PZ):
        for part in range(3):
            at = part * TILES + z * CY
            rows_ref[z, part * CY : (part + 1) * CY, :] = first[at : at + CY]
        total = GAUSS[0] * rows_ref[z, 0:CY, :]
        for j in range(1, 2 * HALF + 1):
            total = total + GAUSS[j] * rows_ref[z, j : j + CY, :]
        planes.append(total)
    load_ref[0:CY, :] = GAUSS[HALF] * planes[0] + GAUSS[HALF + 1] * planes[1]
    load_ref[CY : 2 * CY, :] = GAUSS[HALF - 1] * planes[0] + GAUSS[HALF] * planes[1]


def gather_kernel(asked_ref, table_ref, out_hbm, ids_ref, out_ref, ids_smem, sem, out_sems):
    shape = (OWNERS, 128)
    asked = asked_ref[pl.ds(0, OWNERS, stride=2), :]
    lane = iota(shape, 1)
    place = jnp.where(asked < 0.0, (SB_DEV + lane % CAP).astype(F32), asked) * 4.0
    own = iota(shape, 0) % (128 // CAP) == lane // CAP
    place = jnp.where(own, place, 0.0)
    rows = [
        jnp.sum(place[g * 32 : (g + 1) * 32], axis=0, keepdims=True) for g in range(PIECES)
    ]
    ids_ref[...] = jnp.concatenate(rows + rows, axis=0).astype(I32)
    copy = pltpu.make_async_copy(ids_ref, ids_smem, sem)
    copy.start()
    copy.wait()
    copies = []
    for piece in range(PIECES):
        for c in range(BLOCKS):
            line = pl.multiple_of(ids_smem[piece, c], 4)
            out_ref[piece * BLOCKS + c] = table_ref[pl.ds(line, 4), :]
        part = pl.ds(piece * BLOCKS, BLOCKS)
        copies.append(
            pltpu.make_async_copy(out_ref.at[part], out_hbm.at[part], out_sems.at[piece])
        )
        copies[piece].start()
    for copy in copies:
        copy.wait()


def transport_kernel(
    target_ref,
    arrived_ref,
    lhs_ref,
    point_ref,
    load_ref,
    potential_ref,
    out_ref,
    top_ref,
    sum_ref,
    even_ref,
    odd_ref,
    even_load_ref,
    odd_load_ref,
):
    row = iota((8, 128), 0)
    fixed = (row < 4) | (row == 7)
    factor = jnp.where(row == 7, KAPPA, 1.0)

    def find_top(t):
        tops = [arrived_ref[target_ref[t, k], 3:4, :] for k in range(CAND)]
        while len(tops) > 1:
            tops = [jnp.maximum(a, b) for a, b in zip(tops[::2], tops[1::2])]
        top = jnp.max(tops[0], axis=1, keepdims=True)
        top_ref[pl.ds(t, 1), :] = jnp.broadcast_to(top, (1, 128))

    def scores(t, e_ref, unit_ref):
        lhs = lhs_ref[t]
        centre = jnp.where(row % 4 == 3, top_ref[pl.ds(t, 1), :], 0.0)

        def spread(k):
            block = arrived_ref[target_ref[t, k]]
            both = jnp.concatenate([block, block], axis=0) - centre
            terms = both * jnp.where(fixed, factor, both)
            t1 = jnp.concatenate([terms, terms], axis=0).astype(BF16)
            first = t1.astype(F32)[:8]
            rest = terms - first
            t2 = jnp.concatenate([rest, rest], axis=0).astype(BF16)
            t3 = rest - t2.astype(F32)[:8]
            return jnp.concatenate(
                [t1, t2, jnp.concatenate([t3, first], axis=0).astype(BF16)], axis=0
            )

        total = None
        for q in range(CAND // 2):
            rhs = jnp.concatenate([spread(2 * q), spread(2 * q + 1)], axis=1)
            e = jnp.exp2(jnp.dot(lhs, rhs, preferred_element_type=F32))
            part = e[:, :128] + e[:, 128:]
            total = part if total is None else total + part
            high = e.astype(BF16)
            e_ref[q, 0:128, :] = high
            e_ref[q, 128:256, :] = (e - high.astype(F32)).astype(BF16)
        sums = jnp.sum(jnp.transpose(total), axis=0, keepdims=True)
        sum_ref[pl.ds(t, 1), :] = sums
        coords = [point_ref[c, pl.ds(t, 1), :] for c in range(3)]
        point = jnp.where(
            row % 4 == 0,
            coords[0],
            jnp.where(row % 4 == 1, coords[1], jnp.where(row % 4 == 2, coords[2], 1.0)),
        )
        loads = (load_ref[pl.ds(t, 1), :] / sums) * point
        high = rounded(loads)
        unit_ref[...] = jnp.where(row < 4, high, loads - high)

    def moments(t, e_ref, unit_ref):
        half = unit_ref[...].astype(BF16)
        lhs = jnp.concatenate([half, half], axis=1)
        for q in range(CAND // 2):
            found = jnp.dot(lhs, e_ref[q], preferred_element_type=F32)
            found = found[0:4] + found[4:8]
            out_ref[target_ref[t, 2 * q]] = found[:, :128]
            out_ref[target_ref[t, 2 * q + 1]] = found[:, 128:]

    find_top(0)

    def two_tiles(i, carry):
        t = 2 * i
        find_top(t + 1)
        scores(t, even_ref, even_load_ref)
        moments(jnp.maximum(t - 1, 0), odd_ref, odd_load_ref)
        find_top(jnp.minimum(t + 2, TILES - 1))
        scores(t + 1, odd_ref, odd_load_ref)
        moments(t, even_ref, even_load_ref)
        return carry

    lax.fori_loop(0, TILES // 2, two_tiles, 0)
    moments(TILES - 1, odd_ref, odd_load_ref)
    square = (
        (point_ref[0] - 0.5) ** 2 + (point_ref[1] - 0.5) ** 2 + (point_ref[2] - 0.5) ** 2
    )
    potential_ref[...] = jnp.log(sum_ref[...]) + (top_ref[...] - square) / EPSILON


def reduce_kernel(
    ids_ref,
    back_ref,
    start_ref,
    mass_hbm,
    centre_hbm,
    acc_ref,
    other_ref,
    mass_ref,
    scale_ref,
    centre_ref,
    sems,
):
    other_ref[...] = jnp.zeros_like(other_ref)
    for piece in range(PIECES):
        for peer in range(BLOCKS // CAP):
            into = (acc_ref, other_ref)[peer % 2]
            places = []
            sums = []
            for r in range(CAP):
                c = peer * CAP + r
                place = pl.ds(pl.multiple_of(ids_ref[piece, c], 4), 4)
                places.append(place)
                sums.append(into[place, :] + back_ref[piece * BLOCKS + c])
            for place, total in zip(places, sums):
                into[place, :] = total
    copies = []
    width = BLOCKS * SITE_BLOCK
    for piece in range(PIECES):
        part = pl.ds(piece * BLOCKS, BLOCKS)
        lines = pl.ds(piece * BLOCKS * 4 + 3, BLOCKS, stride=4)
        mass = acc_ref[lines, :] + other_ref[lines, :]
        mass_ref[part, :] = mass
        copies.append(
            pltpu.make_async_copy(
                mass_ref.at[part], mass_hbm.at[part], sems.at[PIECES + piece]
            )
        )
        copies[-1].start()
        scale_ref[part, :] = 1.0 / (mass + PRIOR_MASS)
        for b in range(piece * BLOCKS, (piece + 1) * BLOCKS):
            centre_ref[:, b * SITE_BLOCK : (b + 1) * SITE_BLOCK] = (
                acc_ref[4 * b : 4 * b + 3, :] + other_ref[4 * b : 4 * b + 3, :]
            ) * scale_ref[b : b + 1, :]
        part = pl.ds(piece * width, width)
        copies.append(
            pltpu.make_async_copy(
                centre_ref.at[:, part], centre_hbm.at[:, part], sems.at[piece]
            )
        )
        copies[-1].start()
    for copy in copies:
        copy.wait()


def shape_of(*dims, dtype=F32):
    return jax.ShapeDtypeStruct(dims, dtype)


def in_hbm(values):
    return pltpu.with_memory_space_constraint(values, pltpu.HBM)


def exchange(values):
    return lax.all_to_all(values, AXES, split_axis=0, concat_axis=0, tiled=True)


def neighbours(values, axis):
    count = lax.axis_size(axis)
    before = lax.ppermute(values, axis, [(i, (i + 1) % count) for i in range(count)])
    after = lax.ppermute(values, axis, [((i + 1) % count, i) for i in range(count)])
    return before, after


def local(
    density, point_position, block_owner, block_slot, block_count, site_position, site_weight
):
    cells = density.reshape(TILES, TILE)
    points = point_position.reshape(3, TILES, TILE)
    request, target = pl.pallas_call(
        request_kernel,
        out_shape=(
            shape_of(2 * OWNERS, 128),
            shape_of(TILES, 128, dtype=I32),
        ),
        in_specs=[HBM] * 4,
        out_specs=(VMEM, VMEM),
        scratch_shapes=[
            pltpu.VMEM((TILES, CAND), I32),
            pltpu.VMEM((TILES, CAND), I32),
            pltpu.VMEM((PZ, 1, CY), I32),
            pltpu.VMEM((TILES, TILE), F32),
            pltpu.SemaphoreType.DMA((4,)),
        ],
        compiler_params=LIMIT,
        name="request",
    )(
        in_hbm(block_owner.reshape(TILES, CAND)),
        in_hbm(block_slot.reshape(TILES, CAND)),
        in_hbm(jnp.transpose(block_count, (0, 2, 1))),
        in_hbm(cells),
    )
    asked = exchange(request)
    table = pl.pallas_call(
        table_kernel,
        out_shape=shape_of((SB_DEV + CAP) * 4, SITE_BLOCK),
        in_specs=[HBM] * 2,
        out_specs=VMEM,
        scratch_shapes=[
            pltpu.VMEM((3, SB_DEV * SITE_BLOCK), F32),
            pltpu.VMEM((SB_DEV, SITE_BLOCK), F32),
            pltpu.SemaphoreType.DMA((PIECES + 1,)),
        ],
        compiler_params=LIMIT,
        name="table",
    )(in_hbm(site_position), in_hbm(site_weight.reshape(SB_DEV, SITE_BLOCK)))
    blocks, ids = pl.pallas_call(
        gather_kernel,
        out_shape=(shape_of(SLOTS, 4, SITE_BLOCK), shape_of(8, 128, dtype=I32)),
        in_specs=[VMEM] * 2,
        out_specs=(HBM, VMEM),
        compiler_params=LIMIT,
        scratch_shapes=[
            pltpu.VMEM((SLOTS, 4, SITE_BLOCK), F32),
            pltpu.SMEM((8, 128), I32),
            pltpu.SemaphoreType.DMA,
            pltpu.SemaphoreType.DMA((PIECES,)),
        ],
        name="gather",
    )(asked, table)
    cells, points, site_position, blocks = lax.optimization_barrier(
        (cells, points, site_position, blocks)
    )
    arrived = exchange(blocks)
    above, below = neighbours(cells, "gy")
    start, lhs = pl.pallas_call(
        setup_kernel,
        out_shape=(
            shape_of((SB_DEV + CAP) * 4, SITE_BLOCK),
            shape_of(TILES, TILE, 48, dtype=BF16),
        ),
        in_specs=[HBM, VMEM],
        out_specs=(VMEM, VMEM),
        scratch_shapes=[
            pltpu.VMEM((3, SB_DEV * SITE_BLOCK), F32),
            pltpu.SemaphoreType.DMA((PIECES,)),
        ],
        compiler_params=LIMIT,
        name="setup",
    )(in_hbm(site_position), points)
    load = pl.pallas_call(
        smooth_kernel,
        out_shape=shape_of(TILES, TILE),
        in_specs=[VMEM] * 4,
        out_specs=VMEM,
        scratch_shapes=[pltpu.VMEM((PZ, 3 * CY, 128), F32)],
        compiler_params=LIMIT,
        name="smooth",
    )(asked, above, cells, below)
    potential, moments = pl.pallas_call(
        transport_kernel,
        out_shape=(shape_of(TILES, TILE), shape_of(SLOTS, 4, SITE_BLOCK)),
        in_specs=[SMEM] + [VMEM] * 4,
        out_specs=(VMEM, VMEM),
        scratch_shapes=[
            pltpu.VMEM((TILES, 128), F32),
            pltpu.VMEM((TILES, 128), F32),
            pltpu.VMEM((CAND // 2, 256, 256), BF16),
            pltpu.VMEM((CAND // 2, 256, 256), BF16),
            pltpu.VMEM((8, 128), F32),
            pltpu.VMEM((8, 128), F32),
        ],
        compiler_params=LIMIT,
        name="transport",
    )(target, arrived, lhs, points, load)
    returned = exchange(moments)
    site_mass, barycentre, _ = pl.pallas_call(
        reduce_kernel,
        out_shape=(
            shape_of(SB_DEV, SITE_BLOCK),
            shape_of(3, SB_DEV * SITE_BLOCK),
            shape_of((SB_DEV + CAP) * 4, SITE_BLOCK),
        ),
        in_specs=[SMEM] + [VMEM] * 2,
        out_specs=(HBM, HBM, VMEM),
        scratch_shapes=[
            pltpu.VMEM(((SB_DEV + CAP) * 4, SITE_BLOCK), F32),
            pltpu.VMEM((SB_DEV, SITE_BLOCK), F32),
            pltpu.VMEM((SB_DEV, SITE_BLOCK), F32),
            pltpu.VMEM((3, SB_DEV * SITE_BLOCK), F32),
            pltpu.SemaphoreType.DMA((2 * PIECES,)),
        ],
        input_output_aliases={2: 2},
        compiler_params=LIMIT,
        name="reduce",
    )(ids, returned, start)
    return (
        potential.reshape(PZ, CY, TILE),
        site_mass.reshape(SB_DEV * SITE_BLOCK),
        barycentre,
    )


def solution(mesh):
    in_specs = (
        P(None, "gy", "gx"),
        P(None, None, "gy", "gx"),
        P(None, "gy", "gx"),
        P(None, "gy", "gx"),
        P(None, "gy", "gx"),
        P(None, ("gx", "gy")),
        P(("gx", "gy")),
    )
    out_specs = (P(None, "gy", "gx"), P(("gx", "gy")), P(None, ("gx", "gy")))
    return jax.shard_map(local, mesh=mesh, in_specs=in_specs, out_specs=out_specs, check_vma=False)
```

```python
import math

import jax
import jax.numpy as jnp
import numpy as np
from jax import lax
from jax.experimental import pallas as pl
from jax.experimental.pallas import tpu as pltpu
from jax.sharding import PartitionSpec as P

PZ = 2
CY = 8
TILE = 128
CAND = 16
SITE_BLOCK = 128
SB_DEV = 512
HALF = 8
CAP = 4
OWNERS = 128
TILES = PZ * CY
SLOTS = OWNERS * CAP
ENTRIES = TILES * CAND

EPSILON = 0.05
PRIOR_MASS = 0.5
SIGMA_CELLS = 4.0
KAPPA = math.log2(math.e) / EPSILON
ROOT = math.sqrt(KAPPA)
DEAD = -1e30
PIECES = 4
BLOCKS = SB_DEV // PIECES
F32 = jnp.float32
BF16 = jnp.bfloat16
I32 = jnp.int32
VMEM = pl.BlockSpec(memory_space=pltpu.VMEM)
HBM = pl.BlockSpec(memory_space=pltpu.HBM)
SMEM = pl.BlockSpec(memory_space=pltpu.SMEM)
AXES = ("gx", "gy")
LIMIT = pltpu.CompilerParams(vmem_limit_bytes=8 << 20)


def gauss_values():
    offsets = np.arange(-HALF, HALF + 1, dtype=np.float64)
    values = np.exp(-offsets * offsets / (2.0 * SIGMA_CELLS * SIGMA_CELLS))
    return values / values.sum()


GAUSS = [float(v) for v in gauss_values()]
GAUSS_PEAK = GAUSS[HALF]


def iota(shape, dim):
    return lax.broadcasted_iota(I32, shape, dim)


def rounded(values):
    return values.astype(BF16).astype(F32)


def request_kernel(
    owner_hbm,
    slot_hbm,
    count_hbm,
    cells_hbm,
    request_ref,
    target_ref,
    owner_ref,
    slot_ref,
    count_ref,
    cells_ref,
    sems,
):
    copies = [
        pltpu.make_async_copy(owner_hbm, owner_ref, sems.at[0]),
        pltpu.make_async_copy(slot_hbm, slot_ref, sems.at[1]),
        pltpu.make_async_copy(count_hbm, count_ref, sems.at[2]),
        pltpu.make_async_copy(cells_hbm, cells_ref, sems.at[3]),
    ]
    for copy in copies:
        copy.start()
    corner = iota((CY, CY), 0) == iota((CY, CY), 1)
    square = (ENTRIES, ENTRIES)
    upper = (iota(square, 0) < iota(square, 1)).astype(F32).astype(BF16)
    pick = (iota((CAND, ENTRIES), 0) == iota((CAND, ENTRIES), 1) % CAND).astype(F32).astype(BF16)
    own_tile = iota((TILES, ENTRIES), 0) == iota((TILES, ENTRIES), 1) // CAND
    fold = (iota((ENTRIES, 128), 0) % CAND == iota((ENTRIES, 128), 1)).astype(F32)
    fold = jnp.concatenate([fold * CAP, fold], axis=0).astype(BF16)
    repeat = (iota((2 * CAP, 128), 0) % CAP == iota((2 * CAP, 128), 1) % CAP).astype(F32)
    for copy in copies:
        copy.wait()
    counts = jnp.concatenate(
        [
            jnp.sum(jnp.where(corner, count_ref[z], 0), axis=1, keepdims=True)
            for z in range(PZ)
        ],
        axis=0,
    )
    value = jnp.where(iota((TILES, CAND), 1) < counts, slot_ref[...] + 1, 0)
    parts = jnp.concatenate([owner_ref[...], value & -32, value & 31], axis=0)
    parts = jnp.dot(parts.astype(F32).astype(BF16), pick, preferred_element_type=F32)
    owner, high_part, low_part = [
        jnp.sum(
            jnp.where(own_tile, parts[g * TILES : (g + 1) * TILES], 0.0), axis=0, keepdims=True
        )
        for g in range(3)
    ]
    hot = (iota((OWNERS, ENTRIES), 0).astype(F32) == owner).astype(F32)
    hot_low = hot.astype(BF16)
    before = jnp.dot(hot_low, upper, preferred_element_type=F32)
    rank = jnp.sum(before * hot, axis=0, keepdims=True)
    shape = (2 * CAP, ENTRIES)
    own_rank = (iota(shape, 0) % CAP).astype(F32) == rank
    spread = jnp.where(own_rank, jnp.where(iota(shape, 0) < CAP, high_part, low_part), 0.0)
    request = lax.dot_general(
        hot_low, spread.astype(BF16), (((1,), (1,)), ((), ())), preferred_element_type=F32
    )
    request = jnp.dot(request.astype(BF16), repeat.astype(BF16), preferred_element_type=F32)
    request_ref[pl.ds(0, OWNERS, stride=2), :] = request - 1.0
    place = jnp.concatenate(
        [jnp.where(own_tile, owner, 0.0), jnp.where(own_tile, rank, 0.0)], axis=1
    )
    place = jnp.dot(place.astype(BF16), fold, preferred_element_type=F32)
    target_ref[...] = place.astype(I32)
    edge_shape = (TILE, 2 * TILE)
    edge_lane = iota(edge_shape, 1)
    column = jnp.where(edge_lane < TILE, 0, TILE - HALF) + edge_lane % HALF
    pick = (iota(edge_shape, 0) == column).astype(F32)
    edges = jnp.dot(
        cells_ref[...], pick, preferred_element_type=F32, precision=lax.Precision.HIGHEST
    )
    edge_shape = (TILES, 2 * TILE)
    own_row = (iota(edge_shape, 1) % TILE) // HALF == iota(edge_shape, 0)
    edges = jnp.sum(jnp.where(own_row, edges, 0.0), axis=0, keepdims=True)
    columns = lax.axis_size("gx")
    after = lax.rem(lax.axis_index("gx") + 1, columns)
    to_after = iota((OWNERS, 128), 0) // (OWNERS // columns) == after
    request_ref[pl.ds(1, OWNERS, stride=2), :] = jnp.where(
        to_after, edges[:, TILE:], edges[:, :TILE]
    )


def prepare(point_ref, lhs_ref):
    row = iota((8, 128), 0)

    def tile(t, carry):
        coords = [point_ref[c, pl.ds(t, 1), :] for c in range(3)]
        point = jnp.where(row == 0, coords[0], jnp.where(row == 1, coords[1], coords[2]))
        scaled = jnp.where(row < 3, (2.0 * ROOT) * (point - 0.5), 0.0)
        a1 = rounded(scaled)
        rest = scaled - a1
        a2 = rounded(rest)
        a3 = rest - a2
        lead = jnp.where(row == 7, 1.0, jnp.where(row >= 4, -1.0, a1))
        lhs = jnp.concatenate([lead, a2, lead, a2, lead, a3], axis=0)
        lhs_ref[t] = jnp.transpose(lhs).astype(BF16)
        return carry

    lax.fori_loop(0, TILES, tile, 0, unroll=4)


def piece_copies(source, target, sems):
    width = SB_DEV * SITE_BLOCK // PIECES
    copies = []
    for piece in range(PIECES):
        part = pl.ds(piece * width, width)
        copies.append(
            pltpu.make_async_copy(source.at[:, part], target.at[:, part], sems.at[piece])
        )
    return copies


def table_kernel(position_hbm, weight_hbm, table_ref, position_ref, weight_ref, sems):
    weights = pltpu.make_async_copy(weight_hbm, weight_ref, sems.at[PIECES])
    copies = piece_copies(position_hbm, position_ref, sems)
    weights.start()
    for copy in copies:
        copy.start()
    dead = jnp.where(iota((4, 128), 0) == 3, DEAD, 0.0)
    for r in range(CAP):
        table_ref[(SB_DEV + r) * 4 : (SB_DEV + r + 1) * 4, :] = dead
    weights.wait()
    for piece in range(PIECES):
        copies[piece].wait()
        for b in range(piece * BLOCKS, (piece + 1) * BLOCKS):
            place = position_ref[:, b * SITE_BLOCK : (b + 1) * SITE_BLOCK]
            table_ref[4 * b : 4 * b + 3, :] = (place - 0.5) * ROOT
            table_ref[4 * b + 3 : 4 * b + 4, :] = weight_ref[b : b + 1, :]


def setup_kernel(position_hbm, point_ref, start_ref, lhs_ref, position_ref, sems):
    copies = piece_copies(position_hbm, position_ref, sems)
    for copy in copies:
        copy.start()
    prepare(point_ref, lhs_ref)
    for r in range(CAP):
        start_ref[(SB_DEV + r) * 4 : (SB_DEV + r + 1) * 4, :] = jnp.zeros((4, 128), F32)

    def block(b, carry):
        start = pl.multiple_of(b * SITE_BLOCK, SITE_BLOCK)
        line = pl.multiple_of(b * 4, 4)
        start_ref[pl.ds(line, 3), :] = PRIOR_MASS * position_ref[:, pl.ds(start, SITE_BLOCK)]
        start_ref[pl.ds(line + 3, 1), :] = jnp.zeros((1, 128), F32)
        return carry

    for piece in range(PIECES):
        copies[piece].wait()
        lax.fori_loop(piece * BLOCKS, (piece + 1) * BLOCKS, block, 0, unroll=8)


def smooth_kernel(halo_ref, above_ref, mid_ref, below_ref, load_ref, rows_ref):
    tiles = (above_ref[...], mid_ref[...], below_ref[...])
    count_x, count_y = lax.axis_size("gx"), lax.axis_size("gy")
    here_x, here_y = lax.axis_index("gx"), lax.axis_index("gy")
    shape = (3 * TILE, TILE)
    row = iota(shape, 0)
    source = jnp.where(
        row < TILE, row, row % HALF + jnp.where(row < 2 * TILE, -HALF, TILE)
    )
    shift = (source - iota(shape, 1)).astype(F32)
    taps = jnp.where(
        jnp.abs(shift) <= HALF,
        GAUSS_PEAK * jnp.exp(shift * shift * (-0.5 / (SIGMA_CELLS * SIGMA_CELLS))),
        0.0,
    )
    shape = (TILES, TILE)
    own_row = iota(shape, 1) // HALF == iota(shape, 0)
    rows = []
    for step, tile in zip((count_y - 1, 0, 1), tiles):
        parts = [tile]
        for side in (count_x - 1, 1):
            peer = lax.rem(here_x + side, count_x) * count_y + lax.rem(here_y + step, count_y)
            halo = halo_ref[pl.ds(2 * peer + 1, 1), :]
            parts.append(jnp.where(own_row, halo, 0.0))
        rows.append(jnp.concatenate(parts, axis=1))
    first = jnp.dot(
        jnp.concatenate(rows, axis=0),
        taps,
        preferred_element_type=F32,
        precision=lax.Precision.HIGHEST,
    )
    planes = []
    for z in range(PZ):
        for part in range(3):
            at = part * TILES + z * CY
            rows_ref[z, part * CY : (part + 1) * CY, :] = first[at : at + CY]
        total = GAUSS[0] * rows_ref[z, 0:CY, :]
        for j in range(1, 2 * HALF + 1):
            total = total + GAUSS[j] * rows_ref[z, j : j + CY, :]
        planes.append(total)
    load_ref[0:CY, :] = GAUSS[HALF] * planes[0] + GAUSS[HALF + 1] * planes[1]
    load_ref[CY : 2 * CY, :] = GAUSS[HALF - 1] * planes[0] + GAUSS[HALF] * planes[1]


def gather_kernel(asked_ref, table_ref, out_hbm, ids_ref, out_ref, ids_smem, sem, out_sems):
    shape = (OWNERS, 128)
    asked = asked_ref[pl.ds(0, OWNERS, stride=2), :]
    lane = iota(shape, 1)
    place = jnp.where(asked < 0.0, (SB_DEV + lane % CAP).astype(F32), asked) * 4.0
    own = iota(shape, 0) % (128 // CAP) == lane // CAP
    place = jnp.where(own, place, 0.0)
    rows = [
        jnp.sum(place[g * 32 : (g + 1) * 32], axis=0, keepdims=True) for g in range(PIECES)
    ]
    ids_ref[...] = jnp.concatenate(rows + rows, axis=0).astype(I32)
    copy = pltpu.make_async_copy(ids_ref, ids_smem, sem)
    copy.start()
    copy.wait()
    copies = []
    for piece in range(PIECES):
        for c in range(BLOCKS):
            line = pl.multiple_of(ids_smem[piece, c], 4)
            out_ref[piece * BLOCKS + c] = table_ref[pl.ds(line, 4), :]
        part = pl.ds(piece * BLOCKS, BLOCKS)
        copies.append(
            pltpu.make_async_copy(out_ref.at[part], out_hbm.at[part], out_sems.at[piece])
        )
        copies[piece].start()
    for copy in copies:
        copy.wait()


def transport_kernel(
    target_ref,
    arrived_ref,
    lhs_ref,
    point_ref,
    load_ref,
    potential_ref,
    out_ref,
    top_ref,
    sum_ref,
    even_ref,
    odd_ref,
    even_load_ref,
    odd_load_ref,
):
    row = iota((8, 128), 0)
    fixed = (row < 4) | (row == 7)
    factor = jnp.where(row == 7, KAPPA, 1.0)

    def find_top(t):
        tops = [arrived_ref[target_ref[t, k], 3:4, :] for k in range(CAND)]
        while len(tops) > 1:
            tops = [jnp.maximum(a, b) for a, b in zip(tops[::2], tops[1::2])]
        top = jnp.max(tops[0], axis=1, keepdims=True)
        top_ref[pl.ds(t, 1), :] = jnp.broadcast_to(top, (1, 128))

    def scores(t, e_ref, unit_ref):
        lhs = lhs_ref[t]
        centre = jnp.where(row % 4 == 3, top_ref[pl.ds(t, 1), :], 0.0)

        def spread(k):
            block = arrived_ref[target_ref[t, k]]
            both = jnp.concatenate([block, block], axis=0) - centre
            terms = both * jnp.where(fixed, factor, both)
            t1 = jnp.concatenate([terms, terms], axis=0).astype(BF16)
            first = t1.astype(F32)[:8]
            rest = terms - first
            t2 = jnp.concatenate([rest, rest], axis=0).astype(BF16)
            t3 = rest - t2.astype(F32)[:8]
            return jnp.concatenate(
                [t1, t2, jnp.concatenate([t3, first], axis=0).astype(BF16)], axis=0
            )

        total = None
        for q in range(CAND // 2):
            rhs = jnp.concatenate([spread(2 * q), spread(2 * q + 1)], axis=1)
            e = jnp.exp2(jnp.dot(lhs, rhs, preferred_element_type=F32))
            part = e[:, :128] + e[:, 128:]
            total = part if total is None else total + part
            high = e.astype(BF16)
            e_ref[q, 0:128, :] = high
            e_ref[q, 128:256, :] = (e - high.astype(F32)).astype(BF16)
        sums = jnp.sum(jnp.transpose(total), axis=0, keepdims=True)
        sum_ref[pl.ds(t, 1), :] = sums
        coords = [point_ref[c, pl.ds(t, 1), :] for c in range(3)]
        point = jnp.where(
            row % 4 == 0,
            coords[0],
            jnp.where(row % 4 == 1, coords[1], jnp.where(row % 4 == 2, coords[2], 1.0)),
        )
        loads = (load_ref[pl.ds(t, 1), :] / sums) * point
        high = rounded(loads)
        unit_ref[...] = jnp.where(row < 4, high, loads - high)

    def moments(t, e_ref, unit_ref):
        half = unit_ref[...].astype(BF16)
        lhs = jnp.concatenate([half, half], axis=1)
        for q in range(CAND // 2):
            found = jnp.dot(lhs, e_ref[q], preferred_element_type=F32)
            found = found[0:4] + found[4:8]
            out_ref[target_ref[t, 2 * q]] = found[:, :128]
            out_ref[target_ref[t, 2 * q + 1]] = found[:, 128:]

    find_top(0)

    def two_tiles(i, carry):
        t = 2 * i
        find_top(t + 1)
        scores(t, even_ref, even_load_ref)
        moments(jnp.maximum(t - 1, 0), odd_ref, odd_load_ref)
        find_top(jnp.minimum(t + 2, TILES - 1))
        scores(t + 1, odd_ref, odd_load_ref)
        moments(t, even_ref, even_load_ref)
        return carry

    lax.fori_loop(0, TILES // 2, two_tiles, 0, unroll=8)
    moments(TILES - 1, odd_ref, odd_load_ref)
    square = (
        (point_ref[0] - 0.5) ** 2 + (point_ref[1] - 0.5) ** 2 + (point_ref[2] - 0.5) ** 2
    )
    potential_ref[...] = jnp.log(sum_ref[...]) + (top_ref[...] - square) / EPSILON


def reduce_kernel(
    ids_ref,
    back_ref,
    start_ref,
    mass_hbm,
    centre_hbm,
    acc_ref,
    other_ref,
    mass_ref,
    scale_ref,
    centre_ref,
    sems,
):
    other_ref[...] = jnp.zeros_like(other_ref)
    for piece in range(PIECES):
        for peer in range(BLOCKS // CAP):
            into = (acc_ref, other_ref)[peer % 2]
            places = []
            sums = []
            for r in range(CAP):
                c = peer * CAP + r
                place = pl.ds(pl.multiple_of(ids_ref[piece, c], 4), 4)
                places.append(place)
                sums.append(into[place, :] + back_ref[piece * BLOCKS + c])
            for place, total in zip(places, sums):
                into[place, :] = total
    copies = []
    width = BLOCKS * SITE_BLOCK
    for piece in range(PIECES):
        part = pl.ds(piece * BLOCKS, BLOCKS)
        lines = pl.ds(piece * BLOCKS * 4 + 3, BLOCKS, stride=4)
        mass = acc_ref[lines, :] + other_ref[lines, :]
        mass_ref[part, :] = mass
        copies.append(
            pltpu.make_async_copy(
                mass_ref.at[part], mass_hbm.at[part], sems.at[PIECES + piece]
            )
        )
        copies[-1].start()
        scale_ref[part, :] = 1.0 / (mass + PRIOR_MASS)
        for b in range(piece * BLOCKS, (piece + 1) * BLOCKS):
            centre_ref[:, b * SITE_BLOCK : (b + 1) * SITE_BLOCK] = (
                acc_ref[4 * b : 4 * b + 3, :] + other_ref[4 * b : 4 * b + 3, :]
            ) * scale_ref[b : b + 1, :]
        part = pl.ds(piece * width, width)
        copies.append(
            pltpu.make_async_copy(
                centre_ref.at[:, part], centre_hbm.at[:, part], sems.at[piece]
            )
        )
        copies[-1].start()
    for copy in copies:
        copy.wait()


def shape_of(*dims, dtype=F32):
    return jax.ShapeDtypeStruct(dims, dtype)


def in_hbm(values):
    return pltpu.with_memory_space_constraint(values, pltpu.HBM)


def exchange(values):
    return lax.all_to_all(values, AXES, split_axis=0, concat_axis=0, tiled=True)


def neighbours(values, axis):
    count = lax.axis_size(axis)
    before = lax.ppermute(values, axis, [(i, (i + 1) % count) for i in range(count)])
    after = lax.ppermute(values, axis, [((i + 1) % count, i) for i in range(count)])
    return before, after


def local(
    density, point_position, block_owner, block_slot, block_count, site_position, site_weight
):
    cells = density.reshape(TILES, TILE)
    points = point_position.reshape(3, TILES, TILE)
    request, target = pl.pallas_call(
        request_kernel,
        out_shape=(
            shape_of(2 * OWNERS, 128),
            shape_of(TILES, 128, dtype=I32),
        ),
        in_specs=[HBM] * 4,
        out_specs=(VMEM, VMEM),
        scratch_shapes=[
            pltpu.VMEM((TILES, CAND), I32),
            pltpu.VMEM((TILES, CAND), I32),
            pltpu.VMEM((PZ, 1, CY), I32),
            pltpu.VMEM((TILES, TILE), F32),
            pltpu.SemaphoreType.DMA((4,)),
        ],
        compiler_params=LIMIT,
        name="request",
    )(
        in_hbm(block_owner.reshape(TILES, CAND)),
        in_hbm(block_slot.reshape(TILES, CAND)),
        in_hbm(jnp.transpose(block_count, (0, 2, 1))),
        in_hbm(cells),
    )
    asked = exchange(request)
    table = pl.pallas_call(
        table_kernel,
        out_shape=shape_of((SB_DEV + CAP) * 4, SITE_BLOCK),
        in_specs=[HBM] * 2,
        out_specs=VMEM,
        scratch_shapes=[
            pltpu.VMEM((3, SB_DEV * SITE_BLOCK), F32),
            pltpu.VMEM((SB_DEV, SITE_BLOCK), F32),
            pltpu.SemaphoreType.DMA((PIECES + 1,)),
        ],
        compiler_params=LIMIT,
        name="table",
    )(in_hbm(site_position), in_hbm(site_weight.reshape(SB_DEV, SITE_BLOCK)))
    blocks, ids = pl.pallas_call(
        gather_kernel,
        out_shape=(shape_of(SLOTS, 4, SITE_BLOCK), shape_of(8, 128, dtype=I32)),
        in_specs=[VMEM] * 2,
        out_specs=(HBM, VMEM),
        compiler_params=LIMIT,
        scratch_shapes=[
            pltpu.VMEM((SLOTS, 4, SITE_BLOCK), F32),
            pltpu.SMEM((8, 128), I32),
            pltpu.SemaphoreType.DMA,
            pltpu.SemaphoreType.DMA((PIECES,)),
        ],
        name="gather",
    )(asked, table)
    cells, points, site_position, blocks = lax.optimization_barrier(
        (cells, points, site_position, blocks)
    )
    arrived = exchange(blocks)
    above, below = neighbours(cells, "gy")
    start, lhs = pl.pallas_call(
        setup_kernel,
        out_shape=(
            shape_of((SB_DEV + CAP) * 4, SITE_BLOCK),
            shape_of(TILES, TILE, 48, dtype=BF16),
        ),
        in_specs=[HBM, VMEM],
        out_specs=(VMEM, VMEM),
        scratch_shapes=[
            pltpu.VMEM((3, SB_DEV * SITE_BLOCK), F32),
            pltpu.SemaphoreType.DMA((PIECES,)),
        ],
        compiler_params=LIMIT,
        name="setup",
    )(in_hbm(site_position), points)
    load = pl.pallas_call(
        smooth_kernel,
        out_shape=shape_of(TILES, TILE),
        in_specs=[VMEM] * 4,
        out_specs=VMEM,
        scratch_shapes=[pltpu.VMEM((PZ, 3 * CY, 128), F32)],
        compiler_params=LIMIT,
        name="smooth",
    )(asked, above, cells, below)
    potential, moments = pl.pallas_call(
        transport_kernel,
        out_shape=(shape_of(TILES, TILE), shape_of(SLOTS, 4, SITE_BLOCK)),
        in_specs=[SMEM] + [VMEM] * 4,
        out_specs=(VMEM, VMEM),
        scratch_shapes=[
            pltpu.VMEM((TILES, 128), F32),
            pltpu.VMEM((TILES, 128), F32),
            pltpu.VMEM((CAND // 2, 256, 256), BF16),
            pltpu.VMEM((CAND // 2, 256, 256), BF16),
            pltpu.VMEM((8, 128), F32),
            pltpu.VMEM((8, 128), F32),
        ],
        compiler_params=LIMIT,
        name="transport",
    )(target, arrived, lhs, points, load)
    returned = exchange(moments)
    site_mass, barycentre, _ = pl.pallas_call(
        reduce_kernel,
        out_shape=(
            shape_of(SB_DEV, SITE_BLOCK),
            shape_of(3, SB_DEV * SITE_BLOCK),
            shape_of((SB_DEV + CAP) * 4, SITE_BLOCK),
        ),
        in_specs=[SMEM] + [VMEM] * 2,
        out_specs=(HBM, HBM, VMEM),
        scratch_shapes=[
            pltpu.VMEM(((SB_DEV + CAP) * 4, SITE_BLOCK), F32),
            pltpu.VMEM((SB_DEV, SITE_BLOCK), F32),
            pltpu.VMEM((SB_DEV, SITE_BLOCK), F32),
            pltpu.VMEM((3, SB_DEV * SITE_BLOCK), F32),
            pltpu.SemaphoreType.DMA((2 * PIECES,)),
        ],
        input_output_aliases={2: 2},
        compiler_params=LIMIT,
        name="reduce",
    )(ids, returned, start)
    return (
        potential.reshape(PZ, CY, TILE),
        site_mass.reshape(SB_DEV * SITE_BLOCK),
        barycentre,
    )


def solution(mesh):
    in_specs = (
        P(None, "gy", "gx"),
        P(None, None, "gy", "gx"),
        P(None, "gy", "gx"),
        P(None, "gy", "gx"),
        P(None, "gy", "gx"),
        P(None, ("gx", "gy")),
        P(("gx", "gy")),
    )
    out_specs = (P(None, "gy", "gx"), P(("gx", "gy")), P(None, ("gx", "gy")))
    return jax.shard_map(local, mesh=mesh, in_specs=in_specs, out_specs=out_specs, check_vma=False)
```

```python
import math

import jax
import jax.numpy as jnp
import numpy as np
from jax import lax
from jax.experimental import pallas as pl
from jax.experimental.pallas import tpu as pltpu
from jax.sharding import PartitionSpec as P

PZ = 2
CY = 8
TILE = 128
CAND = 16
SITE_BLOCK = 128
SB_DEV = 512
HALF = 8
CAP = 4
OWNERS = 128
TILES = PZ * CY
SLOTS = OWNERS * CAP
ENTRIES = TILES * CAND

EPSILON = 0.05
PRIOR_MASS = 0.5
SIGMA_CELLS = 4.0
KAPPA = math.log2(math.e) / EPSILON
ROOT = math.sqrt(KAPPA)
DEAD = -1e30
PIECES = 4
BLOCKS = SB_DEV // PIECES
PART = BLOCKS // 2
F32 = jnp.float32
BF16 = jnp.bfloat16
I32 = jnp.int32
VMEM = pl.BlockSpec(memory_space=pltpu.VMEM)
HBM = pl.BlockSpec(memory_space=pltpu.HBM)
SMEM = pl.BlockSpec(memory_space=pltpu.SMEM)
AXES = ("gx", "gy")
LIMIT = pltpu.CompilerParams(vmem_limit_bytes=8 << 20)


def gauss_values():
    offsets = np.arange(-HALF, HALF + 1, dtype=np.float64)
    values = np.exp(-offsets * offsets / (2.0 * SIGMA_CELLS * SIGMA_CELLS))
    return values / values.sum()


GAUSS = [float(v) for v in gauss_values()]
GAUSS_PEAK = GAUSS[HALF]


def iota(shape, dim):
    return lax.broadcasted_iota(I32, shape, dim)


def rounded(values):
    return values.astype(BF16).astype(F32)


def request_kernel(
    owner_hbm,
    slot_hbm,
    count_hbm,
    cells_hbm,
    request_ref,
    target_ref,
    owner_ref,
    slot_ref,
    count_ref,
    cells_ref,
    sems,
):
    copies = [
        pltpu.make_async_copy(owner_hbm, owner_ref, sems.at[0]),
        pltpu.make_async_copy(slot_hbm, slot_ref, sems.at[1]),
        pltpu.make_async_copy(count_hbm, count_ref, sems.at[2]),
        pltpu.make_async_copy(cells_hbm, cells_ref, sems.at[3]),
    ]
    for copy in copies:
        copy.start()
    corner = iota((CY, CY), 0) == iota((CY, CY), 1)
    square = (ENTRIES, ENTRIES)
    upper = (iota(square, 0) < iota(square, 1)).astype(F32).astype(BF16)
    pick = (iota((CAND, ENTRIES), 0) == iota((CAND, ENTRIES), 1) % CAND).astype(F32).astype(BF16)
    own_tile = iota((TILES, ENTRIES), 0) == iota((TILES, ENTRIES), 1) // CAND
    fold = (iota((ENTRIES, 128), 0) % CAND == iota((ENTRIES, 128), 1)).astype(F32)
    fold = jnp.concatenate([fold * CAP, fold], axis=0).astype(BF16)
    repeat = (iota((2 * CAP, 128), 0) % CAP == iota((2 * CAP, 128), 1) % CAP).astype(F32)
    for copy in copies:
        copy.wait()
    counts = jnp.concatenate(
        [
            jnp.sum(jnp.where(corner, count_ref[z], 0), axis=1, keepdims=True)
            for z in range(PZ)
        ],
        axis=0,
    )
    value = jnp.where(iota((TILES, CAND), 1) < counts, slot_ref[...] + 1, 0)
    parts = jnp.concatenate([owner_ref[...], value & -32, value & 31], axis=0)
    parts = jnp.dot(parts.astype(F32).astype(BF16), pick, preferred_element_type=F32)
    owner, high_part, low_part = [
        jnp.sum(
            jnp.where(own_tile, parts[g * TILES : (g + 1) * TILES], 0.0), axis=0, keepdims=True
        )
        for g in range(3)
    ]
    hot = (iota((OWNERS, ENTRIES), 0).astype(F32) == owner).astype(F32)
    hot_low = hot.astype(BF16)
    before = jnp.dot(hot_low, upper, preferred_element_type=F32)
    rank = jnp.sum(before * hot, axis=0, keepdims=True)
    shape = (2 * CAP, ENTRIES)
    own_rank = (iota(shape, 0) % CAP).astype(F32) == rank
    spread = jnp.where(own_rank, jnp.where(iota(shape, 0) < CAP, high_part, low_part), 0.0)
    request = lax.dot_general(
        hot_low, spread.astype(BF16), (((1,), (1,)), ((), ())), preferred_element_type=F32
    )
    request = jnp.dot(request.astype(BF16), repeat.astype(BF16), preferred_element_type=F32)
    request_ref[pl.ds(0, OWNERS, stride=2), :] = request - 1.0
    place = jnp.concatenate(
        [jnp.where(own_tile, owner, 0.0), jnp.where(own_tile, rank, 0.0)], axis=1
    )
    place = jnp.dot(place.astype(BF16), fold, preferred_element_type=F32)
    target_ref[...] = place.astype(I32)
    edge_shape = (TILE, 2 * TILE)
    edge_lane = iota(edge_shape, 1)
    column = jnp.where(edge_lane < TILE, 0, TILE - HALF) + edge_lane % HALF
    pick = (iota(edge_shape, 0) == column).astype(F32)
    edges = jnp.dot(
        cells_ref[...], pick, preferred_element_type=F32, precision=lax.Precision.HIGHEST
    )
    edge_shape = (TILES, 2 * TILE)
    own_row = (iota(edge_shape, 1) % TILE) // HALF == iota(edge_shape, 0)
    edges = jnp.sum(jnp.where(own_row, edges, 0.0), axis=0, keepdims=True)
    columns = lax.axis_size("gx")
    after = lax.rem(lax.axis_index("gx") + 1, columns)
    to_after = iota((OWNERS, 128), 0) // (OWNERS // columns) == after
    request_ref[pl.ds(1, OWNERS, stride=2), :] = jnp.where(
        to_after, edges[:, TILE:], edges[:, :TILE]
    )


def prepare(point_ref, lhs_ref):
    row = iota((8, 128), 0)

    def tile(t, carry):
        coords = [point_ref[c, pl.ds(t, 1), :] for c in range(3)]
        point = jnp.where(row == 0, coords[0], jnp.where(row == 1, coords[1], coords[2]))
        scaled = jnp.where(row < 3, (2.0 * ROOT) * (point - 0.5), 0.0)
        a1 = rounded(scaled)
        rest = scaled - a1
        a2 = rounded(rest)
        a3 = rest - a2
        lead = jnp.where(row == 7, 1.0, jnp.where(row >= 4, -1.0, a1))
        lhs = jnp.concatenate([lead, a2, lead, a2, lead, a3], axis=0)
        lhs_ref[t] = jnp.transpose(lhs).astype(BF16)
        return carry

    lax.fori_loop(0, TILES, tile, 0, unroll=4)


def piece_copies(source, target, sems):
    width = SB_DEV * SITE_BLOCK // PIECES
    copies = []
    for piece in range(PIECES):
        part = pl.ds(piece * width, width)
        copies.append(
            pltpu.make_async_copy(source.at[:, part], target.at[:, part], sems.at[piece])
        )
    return copies


def table_kernel(position_hbm, weight_hbm, table_ref, position_ref, weight_ref, sems):
    weights = pltpu.make_async_copy(weight_hbm, weight_ref, sems.at[PIECES])
    copies = piece_copies(position_hbm, position_ref, sems)
    weights.start()
    for copy in copies:
        copy.start()
    dead = jnp.where(iota((4, 128), 0) == 3, DEAD, 0.0)
    for r in range(CAP):
        table_ref[(SB_DEV + r) * 4 : (SB_DEV + r + 1) * 4, :] = dead
    weights.wait()
    for piece in range(PIECES):
        copies[piece].wait()
        for b in range(piece * BLOCKS, (piece + 1) * BLOCKS):
            place = position_ref[:, b * SITE_BLOCK : (b + 1) * SITE_BLOCK]
            table_ref[4 * b : 4 * b + 3, :] = (place - 0.5) * ROOT
            table_ref[4 * b + 3 : 4 * b + 4, :] = weight_ref[b : b + 1, :]


def filter_taps(taps_ref):
    shape = (3 * TILE, TILE)
    row = iota(shape, 0)
    source = jnp.where(
        row < TILE, row, row % HALF + jnp.where(row < 2 * TILE, -HALF, TILE)
    )
    shift = (source - iota(shape, 1)).astype(F32)
    taps = jnp.where(
        jnp.abs(shift) <= HALF,
        GAUSS_PEAK * jnp.exp(shift * shift * (-0.5 / (SIGMA_CELLS * SIGMA_CELLS))),
        0.0,
    )
    high = rounded(taps)
    rest = taps - high
    middle = rounded(rest)
    for part, values in enumerate((high, middle, rest - middle)):
        taps_ref[part] = values.astype(BF16)


def setup_kernel(position_hbm, point_ref, start_ref, lhs_ref, taps_ref, position_ref, sems):
    copies = piece_copies(position_hbm, position_ref, sems)
    for copy in copies:
        copy.start()
    prepare(point_ref, lhs_ref)
    filter_taps(taps_ref)
    for r in range(CAP):
        start_ref[(SB_DEV + r) * 4 : (SB_DEV + r + 1) * 4, :] = jnp.zeros((4, 128), F32)

    def block(b, carry):
        start = pl.multiple_of(b * SITE_BLOCK, SITE_BLOCK)
        line = pl.multiple_of(b * 4, 4)
        start_ref[pl.ds(line, 3), :] = PRIOR_MASS * position_ref[:, pl.ds(start, SITE_BLOCK)]
        start_ref[pl.ds(line + 3, 1), :] = jnp.zeros((1, 128), F32)
        return carry

    for piece in range(PIECES):
        copies[piece].wait()
        lax.fori_loop(piece * BLOCKS, (piece + 1) * BLOCKS, block, 0, unroll=8)


def smooth_kernel(halo_ref, taps_ref, above_ref, mid_ref, below_ref, load_ref, rows_ref):
    tiles = (above_ref[...], mid_ref[...], below_ref[...])
    count_x, count_y = lax.axis_size("gx"), lax.axis_size("gy")
    here_x, here_y = lax.axis_index("gx"), lax.axis_index("gy")
    shape = (TILES, TILE)
    own_row = iota(shape, 1) // HALF == iota(shape, 0)
    rows = []
    for step, tile in zip((count_y - 1, 0, 1), tiles):
        parts = [tile]
        for side in (count_x - 1, 1):
            peer = lax.rem(here_x + side, count_x) * count_y + lax.rem(here_y + step, count_y)
            halo = halo_ref[pl.ds(2 * peer + 1, 1), :]
            parts.append(jnp.where(own_row, halo, 0.0))
        rows.append(jnp.concatenate(parts, axis=1))
    cells = jnp.concatenate(rows, axis=0)
    high = rounded(cells)
    rest = cells - high
    middle = rounded(rest)
    cells = jnp.concatenate([high, middle, rest - middle], axis=0).astype(BF16)
    count = 3 * TILES
    first = jnp.dot(cells[:count], taps_ref[2], preferred_element_type=F32)
    second = jnp.dot(cells[: 2 * count], taps_ref[1], preferred_element_type=F32)
    third = jnp.dot(cells, taps_ref[0], preferred_element_type=F32)
    first = first + second[count:] + third[2 * count :]
    first = first + second[:count] + third[count : 2 * count] + third[:count]
    planes = []
    for z in range(PZ):
        for part in range(3):
            at = part * TILES + z * CY
            rows_ref[z, part * CY : (part + 1) * CY, :] = first[at : at + CY]
        total = GAUSS[0] * rows_ref[z, 0:CY, :]
        for j in range(1, 2 * HALF + 1):
            total = total + GAUSS[j] * rows_ref[z, j : j + CY, :]
        planes.append(total)
    load_ref[0:CY, :] = GAUSS[HALF] * planes[0] + GAUSS[HALF + 1] * planes[1]
    load_ref[CY : 2 * CY, :] = GAUSS[HALF - 1] * planes[0] + GAUSS[HALF] * planes[1]


def gather_kernel(asked_ref, table_ref, out_hbm, ids_ref, out_ref, ids_smem, sem, out_sems):
    shape = (OWNERS, 128)
    asked = asked_ref[pl.ds(0, OWNERS, stride=2), :]
    lane = iota(shape, 1)
    place = jnp.where(asked < 0.0, (SB_DEV + lane % CAP).astype(F32), asked) * 4.0
    own = iota(shape, 0) % (128 // CAP) == lane // CAP
    place = jnp.where(own, place, 0.0)
    rows = [
        jnp.sum(place[g * 32 : (g + 1) * 32], axis=0, keepdims=True) for g in range(PIECES)
    ]
    ids_ref[...] = jnp.concatenate(rows + rows, axis=0).astype(I32)
    copy = pltpu.make_async_copy(ids_ref, ids_smem, sem)
    copy.start()
    copy.wait()
    copies = []
    for piece in range(PIECES):
        for c in range(BLOCKS):
            line = pl.multiple_of(ids_smem[piece, c], 4)
            out_ref[piece * BLOCKS + c] = table_ref[pl.ds(line, 4), :]
            if (c + 1) % PART == 0:
                part = pl.ds(piece * BLOCKS + c + 1 - PART, PART)
                copies.append(
                    pltpu.make_async_copy(
                        out_ref.at[part], out_hbm.at[part], out_sems.at[len(copies)]
                    )
                )
                copies[-1].start()
    for copy in copies:
        copy.wait()


def transport_kernel(
    target_ref,
    arrived_ref,
    lhs_ref,
    point_ref,
    load_ref,
    potential_ref,
    out_ref,
    top_ref,
    sum_ref,
    even_ref,
    odd_ref,
    even_load_ref,
    odd_load_ref,
):
    row = iota((8, 128), 0)
    fixed = (row < 4) | (row == 7)
    factor = jnp.where(row == 7, KAPPA, 1.0)

    def find_top(t):
        tops = [arrived_ref[target_ref[t, k], 3:4, :] for k in range(CAND)]
        while len(tops) > 1:
            tops = [jnp.maximum(a, b) for a, b in zip(tops[::2], tops[1::2])]
        top = jnp.max(tops[0], axis=1, keepdims=True)
        top_ref[pl.ds(t, 1), :] = jnp.broadcast_to(top, (1, 128))

    def scores(t, e_ref, unit_ref):
        lhs = lhs_ref[t]
        centre = jnp.where(row % 4 == 3, top_ref[pl.ds(t, 1), :], 0.0)

        def spread(k):
            block = arrived_ref[target_ref[t, k]]
            both = jnp.concatenate([block, block], axis=0) - centre
            terms = both * jnp.where(fixed, factor, both)
            t1 = jnp.concatenate([terms, terms], axis=0).astype(BF16)
            first = t1.astype(F32)[:8]
            rest = terms - first
            t2 = jnp.concatenate([rest, rest], axis=0).astype(BF16)
            t3 = rest - t2.astype(F32)[:8]
            return jnp.concatenate(
                [t1, t2, jnp.concatenate([t3, first], axis=0).astype(BF16)], axis=0
            )

        total = None
        for q in range(CAND // 2):
            rhs = jnp.concatenate([spread(2 * q), spread(2 * q + 1)], axis=1)
            e = jnp.exp2(jnp.dot(lhs, rhs, preferred_element_type=F32))
            part = e[:, :128] + e[:, 128:]
            total = part if total is None else total + part
            high = e.astype(BF16)
            e_ref[q, 0:128, :] = high
            e_ref[q, 128:256, :] = (e - high.astype(F32)).astype(BF16)
        sums = jnp.sum(jnp.transpose(total), axis=0, keepdims=True)
        sum_ref[pl.ds(t, 1), :] = sums
        coords = [point_ref[c, pl.ds(t, 1), :] for c in range(3)]
        point = jnp.where(
            row % 4 == 0,
            coords[0],
            jnp.where(row % 4 == 1, coords[1], jnp.where(row % 4 == 2, coords[2], 1.0)),
        )
        loads = (load_ref[pl.ds(t, 1), :] / sums) * point
        high = rounded(loads)
        unit_ref[...] = jnp.where(row < 4, high, loads - high)

    def moments(t, e_ref, unit_ref):
        half = unit_ref[...].astype(BF16)
        lhs = jnp.concatenate([half, half], axis=1)
        for q in range(CAND // 2):
            found = jnp.dot(lhs, e_ref[q], preferred_element_type=F32)
            found = found[0:4] + found[4:8]
            out_ref[target_ref[t, 2 * q]] = found[:, :128]
            out_ref[target_ref[t, 2 * q + 1]] = found[:, 128:]

    find_top(0)

    def two_tiles(i, carry):
        t = 2 * i
        find_top(t + 1)
        scores(t, even_ref, even_load_ref)
        moments(jnp.maximum(t - 1, 0), odd_ref, odd_load_ref)
        find_top(jnp.minimum(t + 2, TILES - 1))
        scores(t + 1, odd_ref, odd_load_ref)
        moments(t, even_ref, even_load_ref)
        return carry

    lax.fori_loop(0, TILES // 2, two_tiles, 0, unroll=8)
    moments(TILES - 1, odd_ref, odd_load_ref)
    square = (
        (point_ref[0] - 0.5) ** 2 + (point_ref[1] - 0.5) ** 2 + (point_ref[2] - 0.5) ** 2
    )
    potential_ref[...] = jnp.log(sum_ref[...]) + (top_ref[...] - square) / EPSILON


def reduce_kernel(
    ids_ref,
    back_ref,
    start_ref,
    mass_hbm,
    centre_hbm,
    acc_ref,
    other_ref,
    mass_ref,
    scale_ref,
    centre_ref,
    sems,
):
    other_ref[...] = jnp.zeros_like(other_ref)
    for piece in range(PIECES):
        for peer in range(BLOCKS // CAP):
            into = (acc_ref, other_ref)[peer % 2]
            places = []
            sums = []
            for r in range(CAP):
                c = peer * CAP + r
                place = pl.ds(pl.multiple_of(ids_ref[piece, c], 4), 4)
                places.append(place)
                sums.append(into[place, :] + back_ref[piece * BLOCKS + c])
            for place, total in zip(places, sums):
                into[place, :] = total
    copies = []
    width = PART * SITE_BLOCK
    for piece in range(SB_DEV // PART):
        part = pl.ds(piece * PART, PART)
        lines = pl.ds(piece * PART * 4 + 3, PART, stride=4)
        mass = acc_ref[lines, :] + other_ref[lines, :]
        mass_ref[part, :] = mass
        copies.append(
            pltpu.make_async_copy(
                mass_ref.at[part], mass_hbm.at[part], sems.at[SB_DEV // PART + piece]
            )
        )
        copies[-1].start()
        scale_ref[part, :] = 1.0 / (mass + PRIOR_MASS)
        for b in range(piece * PART, (piece + 1) * PART):
            centre_ref[:, b * SITE_BLOCK : (b + 1) * SITE_BLOCK] = (
                acc_ref[4 * b : 4 * b + 3, :] + other_ref[4 * b : 4 * b + 3, :]
            ) * scale_ref[b : b + 1, :]
        part = pl.ds(piece * width, width)
        copies.append(
            pltpu.make_async_copy(
                centre_ref.at[:, part], centre_hbm.at[:, part], sems.at[piece]
            )
        )
        copies[-1].start()
    for copy in copies:
        copy.wait()


def shape_of(*dims, dtype=F32):
    return jax.ShapeDtypeStruct(dims, dtype)


def in_hbm(values):
    return pltpu.with_memory_space_constraint(values, pltpu.HBM)


def exchange(values):
    return lax.all_to_all(values, AXES, split_axis=0, concat_axis=0, tiled=True)


def neighbours(values, axis):
    count = lax.axis_size(axis)
    before = lax.ppermute(values, axis, [(i, (i + 1) % count) for i in range(count)])
    after = lax.ppermute(values, axis, [((i + 1) % count, i) for i in range(count)])
    return before, after


def local(
    density, point_position, block_owner, block_slot, block_count, site_position, site_weight
):
    cells = density.reshape(TILES, TILE)
    points = point_position.reshape(3, TILES, TILE)
    request, target = pl.pallas_call(
        request_kernel,
        out_shape=(
            shape_of(2 * OWNERS, 128),
            shape_of(TILES, 128, dtype=I32),
        ),
        in_specs=[HBM] * 4,
        out_specs=(VMEM, VMEM),
        scratch_shapes=[
            pltpu.VMEM((TILES, CAND), I32),
            pltpu.VMEM((TILES, CAND), I32),
            pltpu.VMEM((PZ, 1, CY), I32),
            pltpu.VMEM((TILES, TILE), F32),
            pltpu.SemaphoreType.DMA((4,)),
        ],
        compiler_params=LIMIT,
        name="request",
    )(
        in_hbm(block_owner.reshape(TILES, CAND)),
        in_hbm(block_slot.reshape(TILES, CAND)),
        in_hbm(jnp.transpose(block_count, (0, 2, 1))),
        in_hbm(cells),
    )
    asked = exchange(request)
    table = pl.pallas_call(
        table_kernel,
        out_shape=shape_of((SB_DEV + CAP) * 4, SITE_BLOCK),
        in_specs=[HBM] * 2,
        out_specs=VMEM,
        scratch_shapes=[
            pltpu.VMEM((3, SB_DEV * SITE_BLOCK), F32),
            pltpu.VMEM((SB_DEV, SITE_BLOCK), F32),
            pltpu.SemaphoreType.DMA((PIECES + 1,)),
        ],
        compiler_params=LIMIT,
        name="table",
    )(in_hbm(site_position), in_hbm(site_weight.reshape(SB_DEV, SITE_BLOCK)))
    blocks, ids = pl.pallas_call(
        gather_kernel,
        out_shape=(shape_of(SLOTS, 4, SITE_BLOCK), shape_of(8, 128, dtype=I32)),
        in_specs=[VMEM] * 2,
        out_specs=(HBM, VMEM),
        compiler_params=LIMIT,
        scratch_shapes=[
            pltpu.VMEM((SLOTS, 4, SITE_BLOCK), F32),
            pltpu.SMEM((8, 128), I32),
            pltpu.SemaphoreType.DMA,
            pltpu.SemaphoreType.DMA((SB_DEV // PART,)),
        ],
        name="gather",
    )(asked, table)
    cells, points, site_position, blocks = lax.optimization_barrier(
        (cells, points, site_position, blocks)
    )
    arrived = exchange(blocks)
    above, below = neighbours(cells, "gy")
    start, lhs, taps = pl.pallas_call(
        setup_kernel,
        out_shape=(
            shape_of((SB_DEV + CAP) * 4, SITE_BLOCK),
            shape_of(TILES, TILE, 48, dtype=BF16),
            shape_of(3, 3 * TILE, TILE, dtype=BF16),
        ),
        in_specs=[HBM, VMEM],
        out_specs=(VMEM,) * 3,
        scratch_shapes=[
            pltpu.VMEM((3, SB_DEV * SITE_BLOCK), F32),
            pltpu.SemaphoreType.DMA((PIECES,)),
        ],
        compiler_params=LIMIT,
        name="setup",
    )(in_hbm(site_position), points)
    load = pl.pallas_call(
        smooth_kernel,
        out_shape=shape_of(TILES, TILE),
        in_specs=[VMEM] * 5,
        out_specs=VMEM,
        scratch_shapes=[pltpu.VMEM((PZ, 3 * CY, 128), F32)],
        compiler_params=LIMIT,
        name="smooth",
    )(asked, taps, above, cells, below)
    potential, moments = pl.pallas_call(
        transport_kernel,
        out_shape=(shape_of(TILES, TILE), shape_of(SLOTS, 4, SITE_BLOCK)),
        in_specs=[SMEM] + [VMEM] * 4,
        out_specs=(VMEM, VMEM),
        scratch_shapes=[
            pltpu.VMEM((TILES, 128), F32),
            pltpu.VMEM((TILES, 128), F32),
            pltpu.VMEM((CAND // 2, 256, 256), BF16),
            pltpu.VMEM((CAND // 2, 256, 256), BF16),
            pltpu.VMEM((8, 128), F32),
            pltpu.VMEM((8, 128), F32),
        ],
        compiler_params=LIMIT,
        name="transport",
    )(target, arrived, lhs, points, load)
    returned = exchange(moments)
    site_mass, barycentre, _ = pl.pallas_call(
        reduce_kernel,
        out_shape=(
            shape_of(SB_DEV, SITE_BLOCK),
            shape_of(3, SB_DEV * SITE_BLOCK),
            shape_of((SB_DEV + CAP) * 4, SITE_BLOCK),
        ),
        in_specs=[SMEM] + [VMEM] * 2,
        out_specs=(HBM, HBM, VMEM),
        scratch_shapes=[
            pltpu.VMEM(((SB_DEV + CAP) * 4, SITE_BLOCK), F32),
            pltpu.VMEM((SB_DEV, SITE_BLOCK), F32),
            pltpu.VMEM((SB_DEV, SITE_BLOCK), F32),
            pltpu.VMEM((3, SB_DEV * SITE_BLOCK), F32),
            pltpu.SemaphoreType.DMA((2 * SB_DEV // PART,)),
        ],
        input_output_aliases={2: 2},
        compiler_params=LIMIT,
        name="reduce",
    )(ids, returned, start)
    return (
        potential.reshape(PZ, CY, TILE),
        site_mass.reshape(SB_DEV * SITE_BLOCK),
        barycentre,
    )


def solution(mesh):
    in_specs = (
        P(None, "gy", "gx"),
        P(None, None, "gy", "gx"),
        P(None, "gy", "gx"),
        P(None, "gy", "gx"),
        P(None, "gy", "gx"),
        P(None, ("gx", "gy")),
        P(("gx", "gy")),
    )
    out_specs = (P(None, "gy", "gx"), P(("gx", "gy")), P(None, ("gx", "gy")))
    return jax.shard_map(local, mesh=mesh, in_specs=in_specs, out_specs=out_specs, check_vma=False)
```

```python
import math

import jax
import jax.numpy as jnp
import numpy as np
from jax import lax
from jax.experimental import pallas as pl
from jax.experimental.pallas import tpu as pltpu
from jax.sharding import PartitionSpec as P

PZ = 2
CY = 8
TILE = 128
CAND = 16
SITE_BLOCK = 128
SB_DEV = 512
HALF = 8
CAP = 4
OWNERS = 128
TILES = PZ * CY
SLOTS = OWNERS * CAP
ENTRIES = TILES * CAND

EPSILON = 0.05
PRIOR_MASS = 0.5
SIGMA_CELLS = 4.0
KAPPA = math.log2(math.e) / EPSILON
ROOT = math.sqrt(KAPPA)
DEAD = -1e30
PIECES = 4
BLOCKS = SB_DEV // PIECES
PART = BLOCKS // 2
F32 = jnp.float32
BF16 = jnp.bfloat16
I32 = jnp.int32
VMEM = pl.BlockSpec(memory_space=pltpu.VMEM)
HBM = pl.BlockSpec(memory_space=pltpu.HBM)
SMEM = pl.BlockSpec(memory_space=pltpu.SMEM)
AXES = ("gx", "gy")
LIMIT = pltpu.CompilerParams(vmem_limit_bytes=8 << 20)


def gauss_values():
    offsets = np.arange(-HALF, HALF + 1, dtype=np.float64)
    values = np.exp(-offsets * offsets / (2.0 * SIGMA_CELLS * SIGMA_CELLS))
    return values / values.sum()


GAUSS = [float(v) for v in gauss_values()]
GAUSS_PEAK = GAUSS[HALF]


def iota(shape, dim):
    return lax.broadcasted_iota(I32, shape, dim)


def rounded(values):
    return values.astype(BF16).astype(F32)


def request_kernel(
    owner_hbm,
    slot_hbm,
    count_hbm,
    cells_hbm,
    request_ref,
    target_ref,
    owner_ref,
    slot_ref,
    count_ref,
    cells_ref,
    sems,
):
    copies = [
        pltpu.make_async_copy(owner_hbm, owner_ref, sems.at[0]),
        pltpu.make_async_copy(slot_hbm, slot_ref, sems.at[1]),
        pltpu.make_async_copy(count_hbm, count_ref, sems.at[2]),
        pltpu.make_async_copy(cells_hbm, cells_ref, sems.at[3]),
    ]
    for copy in copies:
        copy.start()
    corner = iota((CY, CY), 0) == iota((CY, CY), 1)
    square = (ENTRIES, ENTRIES)
    upper = (iota(square, 0) < iota(square, 1)).astype(F32).astype(BF16)
    pick = (iota((CAND, ENTRIES), 0) == iota((CAND, ENTRIES), 1) % CAND).astype(F32).astype(BF16)
    own_tile = iota((TILES, ENTRIES), 0) == iota((TILES, ENTRIES), 1) // CAND
    fold = (iota((ENTRIES, 128), 0) % CAND == iota((ENTRIES, 128), 1)).astype(F32)
    fold = jnp.concatenate([fold * CAP, fold], axis=0).astype(BF16)
    repeat = (iota((2 * CAP, 128), 0) % CAP == iota((2 * CAP, 128), 1) % CAP).astype(F32)
    for copy in copies:
        copy.wait()
    counts = jnp.concatenate(
        [
            jnp.sum(jnp.where(corner, count_ref[z], 0), axis=1, keepdims=True)
            for z in range(PZ)
        ],
        axis=0,
    )
    value = jnp.where(iota((TILES, CAND), 1) < counts, slot_ref[...] + 1, 0)
    parts = jnp.concatenate([owner_ref[...], value & -32, value & 31], axis=0)
    parts = jnp.dot(parts.astype(F32).astype(BF16), pick, preferred_element_type=F32)
    owner, high_part, low_part = [
        jnp.sum(
            jnp.where(own_tile, parts[g * TILES : (g + 1) * TILES], 0.0), axis=0, keepdims=True
        )
        for g in range(3)
    ]
    hot = (iota((OWNERS, ENTRIES), 0).astype(F32) == owner).astype(F32)
    hot_low = hot.astype(BF16)
    before = jnp.dot(hot_low, upper, preferred_element_type=F32)
    rank = jnp.sum(before * hot, axis=0, keepdims=True)
    shape = (2 * CAP, ENTRIES)
    own_rank = (iota(shape, 0) % CAP).astype(F32) == rank
    spread = jnp.where(own_rank, jnp.where(iota(shape, 0) < CAP, high_part, low_part), 0.0)
    request = lax.dot_general(
        hot_low, spread.astype(BF16), (((1,), (1,)), ((), ())), preferred_element_type=F32
    )
    request = jnp.dot(request.astype(BF16), repeat.astype(BF16), preferred_element_type=F32)
    request_ref[pl.ds(0, OWNERS, stride=2), :] = request - 1.0
    place = jnp.concatenate(
        [jnp.where(own_tile, owner, 0.0), jnp.where(own_tile, rank, 0.0)], axis=1
    )
    place = jnp.dot(place.astype(BF16), fold, preferred_element_type=F32)
    target_ref[...] = place.astype(I32)
    edge_shape = (TILE, 2 * TILE)
    edge_lane = iota(edge_shape, 1)
    column = jnp.where(edge_lane < TILE, 0, TILE - HALF) + edge_lane % HALF
    pick = (iota(edge_shape, 0) == column).astype(F32)
    edges = jnp.dot(
        cells_ref[...], pick, preferred_element_type=F32, precision=lax.Precision.HIGHEST
    )
    edge_shape = (TILES, 2 * TILE)
    own_row = (iota(edge_shape, 1) % TILE) // HALF == iota(edge_shape, 0)
    edges = jnp.sum(jnp.where(own_row, edges, 0.0), axis=0, keepdims=True)
    columns = lax.axis_size("gx")
    after = lax.rem(lax.axis_index("gx") + 1, columns)
    to_after = iota((OWNERS, 128), 0) // (OWNERS // columns) == after
    request_ref[pl.ds(1, OWNERS, stride=2), :] = jnp.where(
        to_after, edges[:, TILE:], edges[:, :TILE]
    )


def prepare(point_ref, lhs_ref):
    row = iota((8, 128), 0)

    def tile(t, carry):
        coords = [point_ref[c, pl.ds(t, 1), :] for c in range(3)]
        point = jnp.where(row == 0, coords[0], jnp.where(row == 1, coords[1], coords[2]))
        scaled = jnp.where(row < 3, (2.0 * ROOT) * (point - 0.5), 0.0)
        a1 = rounded(scaled)
        rest = scaled - a1
        a2 = rounded(rest)
        a3 = rest - a2
        lead = jnp.where(row == 7, 1.0, jnp.where(row >= 4, -1.0, a1))
        lhs = jnp.concatenate([lead, a2, lead, a2, lead, a3], axis=0)
        lhs_ref[t] = jnp.transpose(lhs).astype(BF16)
        return carry

    lax.fori_loop(0, TILES, tile, 0, unroll=4)


def piece_copies(source, target, sems):
    width = SB_DEV * SITE_BLOCK // PIECES
    copies = []
    for piece in range(PIECES):
        part = pl.ds(piece * width, width)
        copies.append(
            pltpu.make_async_copy(source.at[:, part], target.at[:, part], sems.at[piece])
        )
    return copies


def table_kernel(position_hbm, weight_hbm, table_ref, position_ref, weight_ref, sems):
    weights = pltpu.make_async_copy(weight_hbm, weight_ref, sems.at[PIECES])
    copies = piece_copies(position_hbm, position_ref, sems)
    weights.start()
    for copy in copies:
        copy.start()
    dead = jnp.where(iota((4, 128), 0) == 3, DEAD, 0.0)
    for r in range(CAP):
        table_ref[(SB_DEV + r) * 4 : (SB_DEV + r + 1) * 4, :] = dead
    weights.wait()
    for piece in range(PIECES):
        copies[piece].wait()
        for b in range(piece * BLOCKS, (piece + 1) * BLOCKS):
            place = position_ref[:, b * SITE_BLOCK : (b + 1) * SITE_BLOCK]
            table_ref[4 * b : 4 * b + 3, :] = (place - 0.5) * ROOT
            table_ref[4 * b + 3 : 4 * b + 4, :] = weight_ref[b : b + 1, :]


def filter_taps(taps_ref):
    shape = (3 * TILE, TILE)
    row = iota(shape, 0)
    source = jnp.where(
        row < TILE, row, row % HALF + jnp.where(row < 2 * TILE, -HALF, TILE)
    )
    shift = (source - iota(shape, 1)).astype(F32)
    taps = jnp.where(
        jnp.abs(shift) <= HALF,
        GAUSS_PEAK * jnp.exp(shift * shift * (-0.5 / (SIGMA_CELLS * SIGMA_CELLS))),
        0.0,
    )
    high = rounded(taps)
    rest = taps - high
    middle = rounded(rest)
    for part, values in enumerate((high, middle, rest - middle)):
        taps_ref[part] = values.astype(BF16)


def setup_kernel(position_hbm, point_ref, start_ref, lhs_ref, taps_ref, position_ref, sems):
    copies = piece_copies(position_hbm, position_ref, sems)
    for copy in copies:
        copy.start()
    prepare(point_ref, lhs_ref)
    filter_taps(taps_ref)
    for r in range(CAP):
        start_ref[(SB_DEV + r) * 4 : (SB_DEV + r + 1) * 4, :] = jnp.zeros((4, 128), F32)

    def block(b, carry):
        start = pl.multiple_of(b * SITE_BLOCK, SITE_BLOCK)
        line = pl.multiple_of(b * 4, 4)
        start_ref[pl.ds(line, 3), :] = PRIOR_MASS * position_ref[:, pl.ds(start, SITE_BLOCK)]
        start_ref[pl.ds(line + 3, 1), :] = jnp.zeros((1, 128), F32)
        return carry

    for piece in range(PIECES):
        copies[piece].wait()
        lax.fori_loop(piece * BLOCKS, (piece + 1) * BLOCKS, block, 0, unroll=8)


def smooth_kernel(halo_ref, taps_ref, above_ref, mid_ref, below_ref, load_ref, rows_ref):
    tiles = (above_ref[...], mid_ref[...], below_ref[...])
    count_x, count_y = lax.axis_size("gx"), lax.axis_size("gy")
    here_x, here_y = lax.axis_index("gx"), lax.axis_index("gy")
    shape = (TILES, TILE)
    own_row = iota(shape, 1) // HALF == iota(shape, 0)
    rows = []
    for step, tile in zip((count_y - 1, 0, 1), tiles):
        parts = [tile]
        for side in (count_x - 1, 1):
            peer = lax.rem(here_x + side, count_x) * count_y + lax.rem(here_y + step, count_y)
            halo = halo_ref[pl.ds(2 * peer + 1, 1), :]
            parts.append(jnp.where(own_row, halo, 0.0))
        rows.append(jnp.concatenate(parts, axis=1))
    cells = jnp.concatenate(rows, axis=0)
    high = rounded(cells)
    rest = cells - high
    middle = rounded(rest)
    cells = jnp.concatenate([high, middle, rest - middle], axis=0).astype(BF16)
    count = 3 * TILES
    first = jnp.dot(cells[:count], taps_ref[2], preferred_element_type=F32)
    second = jnp.dot(cells[: 2 * count], taps_ref[1], preferred_element_type=F32)
    third = jnp.dot(cells, taps_ref[0], preferred_element_type=F32)
    first = first + second[count:] + third[2 * count :]
    first = first + second[:count] + third[count : 2 * count] + third[:count]
    planes = []
    for z in range(PZ):
        for part in range(3):
            at = part * TILES + z * CY
            rows_ref[z, part * CY : (part + 1) * CY, :] = first[at : at + CY]
        total = GAUSS[0] * rows_ref[z, 0:CY, :]
        for j in range(1, 2 * HALF + 1):
            total = total + GAUSS[j] * rows_ref[z, j : j + CY, :]
        planes.append(total)
    load_ref[0:CY, :] = GAUSS[HALF] * planes[0] + GAUSS[HALF + 1] * planes[1]
    load_ref[CY : 2 * CY, :] = GAUSS[HALF - 1] * planes[0] + GAUSS[HALF] * planes[1]


def gather_kernel(asked_ref, table_ref, out_hbm, ids_ref, out_ref, ids_smem, sem, out_sems):
    shape = (OWNERS, 128)
    asked = asked_ref[pl.ds(0, OWNERS, stride=2), :]
    lane = iota(shape, 1)
    place = jnp.where(asked < 0.0, (SB_DEV + lane % CAP).astype(F32), asked) * 4.0
    own = iota(shape, 0) % (128 // CAP) == lane // CAP
    place = jnp.where(own, place, 0.0)
    rows = [
        jnp.sum(place[g * 32 : (g + 1) * 32], axis=0, keepdims=True) for g in range(PIECES)
    ]
    ids_ref[...] = jnp.concatenate(rows + rows, axis=0).astype(I32)
    copy = pltpu.make_async_copy(ids_ref, ids_smem, sem)
    copy.start()
    copy.wait()
    copies = []
    for piece in range(PIECES):
        for c in range(BLOCKS):
            line = pl.multiple_of(ids_smem[piece, c], 4)
            out_ref[piece * BLOCKS + c] = table_ref[pl.ds(line, 4), :]
            if (c + 1) % PART == 0:
                part = pl.ds(piece * BLOCKS + c + 1 - PART, PART)
                copies.append(
                    pltpu.make_async_copy(
                        out_ref.at[part], out_hbm.at[part], out_sems.at[len(copies)]
                    )
                )
                copies[-1].start()
    for copy in copies:
        copy.wait()


def transport_kernel(
    target_ref,
    arrived_ref,
    lhs_ref,
    point_ref,
    load_ref,
    potential_ref,
    out_ref,
    top_ref,
    sum_ref,
    even_ref,
    odd_ref,
    even_load_ref,
    odd_load_ref,
):
    row = iota((8, 128), 0)
    fixed = (row < 4) | (row == 7)
    factor = jnp.where(row == 7, KAPPA, 1.0)

    def find_top(t):
        tops = [arrived_ref[target_ref[t, k], 3:4, :] for k in range(CAND)]
        while len(tops) > 1:
            tops = [jnp.maximum(a, b) for a, b in zip(tops[::2], tops[1::2])]
        top = jnp.max(tops[0], axis=1, keepdims=True)
        top_ref[pl.ds(t, 1), :] = jnp.broadcast_to(top, (1, 128))

    def scores(t, e_ref, unit_ref):
        lhs = lhs_ref[t]
        centre = jnp.where(row % 4 == 3, top_ref[pl.ds(t, 1), :], 0.0)

        def spread(k):
            block = arrived_ref[target_ref[t, k]]
            both = jnp.concatenate([block, block], axis=0) - centre
            terms = both * jnp.where(fixed, factor, both)
            t1 = jnp.concatenate([terms, terms], axis=0).astype(BF16)
            first = t1.astype(F32)[:8]
            rest = terms - first
            t2 = jnp.concatenate([rest, rest], axis=0).astype(BF16)
            t3 = rest - t2.astype(F32)[:8]
            return jnp.concatenate(
                [t1, t2, jnp.concatenate([t3, first], axis=0).astype(BF16)], axis=0
            )

        total = None
        for q in range(CAND // 2):
            rhs = jnp.concatenate([spread(2 * q), spread(2 * q + 1)], axis=1)
            e = jnp.exp2(jnp.dot(lhs, rhs, preferred_element_type=F32))
            part = e[:, :128] + e[:, 128:]
            total = part if total is None else total + part
            high = e.astype(BF16)
            e_ref[q, 0:128, :] = high
            e_ref[q, 128:256, :] = (e - high.astype(F32)).astype(BF16)
        sums = jnp.sum(jnp.transpose(total), axis=0, keepdims=True)
        sum_ref[pl.ds(t, 1), :] = sums
        coords = [point_ref[c, pl.ds(t, 1), :] for c in range(3)]
        point = jnp.where(
            row % 4 == 0,
            coords[0],
            jnp.where(row % 4 == 1, coords[1], jnp.where(row % 4 == 2, coords[2], 1.0)),
        )
        loads = (load_ref[pl.ds(t, 1), :] / sums) * point
        high = rounded(loads)
        unit_ref[...] = jnp.where(row < 4, high, loads - high)

    def moments(t, e_ref, unit_ref):
        half = unit_ref[...].astype(BF16)
        lhs = jnp.concatenate([half, half], axis=1)
        for q in range(CAND // 2):
            found = jnp.dot(lhs, e_ref[q], preferred_element_type=F32)
            found = found[0:4] + found[4:8]
            out_ref[target_ref[t, 2 * q]] = found[:, :128]
            out_ref[target_ref[t, 2 * q + 1]] = found[:, 128:]

    find_top(0)

    def two_tiles(i, carry):
        t = 2 * i
        find_top(t + 1)
        scores(t, even_ref, even_load_ref)
        moments(jnp.maximum(t - 1, 0), odd_ref, odd_load_ref)
        find_top(jnp.minimum(t + 2, TILES - 1))
        scores(t + 1, odd_ref, odd_load_ref)
        moments(t, even_ref, even_load_ref)
        return carry

    lax.fori_loop(0, TILES // 2, two_tiles, 0, unroll=8)
    moments(TILES - 1, odd_ref, odd_load_ref)
    square = (
        (point_ref[0] - 0.5) ** 2 + (point_ref[1] - 0.5) ** 2 + (point_ref[2] - 0.5) ** 2
    )
    potential_ref[...] = jnp.log(sum_ref[...]) + (top_ref[...] - square) / EPSILON


def reduce_kernel(
    ids_vmem,
    back_ref,
    start_ref,
    mass_hbm,
    centre_hbm,
    acc_ref,
    other_ref,
    mass_ref,
    scale_ref,
    centre_ref,
    ids_ref,
    ids_sem,
    sems,
):
    ids_copy = pltpu.make_async_copy(ids_vmem, ids_ref, ids_sem)
    ids_copy.start()
    other_ref[...] = jnp.zeros_like(other_ref)
    ids_copy.wait()
    for piece in range(PIECES):
        for peer in range(BLOCKS // CAP):
            into = (acc_ref, other_ref)[peer % 2]
            places = []
            sums = []
            for r in range(CAP):
                c = peer * CAP + r
                place = pl.ds(pl.multiple_of(ids_ref[piece, c], 4), 4)
                places.append(place)
                sums.append(into[place, :] + back_ref[piece * BLOCKS + c])
            for place, total in zip(places, sums):
                into[place, :] = total
    copies = []
    width = PART * SITE_BLOCK
    for piece in range(SB_DEV // PART):
        part = pl.ds(piece * PART, PART)
        lines = pl.ds(piece * PART * 4 + 3, PART, stride=4)
        mass = acc_ref[lines, :] + other_ref[lines, :]
        mass_ref[part, :] = mass
        copies.append(
            pltpu.make_async_copy(
                mass_ref.at[part], mass_hbm.at[part], sems.at[SB_DEV // PART + piece]
            )
        )
        copies[-1].start()
        scale_ref[part, :] = 1.0 / (mass + PRIOR_MASS)
        for b in range(piece * PART, (piece + 1) * PART):
            centre_ref[:, b * SITE_BLOCK : (b + 1) * SITE_BLOCK] = (
                acc_ref[4 * b : 4 * b + 3, :] + other_ref[4 * b : 4 * b + 3, :]
            ) * scale_ref[b : b + 1, :]
        part = pl.ds(piece * width, width)
        copies.append(
            pltpu.make_async_copy(
                centre_ref.at[:, part], centre_hbm.at[:, part], sems.at[piece]
            )
        )
        copies[-1].start()
    for copy in copies:
        copy.wait()


def shape_of(*dims, dtype=F32):
    return jax.ShapeDtypeStruct(dims, dtype)


def in_hbm(values):
    return pltpu.with_memory_space_constraint(values, pltpu.HBM)


def exchange(values):
    return lax.all_to_all(values, AXES, split_axis=0, concat_axis=0, tiled=True)


def neighbours(values, axis):
    count = lax.axis_size(axis)
    before = lax.ppermute(values, axis, [(i, (i + 1) % count) for i in range(count)])
    after = lax.ppermute(values, axis, [((i + 1) % count, i) for i in range(count)])
    return before, after


def local(
    density, point_position, block_owner, block_slot, block_count, site_position, site_weight
):
    cells = density.reshape(TILES, TILE)
    points = point_position.reshape(3, TILES, TILE)
    request, target = pl.pallas_call(
        request_kernel,
        out_shape=(
            shape_of(2 * OWNERS, 128),
            shape_of(TILES, 128, dtype=I32),
        ),
        in_specs=[HBM] * 4,
        out_specs=(VMEM, VMEM),
        scratch_shapes=[
            pltpu.VMEM((TILES, CAND), I32),
            pltpu.VMEM((TILES, CAND), I32),
            pltpu.VMEM((PZ, 1, CY), I32),
            pltpu.VMEM((TILES, TILE), F32),
            pltpu.SemaphoreType.DMA((4,)),
        ],
        compiler_params=LIMIT,
        name="request",
    )(
        in_hbm(block_owner.reshape(TILES, CAND)),
        in_hbm(block_slot.reshape(TILES, CAND)),
        in_hbm(jnp.transpose(block_count, (0, 2, 1))),
        in_hbm(cells),
    )
    asked = exchange(request)
    table = pl.pallas_call(
        table_kernel,
        out_shape=shape_of((SB_DEV + CAP) * 4, SITE_BLOCK),
        in_specs=[HBM] * 2,
        out_specs=VMEM,
        scratch_shapes=[
            pltpu.VMEM((3, SB_DEV * SITE_BLOCK), F32),
            pltpu.VMEM((SB_DEV, SITE_BLOCK), F32),
            pltpu.SemaphoreType.DMA((PIECES + 1,)),
        ],
        compiler_params=LIMIT,
        name="table",
    )(in_hbm(site_position), in_hbm(site_weight.reshape(SB_DEV, SITE_BLOCK)))
    blocks, ids = pl.pallas_call(
        gather_kernel,
        out_shape=(shape_of(SLOTS, 4, SITE_BLOCK), shape_of(8, 128, dtype=I32)),
        in_specs=[VMEM] * 2,
        out_specs=(HBM, VMEM),
        compiler_params=LIMIT,
        scratch_shapes=[
            pltpu.VMEM((SLOTS, 4, SITE_BLOCK), F32),
            pltpu.SMEM((8, 128), I32),
            pltpu.SemaphoreType.DMA,
            pltpu.SemaphoreType.DMA((SB_DEV // PART,)),
        ],
        name="gather",
    )(asked, table)
    cells, points, site_position, blocks = lax.optimization_barrier(
        (cells, points, site_position, blocks)
    )
    arrived = exchange(blocks)
    above, below = neighbours(cells, "gy")
    start, lhs, taps = pl.pallas_call(
        setup_kernel,
        out_shape=(
            shape_of((SB_DEV + CAP) * 4, SITE_BLOCK),
            shape_of(TILES, TILE, 48, dtype=BF16),
            shape_of(3, 3 * TILE, TILE, dtype=BF16),
        ),
        in_specs=[HBM, VMEM],
        out_specs=(VMEM,) * 3,
        scratch_shapes=[
            pltpu.VMEM((3, SB_DEV * SITE_BLOCK), F32),
            pltpu.SemaphoreType.DMA((PIECES,)),
        ],
        compiler_params=LIMIT,
        name="setup",
    )(in_hbm(site_position), points)
    load = pl.pallas_call(
        smooth_kernel,
        out_shape=shape_of(TILES, TILE),
        in_specs=[VMEM] * 5,
        out_specs=VMEM,
        scratch_shapes=[pltpu.VMEM((PZ, 3 * CY, 128), F32)],
        compiler_params=LIMIT,
        name="smooth",
    )(asked, taps, above, cells, below)
    potential, moments = pl.pallas_call(
        transport_kernel,
        out_shape=(shape_of(TILES, TILE), shape_of(SLOTS, 4, SITE_BLOCK)),
        in_specs=[SMEM] + [VMEM] * 4,
        out_specs=(VMEM, VMEM),
        scratch_shapes=[
            pltpu.VMEM((TILES, 128), F32),
            pltpu.VMEM((TILES, 128), F32),
            pltpu.VMEM((CAND // 2, 256, 256), BF16),
            pltpu.VMEM((CAND // 2, 256, 256), BF16),
            pltpu.VMEM((8, 128), F32),
            pltpu.VMEM((8, 128), F32),
        ],
        compiler_params=LIMIT,
        name="transport",
    )(target, arrived, lhs, points, load)
    returned = exchange(moments)
    site_mass, barycentre, _ = pl.pallas_call(
        reduce_kernel,
        out_shape=(
            shape_of(SB_DEV, SITE_BLOCK),
            shape_of(3, SB_DEV * SITE_BLOCK),
            shape_of((SB_DEV + CAP) * 4, SITE_BLOCK),
        ),
        in_specs=[VMEM] * 3,
        out_specs=(HBM, HBM, VMEM),
        scratch_shapes=[
            pltpu.VMEM(((SB_DEV + CAP) * 4, SITE_BLOCK), F32),
            pltpu.VMEM((SB_DEV, SITE_BLOCK), F32),
            pltpu.VMEM((SB_DEV, SITE_BLOCK), F32),
            pltpu.VMEM((3, SB_DEV * SITE_BLOCK), F32),
            pltpu.SMEM((8, 128), I32),
            pltpu.SemaphoreType.DMA,
            pltpu.SemaphoreType.DMA((2 * SB_DEV // PART,)),
        ],
        input_output_aliases={2: 2},
        compiler_params=LIMIT,
        name="reduce",
    )(ids, returned, start)
    return (
        potential.reshape(PZ, CY, TILE),
        site_mass.reshape(SB_DEV * SITE_BLOCK),
        barycentre,
    )


def solution(mesh):
    in_specs = (
        P(None, "gy", "gx"),
        P(None, None, "gy", "gx"),
        P(None, "gy", "gx"),
        P(None, "gy", "gx"),
        P(None, "gy", "gx"),
        P(None, ("gx", "gy")),
        P(("gx", "gy")),
    )
    out_specs = (P(None, "gy", "gx"), P(("gx", "gy")), P(None, ("gx", "gy")))
    return jax.shard_map(local, mesh=mesh, in_specs=in_specs, out_specs=out_specs, check_vma=False)
```
